32 devices in a mesh: spot: 8 (over y, x, core), col: 4 (over z).
Axes of the slice: x: 2, y: 2, z: 4, core: 2. Of those that a mesh axis runs over, the one named last changes fastest.
Arguments:
- logits: float32 [1024, 16384], P(None, ('spot', 'col')), may hold values from -8 to 8
- cell_expr: float32 [1024, 2048], P(('spot', 'col')), may hold values from -6 to 6
- spot_expr: float32 [16384, 2048], P(('spot', 'col')), may hold values from -6 to 6
- cell_slide: int32 [1024], replicated, may hold values from 0 to 10, as said below
- spot_slide: int32 [16384], P(('spot', 'col')), may hold values from 0 to 10
- spot_mask: int32 [16384], P(('spot', 'col')), may hold values 0 or 1
Outputs:
- loss: float32 [], replicated
- grad_logits: float32 [1024, 16384], P(None, ('spot', 'col'))
- grad_expr: float32 [1024, 2048], P(('spot', 'col'))
The draws below stay inside these ranges and needn't reach their ends.
Inputs may be any that keep to these rules, and one draw needn't show every extreme that they name: `cell_slide`: cell i belongs to slide i' mod 11 for a permutation i' of the cells, so each slide holds 93 or one more cells, spread over all devices.
All inputs are finite; a program needn't handle non-finite values. No bound on the sum of `spot_mask` on one device may be relied on, other than what follows from the above.
Results may differ from the reference program's by a relative error of at most 0.0003.
Values sent between devices are 32-bit elements; how exact they have to be, the bound alone decides.
No kernel may reach another device: no remote copies, remote signals or barrier semaphores. Data moves between devices by JAX's collectives and lax.ppermute only.
A program may use at most 320 MiB of HBM per device.

```python
import jax
import jax.numpy as jnp
from jax import lax

GENES = 2048
SLIDES = 11
CELLS = 1024
SPOTS = 16384


def draw_cell_slide(key, part):
    order = jax.random.permutation(key, CELLS)
    return (order % SLIDES).astype(jnp.int32)


def plant(entries, stream_key, least, high):
    spot = [jax.random.randint(jax.random.fold_in(stream_key, axis), (), 0, length) for axis, length in enumerate(entries.shape)]
    widest = entries.shape.index(max(entries.shape))
    neighbour = spot[:widest] + [(spot[widest] + 1) % entries.shape[widest]] + spot[widest + 1:]
    return entries.at[tuple(spot)].set(least).at[tuple(neighbour)].set(high)


def block_scale(rng, dims, split, least, high):
    factor_of, own = 1.0, jax.random.fold_in(rng, 6)
    for dim, parts in split:
        steps = jnp.exp(jax.random.uniform(jax.random.fold_in(own, dim), (parts,), jnp.float32, least / len(split), high / len(split)))
        factor_of = factor_of * jnp.repeat(steps, dims[dim] // parts).reshape([-1 if axis == dim else 1 for axis in range(len(dims))])
    return factor_of


def bell_draw(key, dims, deviation, most, split=(), held_as=jnp.bfloat16):
    drawn = jax.random.normal(key, dims, jnp.float32) * deviation
    if len(split) > 0:
        drawn = block_scale(key, dims, split, -0.22, 0.18) * drawn
    return jnp.clip(drawn, min=-most, max=most).astype(held_as)


def setup_inputs(seed: int = 0) -> dict:
    keys = jax.random.split(jax.random.key(seed), 7)
    logits = bell_draw(keys[0], (CELLS, SPOTS), 1.5, 8.0, ((1, 32),), jnp.float32)
    cell_expr = bell_draw(keys[1], (CELLS, GENES), 1.0, 6.0, ((0, 32),), jnp.float32)
    spot_expr = bell_draw(keys[2], (SPOTS, GENES), 1.0, 6.0, ((0, 32),), jnp.float32)
    cell_slide = draw_cell_slide(jax.random.fold_in(keys[6], 71), 0)
    spot_slide = plant(jax.random.randint(keys[4], (SPOTS,), 0, SLIDES), jax.random.fold_in(keys[4], 1), 0, SLIDES - 1).astype(jnp.int32)
    spot_mask = plant((jax.random.randint(keys[5], (SPOTS,), 0, 4) < 3).astype(jnp.int32), jax.random.fold_in(keys[5], 1), 0, 1)
    return dict(logits=logits, cell_expr=cell_expr, spot_expr=spot_expr, cell_slide=cell_slide, spot_slide=spot_slide, spot_mask=spot_mask)


@jax.custom_vjp
def low(v):
    return lax.optimization_barrier(v.astype(jnp.bfloat16)).astype(jnp.float32)

@jax.custom_vjp
def low_back(v):
    return v

def low_keep(v):
    return (low(v), None)

def low_pass(kept, grad):
    return (grad,)

def back_keep(v):
    return (v, None)

def back_low(kept, grad):
    return (low(grad),)
low.defvjp(low_keep, low_pass)
low_back.defvjp(back_keep, back_low)
epsilon = 1e-06
highest = lax.Precision.HIGHEST

def forward(logits, cell_expr, spot_expr, cell_slide, spot_slide, spot_mask):
    same_slide = cell_slide[:, None] == spot_slide[None, :]
    same_float = same_slide.astype(jnp.float32)
    masked = jnp.where(same_slide, logits, -jnp.inf)
    col_max = lax.optimization_barrier(jnp.max(masked, axis=0))
    weights = jnp.exp(masked - col_max[None, :])
    col_total = lax.optimization_barrier(jnp.sum(weights, axis=0))
    mapping = weights / col_total[None, :]
    counts = lax.optimization_barrier(jnp.sum(same_float, axis=0))
    mean_logit = lax.optimization_barrier(jnp.sum(same_float * logits, axis=0)) / counts
    kl_term = col_max + jnp.log(col_total) - mean_logit - jnp.log(counts)
    predicted = jnp.einsum('cs,cg->sg', mapping, cell_expr, precision=highest)
    spot_sq = lax.optimization_barrier(jnp.sum(predicted * predicted, axis=1))
    true_sq = lax.optimization_barrier(jnp.sum(spot_expr * spot_expr, axis=1))
    cross = lax.optimization_barrier(jnp.sum(predicted * spot_expr, axis=1))
    spot_cos = cross * lax.rsqrt(spot_sq + epsilon) * lax.rsqrt(true_sq + epsilon)
    mask_float = spot_mask.astype(jnp.float32)
    onehot = (spot_slide[:, None] == jnp.arange(SLIDES, dtype=jnp.int32)[None, :]).astype(jnp.float32) * mask_float[:, None]
    dots = jnp.einsum('sl,sg->lg', onehot, predicted * spot_expr, precision=highest)
    np_sum = jnp.einsum('sl,sg->lg', onehot, predicted * predicted, precision=highest)
    ng_sum = jnp.einsum('sl,sg->lg', onehot, spot_expr * spot_expr, precision=highest)
    gene_cos = dots * lax.rsqrt(np_sum + epsilon) * lax.rsqrt(ng_sum + epsilon)
    return -jnp.mean(gene_cos) + jnp.sum(mask_float * (kl_term - spot_cos)) / SPOTS

def reference(logits, cell_expr, spot_expr, cell_slide, spot_slide, spot_mask):

    def wrapped(first, second):
        return forward(first, second, spot_expr, cell_slide, spot_slide, spot_mask)
    loss, pullback = jax.vjp(wrapped, logits, cell_expr)
    grad_first, grad_second = pullback(jnp.ones_like(loss))
    factor = SPOTS * CELLS / SLIDES
    return (loss, grad_first * factor, grad_second * factor)
```

```python
import jax
import jax.numpy as jnp
from jax import lax
from jax.sharding import PartitionSpec as P

SLIDES = 11


epsilon = 1e-06
highest = lax.Precision.HIGHEST
high = lax.Precision.HIGH


def sum_over(value, axis):
    size = lax.axis_size(axis)
    step = 1
    while step < size:
        value = value + lax.ppermute(value, axis, [(i, i ^ step) for i in range(size)])
        step *= 2
    return value


def on_device(logits, cell_expr, spot_expr, cell_slide, spot_slide, spot_mask):
    cells_all = logits.shape[0]
    spots_all = logits.shape[1] * lax.axis_size(("spot", "col"))
    genes_all = cell_expr.shape[1]
    factor = spots_all * cells_all / SLIDES
    same_slide = cell_slide[:, None] == spot_slide[None, :]
    same_float = same_slide.astype(jnp.float32)
    masked = jnp.where(same_slide, logits, -jnp.inf)
    col_max = jnp.max(masked, axis=0)
    weights = jnp.exp(masked - col_max[None, :])
    col_total = jnp.sum(weights, axis=0)
    mapping = weights / col_total[None, :]
    counts = jnp.sum(same_float, axis=0)
    mean_logit = jnp.sum(same_float * logits, axis=0) / counts
    kl_term = col_max + jnp.log(col_total) - mean_logit - jnp.log(counts)
    mask_float = spot_mask.astype(jnp.float32)
    kl_local = jnp.sum(mask_float * kl_term)
    whole_rows = lax.all_gather(cell_expr, ("spot", "col"), axis=0, tiled=True)
    predicted = jnp.einsum("cs,cg->sg", mapping, whole_rows, precision=high)
    spot_sq = jnp.sum(predicted * predicted, axis=1)
    true_sq = jnp.sum(spot_expr * spot_expr, axis=1)
    cross = jnp.sum(predicted * spot_expr, axis=1)
    spot_scale = lax.rsqrt(spot_sq + epsilon) * lax.rsqrt(true_sq + epsilon)
    spot_cos = cross * spot_scale
    onehot = (spot_slide[:, None] == jnp.arange(SLIDES, dtype=jnp.int32)[None, :]).astype(
        jnp.float32
    ) * mask_float[:, None]
    dots = jnp.einsum("sl,sg->lg", onehot, predicted * spot_expr, precision=highest)
    np_part = jnp.einsum("sl,sg->lg", onehot, predicted * predicted, precision=highest)
    ng_part = jnp.einsum("sl,sg->lg", onehot, spot_expr * spot_expr, precision=highest)
    cos_local = jnp.sum(mask_float * spot_cos)
    scalars = jnp.zeros((3, genes_all), jnp.float32).at[0, 0].set(cos_local).at[0, 1].set(kl_local)
    packed = jnp.concatenate([dots, np_part, ng_part, scalars], axis=0)
    packed = sum_over(sum_over(packed, "spot"), "col")
    dots = packed[:SLIDES]
    np_sum = packed[SLIDES : 2 * SLIDES]
    ng_sum = packed[2 * SLIDES : 3 * SLIDES]
    cos_total = packed[3 * SLIDES, 0]
    kl_total = packed[3 * SLIDES, 1]
    gene_scale = lax.rsqrt(np_sum + epsilon) * lax.rsqrt(ng_sum + epsilon)
    gene_cos = dots * gene_scale
    loss = -jnp.mean(gene_cos) + (kl_total - cos_total) / spots_all
    coef_spot = factor * mask_float / spots_all
    coef_gene = factor / (SLIDES * genes_all)
    gene_a = jnp.einsum("sl,lg->sg", onehot, gene_scale, precision=highest)
    gene_b = jnp.einsum("sl,lg->sg", onehot, gene_cos / (np_sum + epsilon), precision=highest)
    spot_b = spot_cos / (spot_sq + epsilon)
    grad_pred = -coef_gene * (gene_a * spot_expr - gene_b * predicted)
    grad_pred = grad_pred - coef_spot[:, None] * (
        spot_scale[:, None] * spot_expr - spot_b[:, None] * predicted
    )
    grad_map = jnp.einsum("cg,sg->cs", whole_rows, grad_pred, precision=high)
    col_inner = jnp.sum(mapping * grad_map, axis=0)
    grad_logits = mapping * (grad_map - col_inner[None, :]) + coef_spot[None, :] * (
        mapping - same_float / counts[None, :]
    )
    grad_expr = jnp.einsum("cs,sg->cg", mapping, grad_pred, precision=high)
    for axis in ("spot", "col"):
        grad_expr = lax.psum_scatter(grad_expr, axis, scatter_dimension=0, tiled=True)
    return (loss, grad_logits, grad_expr)


def solution(mesh):
    in_specs = (
        P(None, ("spot", "col")),
        P(("spot", "col"), None),
        P(("spot", "col"), None),
        P(),
        P(("spot", "col")),
        P(("spot", "col")),
    )
    out_specs = (P(), P(None, ("spot", "col")), P(("spot", "col"), None))
    return jax.shard_map(
        on_device, mesh=mesh, in_specs=in_specs, out_specs=out_specs, check_vma=False
    )
```

```python
import functools

import jax
import jax.numpy as jnp
from jax import lax
from jax.experimental import pallas as pl
from jax.experimental.pallas import tpu as pltpu
from jax.sharding import PartitionSpec as P

SLIDES = 11
ROWS = 16
EPS = 1e-06
AXES = ("spot", "col")
F32 = jnp.float32
BF16 = jnp.bfloat16
LANES = 128


def split(x):
    hi = x.astype(BF16)
    return hi, (x - hi.astype(F32)).astype(BF16)


def params(plan, small=20):
    return pltpu.CompilerParams(vmem_limit_bytes=(small if plan.cells <= 2048 else 60) << 20)


def cost(flops, bytes_accessed):
    return pl.CostEstimate(flops=int(flops), bytes_accessed=int(bytes_accessed), transcendentals=0)


class Plan:
    def __init__(self, n_spot, n_col, cells, spots, genes):
        self.n_col = n_col
        self.plane = n_spot // 2
        self.bits = self.plane.bit_length() - 1
        self.rows = cells // (n_spot * n_col)
        self.cells = cells
        self.half = spots
        self.pair = 2 * spots
        self.genes = genes // 2
        self.unit = 2 * self.rows
        self.chunk = self.plane * self.unit
        self.n_spot = n_spot
        self.total = n_spot * n_col
        self.tile = 256 if cells <= 2048 else 128

    def order(self, core):
        return list(range(self.bits)) if core == 0 else list(range(self.bits))[::-1]

    def reverse(self, m):
        return sum(((m >> b) & 1) << (self.bits - 1 - b) for b in range(self.bits))

    def device(self, plane, core, z):
        return (plane * 2 + core) * self.n_col + z

    def all_places(self):
        for plane in range(self.plane):
            for core in range(2):
                for z in range(self.n_col):
                    yield plane, core, z

    def swap_core(self):
        return [(self.device(q, c, z), self.device(q, 1 - c, z)) for q, c, z in self.all_places()]

    def ring(self):
        return [(self.device(q, c, z), self.device(q, c, (z + 1) % self.n_col)) for q, c, z in self.all_places()]

    def hop(self, step):
        return [
            (self.device(q, c, z), self.device(q ^ (1 << self.order(c)[step]), c, z))
            for q, c, z in self.all_places()
        ]

    def block_start(self, place_ref, k, m, c):
        plane, core, z = place_ref[0], place_ref[1], place_ref[2]
        shift = [0, 0]
        for which in range(2):
            for step, bit in enumerate(self.order(which)):
                shift[which] |= ((m >> step) & 1) << bit
        xor = jnp.where(core == 0, shift[0], shift[1])
        q = jnp.bitwise_xor(plane, xor)
        ring = lax.rem(z - k + self.n_col, self.n_col)
        return ((q * 2 + c) * self.n_col + ring) * self.rows


def blocks(plan):
    for k in range(plan.n_col):
        for m in range(plan.plane):
            for c in range(2):
                yield k, m, c


def mapping_kernel(plan, place, own_ref, sib_ref, cell_ref, meta_own, meta_sib, hi_ref, lo_ref, hit_ref, lot_ref, row_ref, w_ref):
    tiles = plan.half // plan.tile
    j = pl.program_id(0)

    def run(logits_ref, meta_ref):
        meta = jnp.transpose(meta_ref[...])
        slide = meta[0:1, :]
        cell = jnp.concatenate([cell_ref[...]] * (plan.tile // LANES), axis=1)
        same = cell == slide
        x = logits_ref[...]
        masked = jnp.where(same, x, -jnp.inf)
        col_max = jnp.max(masked, axis=0, keepdims=True)
        w = jnp.exp(masked - col_max)
        total = jnp.sum(w, axis=0, keepdims=True)
        w_ref[...] = w * (1.0 / total)
        counts = jnp.sum(jnp.where(same, 1.0, 0.0), axis=0, keepdims=True)
        mean = jnp.sum(jnp.where(same, x, 0.0), axis=0, keepdims=True) / counts
        kl = (col_max + jnp.log(total) - mean - jnp.log(counts)) * meta[1:2, :]
        row = lax.broadcasted_iota(jnp.int32, (8, plan.tile), 0)
        row_ref[...] = jnp.where(row == 0, kl, counts)

    @pl.when(j < tiles)
    def _():
        run(own_ref, meta_own)

    @pl.when(j >= tiles)
    def _():
        run(sib_ref, meta_sib)

    gather = max(LANES // plan.rows, 1)
    held = []
    for i, (k, m, c) in enumerate(blocks(plan)):
        start = pl.multiple_of(plan.block_start(place, k, m, c), plan.rows)
        block = w_ref[pl.ds(start, plan.rows), :]
        hi, lo = split(block)
        hi_ref[i * plan.rows : (i + 1) * plan.rows, :] = hi
        lo_ref[i * plan.rows : (i + 1) * plan.rows, :] = lo
        held.append(block)
        if len(held) == gather:
            wide = jnp.transpose(jnp.concatenate(held, axis=0))
            hi, lo = split(wide)
            end = (i + 1) * plan.rows
            hit_ref[:, end - LANES : end] = hi
            lot_ref[:, end - LANES : end] = lo
            held = []


def make_mapping(plan, place, own, sib, cell, meta_own, meta_sib):
    t, tiles = plan.tile, plan.half // plan.tile
    first = lambda j, *_: (0, jnp.minimum(j, tiles - 1))
    second = lambda j, *_: (0, jnp.maximum(j - tiles, 0))
    wide = jax.ShapeDtypeStruct((plan.cells, plan.pair), BF16)
    tall = jax.ShapeDtypeStruct((plan.pair, plan.cells), BF16)
    return pl.pallas_call(
        functools.partial(mapping_kernel, plan),
        out_shape=(wide, wide, tall, tall, jax.ShapeDtypeStruct((8, plan.pair), F32)),
        grid_spec=pltpu.PrefetchScalarGridSpec(
            num_scalar_prefetch=1,
            grid=(2 * tiles,),
            in_specs=[
                pl.BlockSpec((plan.cells, t), first),
                pl.BlockSpec((plan.cells, t), second),
                pl.BlockSpec((plan.cells, LANES), lambda j, *_: (0, 0)),
                pl.BlockSpec((t, LANES), lambda j, *_: (jnp.minimum(j, tiles - 1), 0)),
                pl.BlockSpec((t, LANES), lambda j, *_: (jnp.maximum(j - tiles, 0), 0)),
            ],
            out_specs=[
                pl.BlockSpec((plan.cells, t), lambda j, *_: (0, j)),
                pl.BlockSpec((plan.cells, t), lambda j, *_: (0, j)),
                pl.BlockSpec((t, plan.cells), lambda j, *_: (j, 0)),
                pl.BlockSpec((t, plan.cells), lambda j, *_: (j, 0)),
                pl.BlockSpec((8, t), lambda j, *_: (0, j)),
            ],
            scratch_shapes=[pltpu.VMEM((plan.cells, t), F32)],
        ),
        compiler_params=params(plan),
        cost_estimate=cost(plan.cells * plan.pair * 20, plan.cells * plan.pair * 12),
        name="mapping",
    )(place, own, sib, cell, meta_own, meta_sib)


def onehot_rows(plan, meta):
    turned = jnp.transpose(meta)
    slide = lax.broadcasted_iota(jnp.int32, (ROWS, meta.shape[0]), 0).astype(F32)
    return jnp.where(turned[0:1, :] == slide, turned[1:2, :], 0.0).astype(BF16)


def slide_sum(onehot, value):
    hi, lo = split(value)
    return jnp.dot(
        jnp.concatenate([onehot, onehot], axis=1),
        jnp.concatenate([hi, lo], axis=0),
        preferred_element_type=F32,
    )


def row_sum(value):
    return jnp.sum(value, axis=1, keepdims=True)


def spots_kernel(plan, place, own_ref, sib_ref, meta_own, meta_sib, spot_ref, stat_ref, ng_ref):
    tiles = plan.half // 256
    j = pl.program_id(0)

    @pl.when(j == 0)
    def _():
        ng_ref[...] = jnp.zeros_like(ng_ref)

    def run(value_ref, meta_ref):
        value = value_ref[...]
        square = value * value
        spot_ref[...] = value
        stat_ref[...] = jnp.broadcast_to(row_sum(square), stat_ref.shape)
        ng_ref[...] += slide_sum(onehot_rows(plan, meta_ref[...]), square)

    @pl.when(j < tiles)
    def _():
        run(own_ref, meta_own)

    @pl.when(j >= tiles)
    def _():
        run(sib_ref, meta_sib)


def make_spots(plan, place, own, sib, meta_own, meta_sib):
    t, tiles, g = 256, plan.half // 256, plan.genes
    return pl.pallas_call(
        functools.partial(spots_kernel, plan),
        out_shape=(
            jax.ShapeDtypeStruct((plan.pair, g), F32),
            jax.ShapeDtypeStruct((plan.pair, LANES), F32),
            jax.ShapeDtypeStruct((ROWS, g), F32),
        ),
        grid_spec=pltpu.PrefetchScalarGridSpec(
            num_scalar_prefetch=1,
            grid=(2 * tiles,),
            in_specs=[
                pl.BlockSpec((t, g), lambda j, place: (jnp.minimum(j, tiles - 1), place[1])),
                pl.BlockSpec((t, g), lambda j, place: (jnp.maximum(j - tiles, 0), 0)),
                pl.BlockSpec((t, LANES), lambda j, place: (jnp.minimum(j, tiles - 1), 0)),
                pl.BlockSpec((t, LANES), lambda j, place: (jnp.maximum(j - tiles, 0), 0)),
            ],
            out_specs=[
                pl.BlockSpec((t, g), lambda j, place: (j, 0)),
                pl.BlockSpec((t, LANES), lambda j, place: (j, 0)),
                pl.BlockSpec((ROWS, g), lambda j, place: (0, 0)),
            ],
        ),
        compiler_params=params(plan),
        cost_estimate=cost(plan.pair * g * 64, plan.pair * g * 8),
        name="spots",
    )(place, own, sib, meta_own, meta_sib)


def predict_kernel(plan, n_parts, first, last, *refs):
    refs = list(refs)
    parts = [refs.pop(0) for _ in range(n_parts)]
    hit_ref, lot_ref = refs.pop(0), refs.pop(0)
    acc_in = None
    if not first:
        acc_in = refs.pop(0)
        refs.pop(0), refs.pop(0)
    if last:
        spot_ref, gg_ref, meta_ref = refs.pop(0), refs.pop(0), refs.pop(0)
    acc_ref, chi_ref, clo_ref = refs.pop(0), refs.pop(0), refs.pop(0)
    if last:
        stat_ref, sums_ref = refs.pop(0), refs.pop(0)
    stack_ref = refs.pop(0)
    j = pl.program_id(0)
    size = plan.chunk

    @pl.when(j == 0)
    def _():
        at = 0
        for part in parts:
            n = part.shape[0]
            hi, lo = split(part[...])
            stack_ref[at : at + n, :] = hi
            stack_ref[size + at : size + at + n, :] = lo
            stack_ref[2 * size + at : 2 * size + at + n, :] = hi
            chi_ref[at : at + n, :] = hi
            clo_ref[at : at + n, :] = lo
            at += n
        if last:
            sums_ref[...] = jnp.zeros_like(sums_ref)

    left = jnp.concatenate([hit_ref[...], hit_ref[...], lot_ref[...]], axis=1)
    value = jnp.dot(left, stack_ref[...], preferred_element_type=F32)
    if not first:
        value = value + acc_in[...]
    acc_ref[...] = value
    if last:
        spot = spot_ref[...]
        square, cross = value * value, value * spot
        lane = lax.broadcasted_iota(jnp.int32, stat_ref.shape, 1)
        stat_ref[...] = jnp.where(lane == 0, row_sum(square), jnp.where(lane == 1, row_sum(cross), gg_ref[...]))
        onehot = onehot_rows(plan, meta_ref[...])
        sums_ref[0:ROWS, :] += slide_sum(onehot, square)
        sums_ref[ROWS : 2 * ROWS, :] += slide_sum(onehot, cross)


def make_predict(plan, k, parts, hit, lot, carry, last=None):
    t, g, size = 256, plan.genes, plan.chunk
    const = lambda j: (0, 0)
    in_specs = [pl.BlockSpec(p.shape, const) for p in parts]
    in_specs += [pl.BlockSpec((t, size), lambda j: (j, k))] * 2
    operands = [*parts, hit, lot]
    aliases = {}
    if carry is not None:
        at = len(operands)
        operands += list(carry)
        in_specs += [pl.BlockSpec((t, g), lambda j: (j, 0)), pl.BlockSpec(memory_space=pl.ANY), pl.BlockSpec(memory_space=pl.ANY)]
        aliases = {at: 0, at + 1: 1, at + 2: 2}
    out_shape = [
        jax.ShapeDtypeStruct((plan.pair, g), F32),
        jax.ShapeDtypeStruct((plan.cells, g), BF16),
        jax.ShapeDtypeStruct((plan.cells, g), BF16),
    ]
    out_specs = [pl.BlockSpec((t, g), lambda j: (j, 0))] + [pl.BlockSpec((size, g), lambda j: (k, 0))] * 2
    if last is not None:
        operands += list(last)
        in_specs += [pl.BlockSpec((t, g), lambda j: (j, 0))] + [pl.BlockSpec((t, LANES), lambda j: (j, 0))] * 2
        out_shape += [jax.ShapeDtypeStruct((plan.pair, LANES), F32), jax.ShapeDtypeStruct((2 * ROWS, g), F32)]
        out_specs += [pl.BlockSpec((t, LANES), lambda j: (j, 0)), pl.BlockSpec((2 * ROWS, g), const)]
    return pl.pallas_call(
        functools.partial(predict_kernel, plan, len(parts), carry is None, last is not None),
        out_shape=tuple(out_shape),
        grid=(plan.pair // t,),
        in_specs=in_specs,
        out_specs=out_specs,
        scratch_shapes=[pltpu.VMEM((3 * size, g), BF16)],
        input_output_aliases=aliases,
        compiler_params=params(plan),
        cost_estimate=cost(6 * plan.pair * g * size, plan.pair * g * 8),
        name="predict",
    )(*operands)


def gradient_kernel(plan, coef_gene, coef_spot, pred_ref, spot_ref, mine_ref, other_ref, meta_ref, sums_ref,
                    mhi_ref, mlo_ref, ghi_ref, glo_ref, keep_ref, send_ref, cos_ref, a_ref, b_ref, acc_ref):
    j = pl.program_id(0)

    @pl.when(j == 0)
    def _():
        np_sum, dots, ng_sum = sums_ref[0:ROWS, :], sums_ref[ROWS : 2 * ROWS, :], sums_ref[2 * ROWS : 3 * ROWS, :]
        scale = lax.rsqrt(np_sum + EPS) * lax.rsqrt(ng_sum + EPS)
        cosine = dots * scale
        hi, lo = split(-coef_gene * scale)
        a_ref[0:ROWS, :] = hi
        a_ref[ROWS : 2 * ROWS, :] = lo
        hi, lo = split(coef_gene * (cosine / (np_sum + EPS)))
        b_ref[0:ROWS, :] = hi
        b_ref[ROWS : 2 * ROWS, :] = lo
        acc_ref[...] = jnp.zeros_like(acc_ref)
        row = lax.broadcasted_iota(jnp.int32, cosine.shape, 0)
        cos_ref[...] = jnp.zeros_like(cos_ref)
        cos_ref[1:2, :] = jnp.broadcast_to(jnp.sum(jnp.where(row < SLIDES, cosine, 0.0), keepdims=True), (1, LANES))

    stat = mine_ref[...] + other_ref[...]
    spot_sq, cross, true_sq = stat[:, 0:1], stat[:, 1:2], stat[:, 2:3]
    slide, mask = meta_ref[...][:, 0:1], meta_ref[...][:, 1:2]
    scale = lax.rsqrt(spot_sq + EPS) * lax.rsqrt(true_sq + EPS)
    cosine = cross * scale

    @pl.when(j < plan.half // 256)
    def _():
        cos_ref[0:1, :] += jnp.broadcast_to(jnp.sum(cosine * mask, keepdims=True), (1, LANES))

    weight = coef_spot * mask
    lane = lax.broadcasted_iota(jnp.int32, (stat.shape[0], ROWS), 1).astype(F32)
    onehot = jnp.where(slide == lane, mask, 0.0).astype(BF16)
    onehot = jnp.concatenate([onehot, onehot], axis=1)
    gene_a = jnp.dot(onehot, a_ref[...], preferred_element_type=F32)
    gene_b = jnp.dot(onehot, b_ref[...], preferred_element_type=F32)
    grad = spot_ref[...] * (gene_a - weight * scale) + pred_ref[...] * (gene_b + weight * (cosine / (spot_sq + EPS)))
    hi, lo = split(grad)
    ghi_ref[...] = hi
    glo_ref[...] = lo
    left = jnp.concatenate([mhi_ref[...], mhi_ref[...], mlo_ref[...]], axis=1)
    right = jnp.concatenate([hi, lo, hi], axis=0)
    acc_ref[...] += jnp.dot(left, right, preferred_element_type=F32)

    @pl.when(j == pl.num_programs(0) - 1)
    def _():
        n = keep_ref.shape[0]
        keep_ref[...] = acc_ref[0:n, :]
        send_ref[...] = acc_ref[n:, :]


def make_gradient(plan, k, coef_gene, coef_spot, pred, spot, mine, other, meta, sums, mhi, mlo):
    t, g, size = 256, plan.genes, plan.chunk
    tiles = plan.pair // t
    tile = lambda j: (j, 0)
    const = lambda j: (0, 0)
    halves = jax.ShapeDtypeStruct((size // 2, g), F32)
    return pl.pallas_call(
        functools.partial(gradient_kernel, plan, coef_gene, coef_spot),
        out_shape=(
            jax.ShapeDtypeStruct((plan.pair, g), BF16),
            jax.ShapeDtypeStruct((plan.pair, g), BF16),
            halves,
            halves,
            jax.ShapeDtypeStruct((8, LANES), F32),
        ),
        grid=(tiles,),
        in_specs=[
            pl.BlockSpec((t, g), tile),
            pl.BlockSpec((t, g), tile),
            pl.BlockSpec((t, LANES), tile),
            pl.BlockSpec((t, LANES), lambda j: ((j + tiles // 2) % tiles, 0)),
            pl.BlockSpec((t, LANES), tile),
            pl.BlockSpec((3 * ROWS, g), const),
            pl.BlockSpec((size, t), lambda j: (k, j)),
            pl.BlockSpec((size, t), lambda j: (k, j)),
        ],
        out_specs=[
            pl.BlockSpec((t, g), tile),
            pl.BlockSpec((t, g), tile),
            pl.BlockSpec((size // 2, g), const),
            pl.BlockSpec((size // 2, g), const),
            pl.BlockSpec((8, LANES), const),
        ],
        scratch_shapes=[pltpu.VMEM((2 * ROWS, g), BF16), pltpu.VMEM((2 * ROWS, g), BF16), pltpu.VMEM((size, g), F32)],
        compiler_params=params(plan),
        cost_estimate=cost(6 * plan.pair * g * size, plan.pair * g * 12),
        name="gradient",
    )(pred, spot, mine, other, meta, sums, mhi, mlo)


def cells_kernel(mhi_ref, mlo_ref, ghi_ref, glo_ref, keep_ref, send_ref):
    left = jnp.concatenate([mhi_ref[...], mhi_ref[...], mlo_ref[...]], axis=1)
    right = jnp.concatenate([ghi_ref[...], glo_ref[...], ghi_ref[...]], axis=0)
    value = jnp.dot(left, right, preferred_element_type=F32)
    n = keep_ref.shape[0]
    keep_ref[...] = value[0:n, :]
    send_ref[...] = value[n:, :]


def make_cells(plan, k, mhi, mlo, ghi, glo):
    t, g, size = 256, plan.genes, plan.chunk
    halves = jax.ShapeDtypeStruct((size // 2, g), F32)
    return pl.pallas_call(
        cells_kernel,
        out_shape=(halves, halves),
        grid=(g // t,),
        in_specs=[pl.BlockSpec((size, plan.pair), lambda i: (k, 0))] * 2 + [pl.BlockSpec((plan.pair, t), lambda i: (0, i))] * 2,
        out_specs=[pl.BlockSpec((size // 2, t), lambda i: (0, i))] * 2,
        compiler_params=params(plan),
        cost_estimate=cost(6 * plan.pair * g * size, plan.pair * g * 4),
        name="cells",
    )(mhi, mlo, ghi, glo)


def turned_dot(chi, clo, ghi, glo):
    left = jnp.concatenate([chi, chi, clo], axis=1)
    right = jnp.concatenate([ghi, glo, ghi], axis=1)
    return lax.dot_general(left, right, (((1,), (1,)), ((), ())), preferred_element_type=F32)


def other_kernel(chi_ref, clo_ref, ghi_ref, glo_ref, out_ref):
    out_ref[...] = turned_dot(chi_ref[...], clo_ref[...], ghi_ref[...], glo_ref[...])


def cell_tile(plan):
    return min(plan.cells, 1024)


def make_other(plan, chi, clo, ghi, glo):
    t, g, ct = plan.tile, plan.genes, cell_tile(plan)
    tiles = plan.half // t
    return pl.pallas_call(
        other_kernel,
        out_shape=jax.ShapeDtypeStruct((plan.cells, plan.half), F32),
        grid=(tiles, plan.cells // ct),
        in_specs=[pl.BlockSpec((ct, g), lambda j, i: (i, 0))] * 2 + [pl.BlockSpec((t, g), lambda j, i: (j + tiles, 0))] * 2,
        out_specs=pl.BlockSpec((ct, t), lambda j, i: (i, j)),
        compiler_params=params(plan),
        cost_estimate=cost(6 * plan.cells * g * plan.half, plan.cells * plan.half * 12),
        name="other",
    )(chi, clo, ghi, glo)


def logits_kernel(plan, coef_spot, place, chi_ref, clo_ref, ghi_ref, glo_ref, got_ref, mhi_ref, mlo_ref, cell_ref, meta_ref, row_ref,
                  out_ref, acc_ref):
    ct = cell_tile(plan)
    i = pl.program_id(1)
    rows = pl.ds(pl.multiple_of(i * ct, ct), ct)
    acc_ref[rows, :] = turned_dot(chi_ref[...], clo_ref[...], ghi_ref[...], glo_ref[...])

    @pl.when(i == pl.num_programs(1) - 1)
    def _():
        for k in range(plan.n_col):
            for m in range(plan.plane):
                at, there = (k * plan.plane + m) * plan.unit, (k * plan.plane + plan.reverse(m)) * plan.unit
                acc_ref[at : at + plan.unit, :] += got_ref[there : there + plan.unit, :]
        value = acc_ref[...]
        weight = mhi_ref[...].astype(F32) + mlo_ref[...].astype(F32)
        inner = jnp.sum(weight * value, axis=0, keepdims=True)
        meta = jnp.transpose(meta_ref[...])
        slide, coef = meta[0:1, :], coef_spot * meta[1:2, :]
        share = coef / row_ref[...][1:2, :]
        acc_ref[...] = weight * (value - inner + coef)
        for n, (k, m, c) in enumerate(blocks(plan)):
            start = pl.multiple_of(plan.block_start(place, k, m, c), plan.rows)
            cell = jnp.concatenate([cell_ref[pl.ds(start, plan.rows), :]] * (plan.tile // LANES), axis=1)
            out_ref[pl.ds(start, plan.rows), :] = acc_ref[n * plan.rows : (n + 1) * plan.rows, :] - jnp.where(cell == slide, share, 0.0)


def make_logits(plan, coef_spot, place, chi, clo, ghi, glo, got, mhi, mlo, cell, meta, row):
    t, g, ct = plan.tile, plan.genes, cell_tile(plan)
    column = lambda j, i, *_: (0, j)
    return pl.pallas_call(
        functools.partial(logits_kernel, plan, coef_spot),
        out_shape=jax.ShapeDtypeStruct((plan.cells, plan.half), F32),
        grid_spec=pltpu.PrefetchScalarGridSpec(
            num_scalar_prefetch=1,
            grid=(plan.half // t, plan.cells // ct),
            in_specs=[pl.BlockSpec((ct, g), lambda j, i, *_: (i, 0))] * 2
            + [pl.BlockSpec((t, g), lambda j, i, *_: (j, 0))] * 2
            + [pl.BlockSpec((plan.cells, t), column)] * 3
            + [
                pl.BlockSpec((plan.cells, LANES), lambda j, i, *_: (0, 0)),
                pl.BlockSpec((t, LANES), lambda j, i, *_: (j, 0)),
                pl.BlockSpec((8, t), column),
            ],
            out_specs=pl.BlockSpec((plan.cells, t), column),
            scratch_shapes=[pltpu.VMEM((plan.cells, t), F32)],
        ),
        compiler_params=params(plan, 28),
        cost_estimate=cost(6 * plan.cells * g * plan.half, plan.cells * plan.half * 20),
        name="logits",
    )(place, chi, clo, ghi, glo, got, mhi, mlo, cell, meta, row)


def on_device(plan, logits, cell_expr, spot_expr, cell_slide, spot_slide, spot_mask):
    g, rows = plan.genes, plan.rows
    spots_all = plan.half * plan.total
    factor = spots_all * plan.cells / SLIDES
    coef_spot = factor / spots_all
    coef_gene = factor / (SLIDES * 2 * g)
    spot_index, z = lax.axis_index("spot"), lax.axis_index("col")
    core, plane = spot_index % 2, spot_index // 2
    place = jnp.stack([plane, core, z]).astype(jnp.int32)
    send = lambda value, perm: lax.ppermute(value, AXES, perm)
    swap, ring = plan.swap_core(), plan.ring()
    hops = [plan.hop(step) for step in range(plan.bits)]

    def half_of(value, which):
        return lax.dynamic_slice_in_dim(value, which * g, g, 1)

    mine, got = half_of(cell_expr, core), send(half_of(cell_expr, 1 - core), swap)
    unit = jnp.where(core == 0, jnp.concatenate([mine, got]), jnp.concatenate([got, mine]))

    lane = lax.broadcasted_iota(jnp.int32, (plan.half, LANES), 1)
    meta_own = jnp.where(lane == 0, spot_slide[:, None], spot_mask[:, None]).astype(F32)
    meta_sib = send(meta_own, swap)
    meta = jnp.concatenate([meta_own, meta_sib])
    cell = jnp.broadcast_to(cell_slide[:, None].astype(F32), (plan.cells, LANES))
    logits_sib = send(logits, swap)
    spot_sib = send(half_of(spot_expr, 1 - core), swap)

    tie = lax.optimization_barrier
    made = {}
    whole = {}

    def work(slot):
        if slot == 0:
            made["spots"] = make_spots(plan, place, spot_expr, spot_sib, meta_own, meta_sib)
            return "spots"
        if slot == 1:
            made["mapping"] = make_mapping(plan, place, logits, logits_sib, cell, meta_own, meta_sib)
            return "mapping"
        if slot % 2 == 1:
            k = slot // 2 - 1
            _, _, hit, lot, _ = made["mapping"]
            made["carry"] = make_predict(plan, k, whole.pop(k), hit, lot, made.get("carry"))
            return "carry"
        return None

    slot = 0
    for k in range(plan.n_col):
        parts = [unit]
        following = send(unit, ring) if k + 1 < plan.n_col else None
        for step in range(plan.bits):
            came = send(jnp.concatenate(parts) if len(parts) > 1 else parts[0], hops[step])
            if step < 2:
                key = work(slot)
                slot += 1
                if key is not None and step + 1 < plan.bits:
                    came, made[key] = tie((came, made[key]))
                elif key is not None and following is not None:
                    following, made[key] = tie((following, made[key]))
            parts.append(came)
        whole[k] = parts
        unit = following
    mhi, mlo, hit, lot, row = made["mapping"]
    spot, true_sq, ng_part = made["spots"]
    carry = made["carry"]
    k = plan.n_col - 1
    pred, chi, clo, stat, sums = make_predict(plan, k, whole.pop(k), hit, lot, carry, (spot, true_sq, meta))

    stat_other = send(stat, swap)
    sums = jnp.concatenate([sums, ng_part])
    for step in range(plan.bits):
        sums = sums + send(sums, hops[step])
    step = 1
    while step < plan.n_col:
        sums = sums + send(
            sums, [(plan.device(q, c, i), plan.device(q, c, i ^ step)) for q, c, i in plan.all_places()]
        )
        step *= 2

    order = [k % plan.n_col for k in range(1, plan.n_col + 1)]
    ghi, glo, keep, away, cosines = make_gradient(
        plan, order[0], coef_gene, coef_spot, pred, spot, stat, stat_other, meta, sums, mhi, mlo
    )
    loss = (jnp.sum(row[0, : plan.half]) - cosines[0, 0]) / spots_all
    loss = loss - cosines[1, 0] / (SLIDES * 2 * g) / (plan.total // 2)
    loss = jnp.broadcast_to(loss, (8, LANES))
    loss_hops = [[(i, i ^ (1 << b)) for i in range(plan.total)] for b in range(plan.total.bit_length() - 1)]

    stages = plan.bits
    flows = []
    flows.append([stages - 1, keep, away])
    travelling = None
    tick = 0
    grad_logits = None
    other = None
    while flows or loss_hops or grad_logits is None:
        landed = [send(flow[2], hops[flow[0]]) for flow in flows if flow[0] >= 0]
        moved = send(travelling, ring) if travelling is not None else None
        loss_came = send(loss, loss_hops.pop(0)) if loss_hops else None
        made = None
        if tick + 1 < plan.n_col:
            made = make_cells(plan, order[tick + 1], mhi, mlo, ghi, glo)
        elif other is None:
            other = make_other(plan, chi, clo, ghi, glo)
            made = other
        elif grad_logits is None:
            grad_logits = make_logits(plan, coef_spot, place, chi, clo, ghi, glo, send(other, swap), mhi, mlo, cell, meta, row)
            made = grad_logits
        landed, moved, loss_came, made = tie((landed, moved, loss_came, made))
        if tick + 1 < plan.n_col:
            pass
        elif grad_logits is not None:
            grad_logits = made
        else:
            other = made
        if loss_came is not None:
            loss = loss + loss_came
        for flow, came in zip(flows, landed):
            keep = flow[1] + came
            flow[0] -= 1
            if flow[0] >= 0:
                n = keep.shape[0] // 2
                flow[1], flow[2] = keep[:n], keep[n:]
            else:
                flow[1], flow[2] = keep, None
        travelling = None
        if flows and flows[0][0] < 0:
            travelling = flows.pop(0)[1]
            if moved is not None:
                travelling = travelling + moved
        if tick + 1 < plan.n_col:
            flows.append([stages - 1, *made])
        tick += 1
        if not flows and travelling is not None:
            result = travelling
            travelling = None
    mine = lax.dynamic_slice_in_dim(result, core * rows, rows, 0)
    got = send(lax.dynamic_slice_in_dim(result, (1 - core) * rows, rows, 0), swap)
    grad_expr = jnp.where(core == 0, jnp.concatenate([mine, got], axis=1), jnp.concatenate([got, mine], axis=1))
    return loss[0, 0], grad_logits, grad_expr


def solution(mesh):
    in_specs = (
        P(None, AXES),
        P(AXES, None),
        P(AXES, None),
        P(),
        P(AXES),
        P(AXES),
    )
    out_specs = (P(), P(None, AXES), P(AXES, None))

    def whole(logits, cell_expr, spot_expr, cell_slide, spot_slide, spot_mask):
        n_spot, n_col = mesh.shape["spot"], mesh.shape["col"]
        plan = Plan(n_spot, n_col, logits.shape[0], logits.shape[1] // (n_spot * n_col), cell_expr.shape[1])
        return jax.shard_map(
            functools.partial(on_device, plan), mesh=mesh, in_specs=in_specs, out_specs=out_specs, check_vma=False
        )(logits, cell_expr, spot_expr, cell_slide, spot_slide, spot_mask)

    return whole
```

```python
import functools

import jax
import jax.numpy as jnp
from jax import lax
from jax.experimental import pallas as pl
from jax.experimental.pallas import tpu as pltpu
from jax.sharding import PartitionSpec as P

SLIDES = 11
ROWS = 16
PACKED = 40
PREDICT_TILE = 512
SCALE = 1.0
EPS = 1e-06
AXES = ("spot", "col")
F32 = jnp.float32
BF16 = jnp.bfloat16
LANES = 128


def split(x):
    hi = x.astype(BF16)
    return hi, (x - hi.astype(F32)).astype(BF16)


def params(plan, small=16):
    return pltpu.CompilerParams(vmem_limit_bytes=(small if plan.cells <= 2048 else 60) << 20)


def kept(plan, shape, dtype):
    return pltpu.VMEM(shape, dtype) if plan.cells <= 2048 else jax.ShapeDtypeStruct(shape, dtype)


def pin(plan, *values):
    if plan.cells > 2048:
        return values
    return tuple(pltpu.with_memory_space_constraint(v, pltpu.VMEM) for v in values)


def cost(flops, bytes_accessed):
    return pl.CostEstimate(flops=int(flops * SCALE), bytes_accessed=int(bytes_accessed * SCALE), transcendentals=0)


class Plan:
    def __init__(self, n_spot, n_col, cells, spots, genes):
        self.n_col = n_col
        self.plane = n_spot // 2
        self.bits = self.plane.bit_length() - 1
        self.rows = cells // (n_spot * n_col)
        self.cells = cells
        self.half = spots
        self.pair = 2 * spots
        self.genes = genes // 2
        self.unit = 2 * self.rows
        self.chunk = self.plane * self.unit
        self.n_spot = n_spot
        self.total = n_spot * n_col
        self.tile = 256 if cells <= 2048 else 128

    def order(self, core):
        return list(range(self.bits)) if core == 0 else list(range(self.bits))[::-1]

    def reverse(self, m):
        return sum(((m >> b) & 1) << (self.bits - 1 - b) for b in range(self.bits))

    def device(self, plane, core, z):
        return (plane * 2 + core) * self.n_col + z

    def all_places(self):
        for plane in range(self.plane):
            for core in range(2):
                for z in range(self.n_col):
                    yield plane, core, z

    def swap_core(self):
        return [(self.device(q, c, z), self.device(q, 1 - c, z)) for q, c, z in self.all_places()]

    def shift(self, k):
        return [(self.device(q, c, z), self.device(q, c, (z + k) % self.n_col)) for q, c, z in self.all_places()]

    def hop(self, step):
        return [
            (self.device(q, c, z), self.device(q ^ (1 << self.order(c)[step]), c, z))
            for q, c, z in self.all_places()
        ]

    def block_start(self, place_ref, k, m, c):
        plane, core, z = place_ref[0], place_ref[1], place_ref[2]
        shift = [0, 0]
        for which in range(2):
            for step, bit in enumerate(self.order(which)):
                shift[which] |= ((m >> step) & 1) << bit
        xor = jnp.where(core == 0, shift[0], shift[1])
        q = jnp.bitwise_xor(plane, xor)
        ring = lax.rem(z - k + self.n_col, self.n_col)
        return ((q * 2 + c) * self.n_col + ring) * self.rows


def blocks(plan):
    for k in range(plan.n_col):
        for m in range(plan.plane):
            for c in range(2):
                yield k, m, c


def mapping_kernel(plan, again, place, logits_ref, cell_ref, meta_ref, *refs):
    hi_ref, lo_ref, hit_ref, lot_ref, row_ref, w_ref = refs[4:] if again else refs
    meta = jnp.transpose(meta_ref[...])
    slide = meta[0:1, :]
    cell = jnp.concatenate([cell_ref[...]] * (plan.tile // LANES), axis=1)
    same = cell == slide
    x = logits_ref[...]
    masked = jnp.where(same, x, -jnp.inf)
    col_max = jnp.max(masked, axis=0, keepdims=True)
    w = jnp.exp(masked - col_max)
    total = jnp.sum(w, axis=0, keepdims=True)
    w_ref[...] = w * (1.0 / total)
    if again:
        row_ref[...] = jnp.zeros_like(row_ref)
    else:
        counts = jnp.sum(jnp.where(same, 1.0, 0.0), axis=0, keepdims=True)
        mean = jnp.sum(jnp.where(same, x, 0.0), axis=0, keepdims=True) / counts
        kl = (col_max + jnp.log(total) - mean - jnp.log(counts)) * meta[1:2, :]
        row = lax.broadcasted_iota(jnp.int32, (8, plan.tile), 0)
        row_ref[...] = jnp.where(row == 0, kl, counts)
    gather = max(LANES // plan.rows, 1)
    held = []
    for i, (k, m, c) in enumerate(blocks(plan)):
        start = pl.multiple_of(plan.block_start(place, k, m, c), plan.rows)
        block = w_ref[pl.ds(start, plan.rows), :]
        hi, lo = split(block)
        hi_ref[i * plan.rows : (i + 1) * plan.rows, :] = hi
        lo_ref[i * plan.rows : (i + 1) * plan.rows, :] = lo
        held.append(block)
        if len(held) == gather:
            wide = jnp.transpose(jnp.concatenate(held, axis=0))
            hi, lo = split(wide)
            end = (i + 1) * plan.rows
            hit_ref[:, end - LANES : end] = hi
            lot_ref[:, end - LANES : end] = lo
            held = []


def make_mapping(plan, place, logits, cell, meta, earlier=None):
    t, tiles = plan.tile, plan.half // plan.tile
    again = earlier is not None
    at = tiles if again else 0
    wide = kept(plan, (plan.cells, plan.pair), BF16)
    tall = kept(plan, (plan.pair, plan.cells), BF16)
    operands = [place, logits, cell, meta]
    in_specs = [
        pl.BlockSpec((plan.cells, t), lambda j, *_: (0, j)),
        pl.BlockSpec((plan.cells, LANES), lambda j, *_: (0, 0)),
        pl.BlockSpec((t, LANES), lambda j, *_: (j, 0)),
    ]
    if again:
        operands += list(pin(plan, *earlier[:4]))
        in_specs += [pl.BlockSpec(memory_space=pl.ANY)] * 4
    return pl.pallas_call(
        functools.partial(mapping_kernel, plan, again),
        out_shape=(wide, wide, tall, tall, jax.ShapeDtypeStruct((8, plan.half), F32)),
        grid_spec=pltpu.PrefetchScalarGridSpec(
            num_scalar_prefetch=1,
            grid=(tiles,),
            in_specs=in_specs,
            out_specs=[
                pl.BlockSpec((plan.cells, t), lambda j, *_: (0, j + at)),
                pl.BlockSpec((plan.cells, t), lambda j, *_: (0, j + at)),
                pl.BlockSpec((t, plan.cells), lambda j, *_: (j + at, 0)),
                pl.BlockSpec((t, plan.cells), lambda j, *_: (j + at, 0)),
                pl.BlockSpec((8, t), lambda j, *_: (0, j)),
            ],
            scratch_shapes=[pltpu.VMEM((plan.cells, t), F32)],
        ),
        input_output_aliases={4 + i: i for i in range(4)} if again else {},
        compiler_params=params(plan),
        cost_estimate=cost(plan.cells * plan.half * 20, plan.cells * plan.half * 12),
        name="mapping",
    )(*operands)


def onehot_rows(plan, meta):
    turned = jnp.transpose(meta)
    slide = lax.broadcasted_iota(jnp.int32, (ROWS, meta.shape[0]), 0).astype(F32)
    return jnp.where(turned[0:1, :] == slide, turned[1:2, :], 0.0).astype(BF16)


def slide_sum(onehot, value):
    hi, lo = split(value)
    return jnp.dot(
        jnp.concatenate([onehot, onehot], axis=1),
        jnp.concatenate([hi, lo], axis=0),
        preferred_element_type=F32,
    )


def row_sum(value):
    return jnp.sum(value, axis=1, keepdims=True)


def spots_kernel(plan, place, own_ref, sib_ref, meta_own, meta_sib, spot_ref, stat_ref, ng_ref):
    tiles = plan.half // 256
    j = pl.program_id(0)

    @pl.when(j == 0)
    def _():
        ng_ref[...] = jnp.zeros_like(ng_ref)

    def run(value_ref, meta_ref):
        value = value_ref[...]
        square = value * value
        spot_ref[...] = value
        stat_ref[...] = jnp.broadcast_to(row_sum(square), stat_ref.shape)
        ng_ref[...] += slide_sum(onehot_rows(plan, meta_ref[...]), square)

    @pl.when(j < tiles)
    def _():
        run(own_ref, meta_own)

    @pl.when(j >= tiles)
    def _():
        run(sib_ref, meta_sib)


def make_spots(plan, place, own, sib, meta_own, meta_sib):
    t, tiles, g = 256, plan.half // 256, plan.genes
    return pl.pallas_call(
        functools.partial(spots_kernel, plan),
        out_shape=(
            kept(plan, (plan.pair, g), F32),
            kept(plan, (plan.pair, LANES), F32),
            jax.ShapeDtypeStruct((ROWS, g), F32),
        ),
        grid_spec=pltpu.PrefetchScalarGridSpec(
            num_scalar_prefetch=1,
            grid=(2 * tiles,),
            in_specs=[
                pl.BlockSpec((t, g), lambda j, place: (jnp.minimum(j, tiles - 1), place[1])),
                pl.BlockSpec((t, g), lambda j, place: (jnp.maximum(j - tiles, 0), place[1])),
                pl.BlockSpec((t, LANES), lambda j, place: (jnp.minimum(j, tiles - 1), 0)),
                pl.BlockSpec((t, LANES), lambda j, place: (jnp.maximum(j - tiles, 0), 0)),
            ],
            out_specs=[
                pl.BlockSpec((t, g), lambda j, place: (j, 0)),
                pl.BlockSpec((t, LANES), lambda j, place: (j, 0)),
                pl.BlockSpec((ROWS, g), lambda j, place: (0, 0)),
            ],
        ),
        compiler_params=params(plan),
        cost_estimate=cost(plan.pair * g * 64, plan.pair * g * 8),
        name="spots",
    )(place, own, sib, meta_own, meta_sib)


def predict_kernel(plan, n_parts, first, last, *refs):
    refs = list(refs)
    parts = [refs.pop(0) for _ in range(n_parts)]
    hit_ref, lot_ref = refs.pop(0), refs.pop(0)
    acc_in = None
    if not first:
        acc_in = refs.pop(0)
        refs.pop(0), refs.pop(0)
    if last:
        spot_ref, gg_ref, meta_ref, ng_ref = refs.pop(0), refs.pop(0), refs.pop(0), refs.pop(0)
    acc_ref, chi_ref, clo_ref = refs.pop(0), refs.pop(0), refs.pop(0)
    if last:
        stat_ref, sums_ref = refs.pop(0), refs.pop(0)
    stack_ref = refs.pop(0)
    j = pl.program_id(0)
    size = plan.chunk

    @pl.when(j == 0)
    def _():
        at = 0
        for part in parts:
            n = part.shape[0]
            hi, lo = split(part[...])
            stack_ref[at : at + n, :] = hi
            stack_ref[size + at : size + at + n, :] = lo
            stack_ref[2 * size + at : 2 * size + at + n, :] = hi
            chi_ref[at : at + n, :] = hi
            clo_ref[at : at + n, :] = lo
            at += n
        if last:
            sums_ref[...] = jnp.zeros_like(sums_ref)

    left = jnp.concatenate([hit_ref[...], hit_ref[...], lot_ref[...]], axis=1)
    value = jnp.dot(left, stack_ref[...], preferred_element_type=F32)
    if not first:
        value = value + acc_in[...]
    acc_ref[...] = value
    if last:
        spot = spot_ref[...]
        square, cross = value * value, value * spot
        lane = lax.broadcasted_iota(jnp.int32, stat_ref.shape, 1)
        stat_ref[...] = jnp.where(lane == 0, row_sum(square), jnp.where(lane == 1, row_sum(cross), gg_ref[...]))
        turned = jnp.transpose(meta_ref[...])
        row = lax.broadcasted_iota(jnp.int32, (PACKED, value.shape[0]), 0).astype(F32)
        pick = lambda first: jnp.where(turned[0:1, :] + first == row, turned[1:2, :], 0.0).astype(BF16)
        left = jnp.concatenate([pick(0), pick(0), pick(SLIDES), pick(SLIDES)], axis=1)
        right = jnp.concatenate([*split(square), *split(cross)], axis=0)
        sums_ref[...] += jnp.dot(left, right, preferred_element_type=F32)

        @pl.when(j == 0)
        def _():
            sums_ref[2 * SLIDES : 3 * SLIDES, :] += ng_ref[0:SLIDES, :]


def make_predict(plan, k, parts, hit, lot, carry, last=None):
    t, g, size = PREDICT_TILE if plan.cells <= 2048 else 256, plan.genes, plan.chunk
    const = lambda j: (0, 0)
    in_specs = [pl.BlockSpec(p.shape, const) for p in parts]
    in_specs += [pl.BlockSpec((t, size), lambda j: (j, k))] * 2
    operands = [*parts, *pin(plan, hit, lot)]
    aliases = {}
    if carry is not None:
        at = len(operands)
        operands += list(pin(plan, *carry))
        in_specs += [pl.BlockSpec((t, g), lambda j: (j, 0)), pl.BlockSpec(memory_space=pl.ANY), pl.BlockSpec(memory_space=pl.ANY)]
        aliases = {at: 0, at + 1: 1, at + 2: 2}
    out_shape = [
        kept(plan, (plan.pair, g), F32),
        kept(plan, (plan.cells, g), BF16),
        kept(plan, (plan.cells, g), BF16),
    ]
    out_specs = [pl.BlockSpec((t, g), lambda j: (j, 0))] + [pl.BlockSpec((size, g), lambda j: (k, 0))] * 2
    if last is not None:
        operands += list(pin(plan, *last[:2])) + list(last[2:])
        in_specs += [pl.BlockSpec((t, g), lambda j: (j, 0))] + [pl.BlockSpec((t, LANES), lambda j: (j, 0))] * 2
        in_specs += [pl.BlockSpec((ROWS, g), const)]
        out_shape += [jax.ShapeDtypeStruct((plan.pair, LANES), F32), jax.ShapeDtypeStruct((PACKED, g), F32)]
        out_specs += [pl.BlockSpec((t, LANES), lambda j: (j, 0)), pl.BlockSpec((PACKED, g), const)]
    return pl.pallas_call(
        functools.partial(predict_kernel, plan, len(parts), carry is None, last is not None),
        out_shape=tuple(out_shape),
        grid=(plan.pair // t,),
        in_specs=in_specs,
        out_specs=out_specs,
        scratch_shapes=[pltpu.VMEM((3 * size, g), BF16)],
        input_output_aliases=aliases,
        compiler_params=params(plan),
        cost_estimate=cost(6 * plan.pair * g * size, plan.pair * g * 8),
        name="predict",
    )(*operands)


def spot_loss_kernel(plan, mine_ref, other_ref, meta_ref, row_ref, out_ref):
    stat = mine_ref[0 : plan.half, :] + other_ref[plan.half :, :]
    cosine = stat[:, 1:2] * (lax.rsqrt(stat[:, 0:1] + EPS) * lax.rsqrt(stat[:, 2:3] + EPS))
    total = jnp.sum(row_ref[0:1, :], keepdims=True) - jnp.sum(cosine * meta_ref[...][0 : plan.half, 1:2], keepdims=True)
    row = lax.broadcasted_iota(jnp.int32, out_ref.shape, 0)
    out_ref[...] = jnp.where(row == (3 * SLIDES) % 8, total / (plan.half * plan.total), 0.0)


def make_spot_loss(plan, mine, other, meta, row):
    return pl.pallas_call(
        functools.partial(spot_loss_kernel, plan),
        out_shape=jax.ShapeDtypeStruct((8, plan.genes), F32),
        in_specs=[pl.BlockSpec(memory_space=pltpu.VMEM)] * 4,
        out_specs=pl.BlockSpec(memory_space=pltpu.VMEM),
        compiler_params=params(plan),
        cost_estimate=cost(plan.half * 8, plan.half * 1024),
        name="spot_loss",
    )(*pin(plan, mine), other, meta, row)


def gradient_kernel(plan, coef_gene, coef_spot, pred_ref, spot_ref, mine_ref, other_ref, meta_ref, sums_ref,
                    mhi_ref, mlo_ref, ghi_ref, glo_ref, keep_ref, send_ref, loss_ref, a_ref, b_ref, acc_ref):
    j = pl.program_id(0)

    @pl.when(j == 0)
    def _():
        pad = jnp.zeros((ROWS - SLIDES, sums_ref.shape[1]), F32)
        parts = [sums_ref[i * SLIDES : (i + 1) * SLIDES, :] for i in range(3)]
        np_sum, dots, ng_sum = [jnp.concatenate([part, pad], axis=0) for part in parts]
        scale = lax.rsqrt(np_sum + EPS) * lax.rsqrt(ng_sum + EPS)
        cosine = dots * scale
        hi, lo = split(-coef_gene * scale)
        a_ref[0:ROWS, :] = hi
        a_ref[ROWS : 2 * ROWS, :] = lo
        hi, lo = split(coef_gene * (cosine / (np_sum + EPS)))
        b_ref[0:ROWS, :] = hi
        b_ref[ROWS : 2 * ROWS, :] = lo
        acc_ref[...] = jnp.zeros_like(acc_ref)
        row = lax.broadcasted_iota(jnp.int32, cosine.shape, 0)
        gene = jnp.sum(jnp.where(row < SLIDES, cosine, 0.0), keepdims=True) / (SLIDES * 2 * plan.genes)
        loss_ref[...] = jnp.broadcast_to(-gene, loss_ref.shape)

    stat = mine_ref[...] + other_ref[...]
    spot_sq, cross, true_sq = stat[:, 0:1], stat[:, 1:2], stat[:, 2:3]
    slide, mask = meta_ref[...][:, 0:1], meta_ref[...][:, 1:2]
    scale = lax.rsqrt(spot_sq + EPS) * lax.rsqrt(true_sq + EPS)
    cosine = cross * scale

    weight = coef_spot * mask
    lane = lax.broadcasted_iota(jnp.int32, (stat.shape[0], ROWS), 1).astype(F32)
    onehot = jnp.where(slide == lane, mask, 0.0).astype(BF16)
    onehot = jnp.concatenate([onehot, onehot], axis=1)
    gene_a = jnp.dot(onehot, a_ref[...], preferred_element_type=F32)
    gene_b = jnp.dot(onehot, b_ref[...], preferred_element_type=F32)
    grad = spot_ref[...] * (gene_a - weight * scale) + pred_ref[...] * (gene_b + weight * (cosine / (spot_sq + EPS)))
    hi, lo = split(grad)
    ghi_ref[...] = hi
    glo_ref[...] = lo
    left = jnp.concatenate([mhi_ref[...], mhi_ref[...], mlo_ref[...]], axis=1)
    right = jnp.concatenate([hi, lo, hi], axis=0)
    acc_ref[...] += jnp.dot(left, right, preferred_element_type=F32)

    @pl.when(j == pl.num_programs(0) - 1)
    def _():
        n = keep_ref.shape[0]
        keep_ref[...] = acc_ref[0:n, :]
        send_ref[...] = acc_ref[n:, :]


def make_gradient(plan, k, coef_gene, coef_spot, pred, spot, mine, other, meta, sums, mhi, mlo):
    t, g, size = 256, plan.genes, plan.chunk
    tiles = plan.pair // t
    tile = lambda j: (j, 0)
    const = lambda j: (0, 0)
    halves = jax.ShapeDtypeStruct((size // 2, g), F32)
    return pl.pallas_call(
        functools.partial(gradient_kernel, plan, coef_gene, coef_spot),
        out_shape=(
            kept(plan, (plan.pair, g), BF16),
            kept(plan, (plan.pair, g), BF16),
            halves,
            halves,
            jax.ShapeDtypeStruct((8, LANES), F32),
        ),
        grid=(tiles,),
        in_specs=[
            pl.BlockSpec((t, g), tile),
            pl.BlockSpec((t, g), tile),
            pl.BlockSpec((t, LANES), tile),
            pl.BlockSpec((t, LANES), lambda j: ((j + tiles // 2) % tiles, 0)),
            pl.BlockSpec((t, LANES), tile),
            pl.BlockSpec((PACKED, g), const),
            pl.BlockSpec((size, t), lambda j: (k, j)),
            pl.BlockSpec((size, t), lambda j: (k, j)),
        ],
        out_specs=[
            pl.BlockSpec((t, g), tile),
            pl.BlockSpec((t, g), tile),
            pl.BlockSpec((size // 2, g), const),
            pl.BlockSpec((size // 2, g), const),
            pl.BlockSpec((8, LANES), const),
        ],
        scratch_shapes=[pltpu.VMEM((2 * ROWS, g), BF16), pltpu.VMEM((2 * ROWS, g), BF16), pltpu.VMEM((size, g), F32)],
        compiler_params=params(plan),
        cost_estimate=cost(6 * plan.pair * g * size, plan.pair * g * 12),
        name="gradient",
    )(*pin(plan, pred, spot), mine, other, meta, sums, *pin(plan, mhi, mlo))


def cells_kernel(plan, ks, whole, mhi_ref, mlo_ref, ghi_ref, glo_ref, *outs):
    def rows(ref):
        if not whole:
            return ref[...]
        return jnp.concatenate([ref[k * plan.chunk : (k + 1) * plan.chunk, :] for k in ks], axis=0)

    hi, lo = rows(mhi_ref), rows(mlo_ref)
    left = jnp.concatenate([hi, hi, lo], axis=1)
    right = jnp.concatenate([ghi_ref[...], glo_ref[...], ghi_ref[...]], axis=0)
    value = jnp.dot(left, right, preferred_element_type=F32)
    at = 0
    for out in outs:
        out[...] = value[at : at + out.shape[0], :]
        at += out.shape[0]


def make_cells(plan, ks, sizes, mhi, mlo, ghi, glo):
    t, g, size = 256, plan.genes, plan.chunk
    whole = len(ks) > 1
    rows = (plan.cells, plan.pair) if whole else (size, plan.pair)
    at = 0 if whole else ks[0]
    return pl.pallas_call(
        functools.partial(cells_kernel, plan, ks, whole),
        out_shape=tuple(jax.ShapeDtypeStruct((n, g), F32) for n in sizes),
        grid=(g // t,),
        in_specs=[pl.BlockSpec(rows, lambda i: (at, 0))] * 2 + [pl.BlockSpec((plan.pair, t), lambda i: (0, i))] * 2,
        out_specs=[pl.BlockSpec((n, t), lambda i: (0, i)) for n in sizes],
        compiler_params=params(plan),
        cost_estimate=cost(6 * plan.pair * g * size * len(ks), plan.pair * g * 4),
        name="cells",
    )(*pin(plan, mhi, mlo, ghi, glo))


def turned_dot(chi, clo, ghi, glo):
    left = jnp.concatenate([chi, chi, clo], axis=1)
    right = jnp.concatenate([ghi, glo, ghi], axis=1)
    return lax.dot_general(left, right, (((1,), (1,)), ((), ())), preferred_element_type=F32)


def other_kernel(chi_ref, clo_ref, ghi_ref, glo_ref, out_ref):
    out_ref[...] = turned_dot(chi_ref[...], clo_ref[...], ghi_ref[...], glo_ref[...])


def cell_tile(plan):
    return min(plan.cells, 1024)


def make_other(plan, chi, clo, ghi, glo):
    t, g, ct = plan.tile, plan.genes, cell_tile(plan)
    tiles = plan.half // t
    return pl.pallas_call(
        other_kernel,
        out_shape=jax.ShapeDtypeStruct((plan.cells, plan.half), F32),
        grid=(tiles, plan.cells // ct),
        in_specs=[pl.BlockSpec((ct, g), lambda j, i: (i, 0))] * 2 + [pl.BlockSpec((t, g), lambda j, i: (j + tiles, 0))] * 2,
        out_specs=pl.BlockSpec((ct, t), lambda j, i: (i, j)),
        compiler_params=params(plan),
        cost_estimate=cost(6 * plan.cells * g * plan.half, plan.cells * plan.half * 12),
        name="other",
    )(*pin(plan, chi, clo, ghi, glo))


def logits_kernel(plan, coef_spot, place, chi_ref, clo_ref, ghi_ref, glo_ref, got_ref, mhi_ref, mlo_ref, cell_ref, meta_ref, row_ref,
                  out_ref, acc_ref):
    ct = cell_tile(plan)
    i = pl.program_id(1)
    rows = pl.ds(pl.multiple_of(i * ct, ct), ct)
    acc_ref[rows, :] = turned_dot(chi_ref[...], clo_ref[...], ghi_ref[...], glo_ref[...])

    @pl.when(i == pl.num_programs(1) - 1)
    def _():
        for k in range(plan.n_col):
            for m in range(plan.plane):
                at, there = (k * plan.plane + m) * plan.unit, (k * plan.plane + plan.reverse(m)) * plan.unit
                acc_ref[at : at + plan.unit, :] += got_ref[there : there + plan.unit, :]
        value = acc_ref[...]
        weight = mhi_ref[...].astype(F32) + mlo_ref[...].astype(F32)
        inner = jnp.sum(weight * value, axis=0, keepdims=True)
        meta = jnp.transpose(meta_ref[...])
        slide, coef = meta[0:1, :], coef_spot * meta[1:2, :]
        share = coef / row_ref[...][1:2, :]
        acc_ref[...] = weight * (value - inner + coef)
        for n, (k, m, c) in enumerate(blocks(plan)):
            start = pl.multiple_of(plan.block_start(place, k, m, c), plan.rows)
            cell = jnp.concatenate([cell_ref[pl.ds(start, plan.rows), :]] * (plan.tile // LANES), axis=1)
            out_ref[pl.ds(start, plan.rows), :] = acc_ref[n * plan.rows : (n + 1) * plan.rows, :] - jnp.where(cell == slide, share, 0.0)


def make_logits(plan, coef_spot, place, chi, clo, ghi, glo, got, mhi, mlo, cell, meta, row):
    t, g, ct = plan.tile, plan.genes, cell_tile(plan)
    column = lambda j, i, *_: (0, j)
    return pl.pallas_call(
        functools.partial(logits_kernel, plan, coef_spot),
        out_shape=jax.ShapeDtypeStruct((plan.cells, plan.half), F32),
        grid_spec=pltpu.PrefetchScalarGridSpec(
            num_scalar_prefetch=1,
            grid=(plan.half // t, plan.cells // ct),
            in_specs=[pl.BlockSpec((ct, g), lambda j, i, *_: (i, 0))] * 2
            + [pl.BlockSpec((t, g), lambda j, i, *_: (j, 0))] * 2
            + [pl.BlockSpec((plan.cells, t), column)] * 3
            + [
                pl.BlockSpec((plan.cells, LANES), lambda j, i, *_: (0, 0)),
                pl.BlockSpec((t, LANES), lambda j, i, *_: (j, 0)),
                pl.BlockSpec((8, t), column),
            ],
            out_specs=pl.BlockSpec((plan.cells, t), column),
            scratch_shapes=[pltpu.VMEM((plan.cells, t), F32)],
        ),
        compiler_params=params(plan, 24),
        cost_estimate=cost(6 * plan.cells * g * plan.half, plan.cells * plan.half * 20),
        name="logits",
    )(place, *pin(plan, chi, clo, ghi, glo), got, *pin(plan, mhi, mlo), cell, meta, row)


def on_device(plan, logits, cell_expr, spot_expr, cell_slide, spot_slide, spot_mask):
    g, rows = plan.genes, plan.rows
    spots_all = plan.half * plan.total
    factor = spots_all * plan.cells / SLIDES
    coef_spot = factor / spots_all
    coef_gene = factor / (SLIDES * 2 * g)
    spot_index, z = lax.axis_index("spot"), lax.axis_index("col")
    core, plane = spot_index % 2, spot_index // 2
    place = jnp.stack([plane, core, z]).astype(jnp.int32)
    send = lambda value, perm: lax.ppermute(value, AXES, perm)
    swap = plan.swap_core()
    hops = [plan.hop(step) for step in range(plan.bits)]

    tie = lax.optimization_barrier
    got, is_first = send(cell_expr, swap), core == 0
    got, logits, spot_expr, spot_slide, place, is_first = tie((got, logits, spot_expr, spot_slide, place, is_first))
    first, second = jnp.concatenate([cell_expr[:, :g], got[:, :g]]), jnp.concatenate([got[:, g:], cell_expr[:, g:]])
    unit = jnp.where(is_first, first, second)
    lane = lax.broadcasted_iota(jnp.int32, (plan.half, LANES), 1)
    meta_own = jnp.where(lane == 0, spot_slide[:, None], spot_mask[:, None]).astype(F32)
    cell = jnp.broadcast_to(cell_slide[:, None].astype(F32), (plan.cells, LANES))
    logits_sib = send(logits, swap)
    meta_sib = send(meta_own, swap)
    meta = jnp.concatenate([meta_own, meta_sib])

    plane_hops = [("plane", 1 << bit) for bit in range(plan.bits)]
    ring_hops = [("ring", 1 << bit) for bit in range(plan.n_col.bit_length() - 1)]
    sum_orders = (plane_hops + ring_hops, ring_hops + plane_hops)

    def sum_hop(index):
        perm = []
        for q, c, i in plan.all_places():
            kind, bit = sum_orders[c][index]
            there = plan.device(q ^ bit, c, i) if kind == "plane" else plan.device(q, c, i ^ bit)
            perm.append((plan.device(q, c, i), there))
        return perm

    sum_hops = [sum_hop(index) for index in range(len(plane_hops) + len(ring_hops))]

    order = sorted(range(plan.n_col), key=lambda k: (min(k, plan.n_col - k), k))
    units = {0: unit}
    for k in order[1:-1]:
        units[k] = send(unit, plan.shift(k))
    mapping = make_mapping(plan, place, logits, cell, meta_own)
    units[order[-1]] = send(unit, plan.shift(order[-1]))
    logits_sib, spot_expr, mapping = tie((logits_sib, spot_expr, mapping))
    spot_sib = send(spot_expr, swap)
    row = mapping[4]
    carry = None
    whole = {}

    def predict(i):
        return make_predict(plan, order[i], whole.pop(order[i]), mapping[2], mapping[3], carry)

    for i, k in enumerate(order):
        following = order[i + 1] if i + 1 < plan.n_col else None
        parts = [units[k]]
        apart = i == 0 or following is None
        for step in range(plan.bits):
            if apart:
                came = [send(part, hops[step]) for part in parts]
            else:
                came = [send(jnp.concatenate(parts) if len(parts) > 1 else parts[0], hops[step])]
            if step == 0:
                if i == 0:
                    done = make_mapping(plan, place, logits_sib, cell, meta_sib, mapping)
                elif i == 1:
                    done = make_spots(plan, place, spot_expr, spot_sib, meta_own, meta_sib)
                else:
                    done = predict(i - 2)
                came, done = tie((came, done))
                if following is not None:
                    units[following], done = tie((units[following], done))
                if i == 0:
                    mapping = done
                elif i == 1:
                    spot, true_sq, ng_part = done
                else:
                    carry = done
            parts = parts + came
        whole[k] = parts
    mhi, mlo, hit, lot, _ = mapping
    carry = predict(plan.n_col - 2)
    k = order[-1]
    pred, chi, clo, stat, sums = make_predict(plan, k, whole.pop(k), hit, lot, carry, (spot, true_sq, meta, ng_part))
    stat_other = send(stat, swap)
    spot_loss = make_spot_loss(plan, stat, stat_other, meta, row)
    for index, perm in enumerate(sum_hops):
        came = send(sums, perm)
        if index == 0:
            came, spot_loss = tie((came, spot_loss))
            sums = sums + came + jnp.concatenate([jnp.zeros((PACKED - 8, g), F32), spot_loss])
        else:
            sums = sums + came

    order = order[::-1]
    ghi, glo, keep, away, loss = make_gradient(
        plan, order[0], coef_gene, coef_spot, pred, spot, stat, stat_other, meta, sums, mhi, mlo
    )
    half = plan.chunk // 2
    sizes = [half] * (2 * (plan.n_col - 1))
    keeps, aways, first_hop = {0: keep}, {0: away}, hops[-1]
    came = send(away, first_hop)
    if plan.cells <= 2048:
        made = make_cells(plan, order[1:], sizes, mhi, mlo, ghi, glo)
        came, made = tie((came, made))
    else:
        made = sum([list(make_cells(plan, [k], [half, half], mhi, mlo, ghi, glo)) for k in order[1:]], [])
    for i in range(1, plan.n_col):
        keeps[i], aways[i] = made[2 * i - 2], made[2 * i - 1]
    landing = {0: came, 1: send(aways[1], first_hop)}
    arrived = []
    other_sib = grad_logits = None
    for i, k in enumerate(order):
        came, keep = landing[i], keeps[i]
        if i + 2 < plan.n_col:
            came, aways[i + 2] = tie((came, aways[i + 2]))
            landing[i + 2] = send(aways[i + 2], first_hop)
        for step in reversed(range(plan.bits)):
            keep = keep + came
            if step > 0:
                n = keep.shape[0] // 2
                keep, came = keep[:n], send(keep[n:], hops[step - 1])
            if step == 1 and i == 0:
                other = make_other(plan, chi, clo, ghi, glo)
                came, other = tie((came, other))
                landing[1], other = tie((landing[1], other))
                other_sib = send(other, swap)
            elif step == 1 and i == 1:
                grad_logits = make_logits(plan, coef_spot, place, chi, clo, ghi, glo, other_sib, mhi, mlo, cell, meta, row)
                came, grad_logits = tie((came, grad_logits))
        arrived.append(send(keep, plan.shift(plan.n_col - k)) if k > 0 else keep)
    result = sum(arrived[1:], arrived[0])
    got = send(result, swap)
    first = jnp.concatenate([result[:rows], got[:rows]], axis=1)
    second = jnp.concatenate([got[rows:], result[rows:]], axis=1)
    grad_expr = jnp.where(is_first, first, second)
    part = sums[PACKED - 8 :, :LANES]
    part = part + send(part, sum_hops[0])
    part = part[(3 * SLIDES) % 8 : (3 * SLIDES) % 8 + 1, :] + loss[0:1, :]
    part = part + send(part, swap)
    return part[0, 0], grad_logits, grad_expr


def solution(mesh):
    in_specs = (
        P(None, AXES),
        P(AXES, None),
        P(AXES, None),
        P(),
        P(AXES),
        P(AXES),
    )
    out_specs = (P(), P(None, AXES), P(AXES, None))

    def whole(logits, cell_expr, spot_expr, cell_slide, spot_slide, spot_mask):
        n_spot, n_col = mesh.shape["spot"], mesh.shape["col"]
        plan = Plan(n_spot, n_col, logits.shape[0], logits.shape[1] // (n_spot * n_col), cell_expr.shape[1])
        return jax.shard_map(
            functools.partial(on_device, plan), mesh=mesh, in_specs=in_specs, out_specs=out_specs, check_vma=False
        )(logits, cell_expr, spot_expr, cell_slide, spot_slide, spot_mask)

    return whole
```

```python
import functools

import jax
import jax.numpy as jnp
from jax import lax
from jax.experimental import pallas as pl
from jax.experimental.pallas import tpu as pltpu
from jax.sharding import PartitionSpec as P

SLIDES = 11
ROWS = 16
PACKED = 24
LOSS_ROW = 22
PREDICT_TILE = 512
SCALE = 0.001
EPS = 1e-06
AXES = ("spot", "col")
F32 = jnp.float32
BF16 = jnp.bfloat16
LANES = 128


def split(x):
    hi = x.astype(BF16)
    return hi, (x - hi.astype(F32)).astype(BF16)


def params(plan, small=16):
    return pltpu.CompilerParams(vmem_limit_bytes=(small if plan.cells <= 2048 else 60) << 20)


def kept(plan, shape, dtype):
    return pltpu.VMEM(shape, dtype) if plan.cells <= 2048 else jax.ShapeDtypeStruct(shape, dtype)


def pin(plan, *values):
    if plan.cells > 2048:
        return values
    return tuple(pltpu.with_memory_space_constraint(v, pltpu.VMEM) for v in values)


def cost(flops, bytes_accessed):
    return pl.CostEstimate(flops=int(flops * SCALE), bytes_accessed=int(bytes_accessed * SCALE), transcendentals=0)


class Plan:
    def __init__(self, n_spot, n_col, cells, spots, genes):
        self.n_col = n_col
        self.plane = n_spot // 2
        self.bits = self.plane.bit_length() - 1
        self.rows = cells // (n_spot * n_col)
        self.cells = cells
        self.half = spots
        self.pair = 2 * spots
        self.genes = genes // 2
        self.unit = 2 * self.rows
        self.chunk = self.plane * self.unit
        self.n_spot = n_spot
        self.total = n_spot * n_col
        self.tile = 256 if cells <= 2048 else 128

    def order(self, core):
        return list(range(self.bits)) if core == 0 else list(range(self.bits))[::-1]

    def reverse(self, m):
        return sum(((m >> b) & 1) << (self.bits - 1 - b) for b in range(self.bits))

    def device(self, plane, core, z):
        return (plane * 2 + core) * self.n_col + z

    def all_places(self):
        for plane in range(self.plane):
            for core in range(2):
                for z in range(self.n_col):
                    yield plane, core, z

    def swap_core(self):
        return [(self.device(q, c, z), self.device(q, 1 - c, z)) for q, c, z in self.all_places()]

    def ring(self):
        return [(self.device(q, c, z), self.device(q, c, (z + 1) % self.n_col)) for q, c, z in self.all_places()]

    def hop(self, step):
        return [
            (self.device(q, c, z), self.device(q ^ (1 << self.order(c)[step]), c, z))
            for q, c, z in self.all_places()
        ]

    def block_start(self, place_ref, k, m, c):
        plane, core, z = place_ref[0], place_ref[1], place_ref[2]
        shift = [0, 0]
        for which in range(2):
            for step, bit in enumerate(self.order(which)):
                shift[which] |= ((m >> step) & 1) << bit
        xor = jnp.where(core == 0, shift[0], shift[1])
        q = jnp.bitwise_xor(plane, xor)
        ring = lax.rem(z - k + self.n_col, self.n_col)
        return ((q * 2 + c) * self.n_col + ring) * self.rows


def blocks(plan):
    for k in range(plan.n_col):
        for m in range(plan.plane):
            for c in range(2):
                yield k, m, c


def mapping_kernel(plan, again, place, logits_ref, cell_ref, meta_ref, *refs):
    hi_ref, lo_ref, hit_ref, lot_ref, row_ref, w_ref = refs[4:] if again else refs
    meta = jnp.transpose(meta_ref[...])
    slide = meta[0:1, :]
    cell = jnp.concatenate([cell_ref[...]] * (plan.tile // LANES), axis=1)
    same = cell == slide
    x = logits_ref[...]
    masked = jnp.where(same, x, -jnp.inf)
    col_max = jnp.max(masked, axis=0, keepdims=True)
    w = jnp.exp(masked - col_max)
    total = jnp.sum(w, axis=0, keepdims=True)
    w_ref[...] = w * (1.0 / total)
    if again:
        row_ref[...] = jnp.zeros_like(row_ref)
    else:
        counts = jnp.sum(jnp.where(same, 1.0, 0.0), axis=0, keepdims=True)
        mean = jnp.sum(jnp.where(same, x, 0.0), axis=0, keepdims=True) / counts
        kl = (col_max + jnp.log(total) - mean - jnp.log(counts)) * meta[1:2, :]
        row = lax.broadcasted_iota(jnp.int32, (8, plan.tile), 0)
        row_ref[...] = jnp.where(row == 0, kl, counts)
    gather = max(LANES // plan.rows, 1)
    held = []
    for i, (k, m, c) in enumerate(blocks(plan)):
        start = pl.multiple_of(plan.block_start(place, k, m, c), plan.rows)
        block = w_ref[pl.ds(start, plan.rows), :]
        hi, lo = split(block)
        hi_ref[i * plan.rows : (i + 1) * plan.rows, :] = hi
        lo_ref[i * plan.rows : (i + 1) * plan.rows, :] = lo
        held.append(block)
        if len(held) == gather:
            wide = jnp.transpose(jnp.concatenate(held, axis=0))
            hi, lo = split(wide)
            end = (i + 1) * plan.rows
            hit_ref[:, end - LANES : end] = hi
            lot_ref[:, end - LANES : end] = lo
            held = []


def make_mapping(plan, place, logits, cell, meta, earlier=None):
    t, tiles = plan.tile, plan.half // plan.tile
    again = earlier is not None
    at = tiles if again else 0
    wide = kept(plan, (plan.cells, plan.pair), BF16)
    tall = kept(plan, (plan.pair, plan.cells), BF16)
    operands = [place, logits, cell, meta]
    in_specs = [
        pl.BlockSpec((plan.cells, t), lambda j, *_: (0, j)),
        pl.BlockSpec((plan.cells, LANES), lambda j, *_: (0, 0)),
        pl.BlockSpec((t, LANES), lambda j, *_: (j, 0)),
    ]
    if again:
        operands += list(pin(plan, *earlier[:4]))
        in_specs += [pl.BlockSpec(memory_space=pl.ANY)] * 4
    return pl.pallas_call(
        functools.partial(mapping_kernel, plan, again),
        out_shape=(wide, wide, tall, tall, jax.ShapeDtypeStruct((8, plan.half), F32)),
        grid_spec=pltpu.PrefetchScalarGridSpec(
            num_scalar_prefetch=1,
            grid=(tiles,),
            in_specs=in_specs,
            out_specs=[
                pl.BlockSpec((plan.cells, t), lambda j, *_: (0, j + at)),
                pl.BlockSpec((plan.cells, t), lambda j, *_: (0, j + at)),
                pl.BlockSpec((t, plan.cells), lambda j, *_: (j + at, 0)),
                pl.BlockSpec((t, plan.cells), lambda j, *_: (j + at, 0)),
                pl.BlockSpec((8, t), lambda j, *_: (0, j)),
            ],
            scratch_shapes=[pltpu.VMEM((plan.cells, t), F32)],
        ),
        input_output_aliases={4 + i: i for i in range(4)} if again else {},
        compiler_params=params(plan),
        cost_estimate=cost(plan.cells * plan.half * 20, plan.cells * plan.half * 12),
        name="mapping",
    )(*operands)


def onehot_rows(plan, meta):
    turned = jnp.transpose(meta)
    slide = lax.broadcasted_iota(jnp.int32, (ROWS, meta.shape[0]), 0).astype(F32)
    return jnp.where(turned[0:1, :] == slide, turned[1:2, :], 0.0).astype(BF16)


def slide_sum(onehot, value):
    hi, lo = split(value)
    return jnp.dot(
        jnp.concatenate([onehot, onehot], axis=1),
        jnp.concatenate([hi, lo], axis=0),
        preferred_element_type=F32,
    )


def row_sum(value):
    return jnp.sum(value, axis=1, keepdims=True)


def spots_kernel(plan, place, own_ref, sib_ref, meta_own, meta_sib, spot_ref, stat_ref, ng_ref):
    tiles = plan.half // 256
    j = pl.program_id(0)

    @pl.when(j == 0)
    def _():
        ng_ref[...] = jnp.zeros_like(ng_ref)

    def run(value_ref, meta_ref):
        value = value_ref[...]
        square = value * value
        spot_ref[...] = value
        stat_ref[...] = jnp.broadcast_to(row_sum(square), stat_ref.shape)
        ng_ref[...] += slide_sum(onehot_rows(plan, meta_ref[...]), square)

    @pl.when(j < tiles)
    def _():
        run(own_ref, meta_own)

    @pl.when(j >= tiles)
    def _():
        run(sib_ref, meta_sib)


def make_spots(plan, place, own, sib, meta_own, meta_sib):
    t, tiles, g = 256, plan.half // 256, plan.genes
    return pl.pallas_call(
        functools.partial(spots_kernel, plan),
        out_shape=(
            kept(plan, (plan.pair, g), F32),
            kept(plan, (plan.pair, LANES), F32),
            jax.ShapeDtypeStruct((ROWS, g), F32),
        ),
        grid_spec=pltpu.PrefetchScalarGridSpec(
            num_scalar_prefetch=1,
            grid=(2 * tiles,),
            in_specs=[
                pl.BlockSpec((t, g), lambda j, place: (jnp.minimum(j, tiles - 1), place[1])),
                pl.BlockSpec((t, g), lambda j, place: (jnp.maximum(j - tiles, 0), place[1])),
                pl.BlockSpec((t, LANES), lambda j, place: (jnp.minimum(j, tiles - 1), 0)),
                pl.BlockSpec((t, LANES), lambda j, place: (jnp.maximum(j - tiles, 0), 0)),
            ],
            out_specs=[
                pl.BlockSpec((t, g), lambda j, place: (j, 0)),
                pl.BlockSpec((t, LANES), lambda j, place: (j, 0)),
                pl.BlockSpec((ROWS, g), lambda j, place: (0, 0)),
            ],
        ),
        compiler_params=params(plan),
        cost_estimate=cost(plan.pair * g * 64, plan.pair * g * 8),
        name="spots",
    )(place, own, sib, meta_own, meta_sib)


def predict_kernel(plan, n_parts, first, last, *refs):
    refs = list(refs)
    parts = [refs.pop(0) for _ in range(n_parts)]
    hit_ref, lot_ref = refs.pop(0), refs.pop(0)
    acc_in = None
    if not first:
        acc_in = refs.pop(0)
        refs.pop(0), refs.pop(0)
    if last:
        spot_ref, gg_ref, meta_ref = refs.pop(0), refs.pop(0), refs.pop(0)
    acc_ref, chi_ref, clo_ref = refs.pop(0), refs.pop(0), refs.pop(0)
    if last:
        stat_ref, sums_ref = refs.pop(0), refs.pop(0)
    stack_ref = refs.pop(0)
    j = pl.program_id(0)
    size = plan.chunk

    @pl.when(j == 0)
    def _():
        at = 0
        for part in parts:
            n = part.shape[0]
            hi, lo = split(part[...])
            stack_ref[at : at + n, :] = hi
            stack_ref[size + at : size + at + n, :] = lo
            stack_ref[2 * size + at : 2 * size + at + n, :] = hi
            chi_ref[at : at + n, :] = hi
            clo_ref[at : at + n, :] = lo
            at += n
        if last:
            sums_ref[...] = jnp.zeros_like(sums_ref)

    left = jnp.concatenate([hit_ref[...], hit_ref[...], lot_ref[...]], axis=1)
    value = jnp.dot(left, stack_ref[...], preferred_element_type=F32)
    if not first:
        value = value + acc_in[...]
    acc_ref[...] = value
    if last:
        spot = spot_ref[...]
        square, cross = value * value, value * spot
        lane = lax.broadcasted_iota(jnp.int32, stat_ref.shape, 1)
        stat_ref[...] = jnp.where(lane == 0, row_sum(square), jnp.where(lane == 1, row_sum(cross), gg_ref[...]))
        turned = jnp.transpose(meta_ref[...])
        row = lax.broadcasted_iota(jnp.int32, (PACKED, value.shape[0]), 0).astype(F32)
        pick = lambda first: jnp.where(turned[0:1, :] + first == row, turned[1:2, :], 0.0).astype(BF16)
        left = jnp.concatenate([pick(0), pick(0), pick(SLIDES), pick(SLIDES)], axis=1)
        right = jnp.concatenate([*split(square), *split(cross)], axis=0)
        sums_ref[...] += jnp.dot(left, right, preferred_element_type=F32)


def make_predict(plan, k, parts, hit, lot, carry, last=None):
    t, g, size = PREDICT_TILE if plan.cells <= 2048 else 256, plan.genes, plan.chunk
    const = lambda j: (0, 0)
    in_specs = [pl.BlockSpec(p.shape, const) for p in parts]
    in_specs += [pl.BlockSpec((t, size), lambda j: (j, k))] * 2
    operands = [*parts, *pin(plan, hit, lot)]
    aliases = {}
    if carry is not None:
        at = len(operands)
        operands += list(pin(plan, *carry))
        in_specs += [pl.BlockSpec((t, g), lambda j: (j, 0)), pl.BlockSpec(memory_space=pl.ANY), pl.BlockSpec(memory_space=pl.ANY)]
        aliases = {at: 0, at + 1: 1, at + 2: 2}
    out_shape = [
        kept(plan, (plan.pair, g), F32),
        kept(plan, (plan.cells, g), BF16),
        kept(plan, (plan.cells, g), BF16),
    ]
    out_specs = [pl.BlockSpec((t, g), lambda j: (j, 0))] + [pl.BlockSpec((size, g), lambda j: (k, 0))] * 2
    if last is not None:
        operands += list(pin(plan, *last[:2])) + list(last[2:])
        in_specs += [pl.BlockSpec((t, g), lambda j: (j, 0))] + [pl.BlockSpec((t, LANES), lambda j: (j, 0))] * 2
        out_shape += [jax.ShapeDtypeStruct((plan.pair, LANES), F32), jax.ShapeDtypeStruct((PACKED, g), F32)]
        out_specs += [pl.BlockSpec((t, LANES), lambda j: (j, 0)), pl.BlockSpec((PACKED, g), const)]
    return pl.pallas_call(
        functools.partial(predict_kernel, plan, len(parts), carry is None, last is not None),
        out_shape=tuple(out_shape),
        grid=(plan.pair // t,),
        in_specs=in_specs,
        out_specs=out_specs,
        scratch_shapes=[pltpu.VMEM((3 * size, g), BF16)],
        input_output_aliases=aliases,
        compiler_params=params(plan),
        cost_estimate=cost(6 * plan.pair * g * size, plan.pair * g * 8),
        name="predict",
    )(*operands)


def spot_loss_kernel(plan, mine_ref, other_ref, meta_ref, row_ref, out_ref):
    stat = mine_ref[0 : plan.half, :] + other_ref[plan.half :, :]
    cosine = stat[:, 1:2] * (lax.rsqrt(stat[:, 0:1] + EPS) * lax.rsqrt(stat[:, 2:3] + EPS))
    total = jnp.sum(row_ref[0:1, :], keepdims=True) - jnp.sum(cosine * meta_ref[...][0 : plan.half, 1:2], keepdims=True)
    row = lax.broadcasted_iota(jnp.int32, out_ref.shape, 0)
    out_ref[...] = jnp.where(row == LOSS_ROW % 8, total / (plan.half * plan.total), 0.0)


def make_spot_loss(plan, mine, other, meta, row):
    return pl.pallas_call(
        functools.partial(spot_loss_kernel, plan),
        out_shape=jax.ShapeDtypeStruct((8, plan.genes), F32),
        in_specs=[pl.BlockSpec(memory_space=pltpu.VMEM)] * 4,
        out_specs=pl.BlockSpec(memory_space=pltpu.VMEM),
        compiler_params=params(plan),
        cost_estimate=cost(plan.half * 8, plan.half * 1024),
        name="spot_loss",
    )(*pin(plan, mine), other, meta, row)


def gradient_kernel(plan, coef_gene, coef_spot, pred_ref, spot_ref, mine_ref, other_ref, meta_ref, sums_ref, ng_ref,
                    mhi_ref, mlo_ref, ghi_ref, glo_ref, keep_ref, send_ref, loss_ref, a_ref, b_ref, acc_ref):
    j = pl.program_id(0)

    @pl.when(j == 0)
    def _():
        pad = jnp.zeros((ROWS - SLIDES, sums_ref.shape[1]), F32)
        parts = [sums_ref[i * SLIDES : (i + 1) * SLIDES, :] for i in range(2)]
        np_sum, dots = [jnp.concatenate([part, pad], axis=0) for part in parts]
        ng_sum = ng_ref[...]
        scale = lax.rsqrt(np_sum + EPS) * lax.rsqrt(ng_sum + EPS)
        cosine = dots * scale
        hi, lo = split(-coef_gene * scale)
        a_ref[0:ROWS, :] = hi
        a_ref[ROWS : 2 * ROWS, :] = lo
        hi, lo = split(coef_gene * (cosine / (np_sum + EPS)))
        b_ref[0:ROWS, :] = hi
        b_ref[ROWS : 2 * ROWS, :] = lo
        acc_ref[...] = jnp.zeros_like(acc_ref)
        row = lax.broadcasted_iota(jnp.int32, cosine.shape, 0)
        gene = jnp.sum(jnp.where(row < SLIDES, cosine, 0.0), keepdims=True) / (SLIDES * 2 * plan.genes)
        loss_ref[...] = jnp.broadcast_to(-gene, loss_ref.shape)

    stat = mine_ref[...] + other_ref[...]
    spot_sq, cross, true_sq = stat[:, 0:1], stat[:, 1:2], stat[:, 2:3]
    slide, mask = meta_ref[...][:, 0:1], meta_ref[...][:, 1:2]
    scale = lax.rsqrt(spot_sq + EPS) * lax.rsqrt(true_sq + EPS)
    cosine = cross * scale

    weight = coef_spot * mask
    lane = lax.broadcasted_iota(jnp.int32, (stat.shape[0], ROWS), 1).astype(F32)
    onehot = jnp.where(slide == lane, mask, 0.0).astype(BF16)
    onehot = jnp.concatenate([onehot, onehot], axis=1)
    gene_a = jnp.dot(onehot, a_ref[...], preferred_element_type=F32)
    gene_b = jnp.dot(onehot, b_ref[...], preferred_element_type=F32)
    grad = spot_ref[...] * (gene_a - weight * scale) + pred_ref[...] * (gene_b + weight * (cosine / (spot_sq + EPS)))
    hi, lo = split(grad)
    ghi_ref[...] = hi
    glo_ref[...] = lo
    left = jnp.concatenate([mhi_ref[...], mhi_ref[...], mlo_ref[...]], axis=1)
    right = jnp.concatenate([hi, lo, hi], axis=0)
    acc_ref[...] += jnp.dot(left, right, preferred_element_type=F32)

    @pl.when(j == pl.num_programs(0) - 1)
    def _():
        n = keep_ref.shape[0]
        keep_ref[...] = acc_ref[0:n, :]
        send_ref[...] = acc_ref[n:, :]


def make_gradient(plan, k, coef_gene, coef_spot, pred, spot, mine, other, meta, sums, ng_sum, mhi, mlo):
    t, g, size = 256, plan.genes, plan.chunk
    tiles = plan.pair // t
    tile = lambda j: (j, 0)
    const = lambda j: (0, 0)
    halves = jax.ShapeDtypeStruct((size // 2, g), F32)
    return pl.pallas_call(
        functools.partial(gradient_kernel, plan, coef_gene, coef_spot),
        out_shape=(
            kept(plan, (plan.pair, g), BF16),
            kept(plan, (plan.pair, g), BF16),
            halves,
            halves,
            jax.ShapeDtypeStruct((8, LANES), F32),
        ),
        grid=(tiles,),
        in_specs=[
            pl.BlockSpec((t, g), tile),
            pl.BlockSpec((t, g), tile),
            pl.BlockSpec((t, LANES), tile),
            pl.BlockSpec((t, LANES), lambda j: ((j + tiles // 2) % tiles, 0)),
            pl.BlockSpec((t, LANES), tile),
            pl.BlockSpec((PACKED, g), const),
            pl.BlockSpec((ROWS, g), const),
            pl.BlockSpec((size, t), lambda j: (k, j)),
            pl.BlockSpec((size, t), lambda j: (k, j)),
        ],
        out_specs=[
            pl.BlockSpec((t, g), tile),
            pl.BlockSpec((t, g), tile),
            pl.BlockSpec((size // 2, g), const),
            pl.BlockSpec((size // 2, g), const),
            pl.BlockSpec((8, LANES), const),
        ],
        scratch_shapes=[pltpu.VMEM((2 * ROWS, g), BF16), pltpu.VMEM((2 * ROWS, g), BF16), pltpu.VMEM((size, g), F32)],
        compiler_params=params(plan),
        cost_estimate=cost(6 * plan.pair * g * size, plan.pair * g * 12),
        name="gradient",
    )(*pin(plan, pred, spot), mine, other, meta, sums, ng_sum, *pin(plan, mhi, mlo))


def cells_kernel(plan, ks, whole, mhi_ref, mlo_ref, ghi_ref, glo_ref, *outs):
    def rows(ref):
        if not whole:
            return ref[...]
        return jnp.concatenate([ref[k * plan.chunk : (k + 1) * plan.chunk, :] for k in ks], axis=0)

    hi, lo = rows(mhi_ref), rows(mlo_ref)
    left = jnp.concatenate([hi, hi, lo], axis=1)
    right = jnp.concatenate([ghi_ref[...], glo_ref[...], ghi_ref[...]], axis=0)
    value = jnp.dot(left, right, preferred_element_type=F32)
    at = 0
    for out in outs:
        out[...] = value[at : at + out.shape[0], :]
        at += out.shape[0]


def make_cells(plan, ks, sizes, mhi, mlo, ghi, glo):
    t, g, size = 256, plan.genes, plan.chunk
    whole = len(ks) > 1
    rows = (plan.cells, plan.pair) if whole else (size, plan.pair)
    at = 0 if whole else ks[0]
    return pl.pallas_call(
        functools.partial(cells_kernel, plan, ks, whole),
        out_shape=tuple(jax.ShapeDtypeStruct((n, g), F32) for n in sizes),
        grid=(g // t,),
        in_specs=[pl.BlockSpec(rows, lambda i: (at, 0))] * 2 + [pl.BlockSpec((plan.pair, t), lambda i: (0, i))] * 2,
        out_specs=[pl.BlockSpec((n, t), lambda i: (0, i)) for n in sizes],
        compiler_params=params(plan),
        cost_estimate=cost(6 * plan.pair * g * size * len(ks), plan.pair * g * 4),
        name="cells",
    )(*pin(plan, mhi, mlo, ghi, glo))


def turned_dot(chi, clo, ghi, glo):
    left = jnp.concatenate([chi, chi, clo], axis=1)
    right = jnp.concatenate([ghi, glo, ghi], axis=1)
    return lax.dot_general(left, right, (((1,), (1,)), ((), ())), preferred_element_type=F32)


def other_kernel(chi_ref, clo_ref, ghi_ref, glo_ref, out_ref):
    out_ref[...] = turned_dot(chi_ref[...], clo_ref[...], ghi_ref[...], glo_ref[...])


def cell_tile(plan):
    return min(plan.cells, 1024)


def make_other(plan, chi, clo, ghi, glo):
    t, g, ct = plan.tile, plan.genes, cell_tile(plan)
    tiles = plan.half // t
    return pl.pallas_call(
        other_kernel,
        out_shape=jax.ShapeDtypeStruct((plan.cells, plan.half), F32),
        grid=(tiles, plan.cells // ct),
        in_specs=[pl.BlockSpec((ct, g), lambda j, i: (i, 0))] * 2 + [pl.BlockSpec((t, g), lambda j, i: (j + tiles, 0))] * 2,
        out_specs=pl.BlockSpec((ct, t), lambda j, i: (i, j)),
        compiler_params=params(plan),
        cost_estimate=cost(6 * plan.cells * g * plan.half, plan.cells * plan.half * 12),
        name="other",
    )(*pin(plan, chi, clo, ghi, glo))


def logits_kernel(plan, coef_spot, place, chi_ref, clo_ref, ghi_ref, glo_ref, got_ref, mhi_ref, mlo_ref, cell_ref, meta_ref, row_ref,
                  out_ref, acc_ref):
    ct = cell_tile(plan)
    i = pl.program_id(1)
    rows = pl.ds(pl.multiple_of(i * ct, ct), ct)
    acc_ref[rows, :] = turned_dot(chi_ref[...], clo_ref[...], ghi_ref[...], glo_ref[...])

    @pl.when(i == pl.num_programs(1) - 1)
    def _():
        for k in range(plan.n_col):
            for m in range(plan.plane):
                at, there = (k * plan.plane + m) * plan.unit, (k * plan.plane + plan.reverse(m)) * plan.unit
                acc_ref[at : at + plan.unit, :] += got_ref[there : there + plan.unit, :]
        value = acc_ref[...]
        weight = mhi_ref[...].astype(F32) + mlo_ref[...].astype(F32)
        inner = jnp.sum(weight * value, axis=0, keepdims=True)
        meta = jnp.transpose(meta_ref[...])
        slide, coef = meta[0:1, :], coef_spot * meta[1:2, :]
        share = coef / row_ref[...][1:2, :]
        acc_ref[...] = weight * (value - inner + coef)
        for n, (k, m, c) in enumerate(blocks(plan)):
            start = pl.multiple_of(plan.block_start(place, k, m, c), plan.rows)
            cell = jnp.concatenate([cell_ref[pl.ds(start, plan.rows), :]] * (plan.tile // LANES), axis=1)
            out_ref[pl.ds(start, plan.rows), :] = acc_ref[n * plan.rows : (n + 1) * plan.rows, :] - jnp.where(cell == slide, share, 0.0)


def make_logits(plan, coef_spot, place, chi, clo, ghi, glo, got, mhi, mlo, cell, meta, row):
    t, g, ct = plan.tile, plan.genes, cell_tile(plan)
    column = lambda j, i, *_: (0, j)
    return pl.pallas_call(
        functools.partial(logits_kernel, plan, coef_spot),
        out_shape=jax.ShapeDtypeStruct((plan.cells, plan.half), F32),
        grid_spec=pltpu.PrefetchScalarGridSpec(
            num_scalar_prefetch=1,
            grid=(plan.half // t, plan.cells // ct),
            in_specs=[pl.BlockSpec((ct, g), lambda j, i, *_: (i, 0))] * 2
            + [pl.BlockSpec((t, g), lambda j, i, *_: (j, 0))] * 2
            + [pl.BlockSpec((plan.cells, t), column)] * 3
            + [
                pl.BlockSpec((plan.cells, LANES), lambda j, i, *_: (0, 0)),
                pl.BlockSpec((t, LANES), lambda j, i, *_: (j, 0)),
                pl.BlockSpec((8, t), column),
            ],
            out_specs=pl.BlockSpec((plan.cells, t), column),
            scratch_shapes=[pltpu.VMEM((plan.cells, t), F32)],
        ),
        compiler_params=params(plan, 24),
        cost_estimate=cost(6 * plan.cells * g * plan.half, plan.cells * plan.half * 20),
        name="logits",
    )(place, *pin(plan, chi, clo, ghi, glo), got, *pin(plan, mhi, mlo), cell, meta, row)


def on_device(plan, logits, cell_expr, spot_expr, cell_slide, spot_slide, spot_mask):
    g, rows = plan.genes, plan.rows
    spots_all = plan.half * plan.total
    factor = spots_all * plan.cells / SLIDES
    coef_spot = factor / spots_all
    coef_gene = factor / (SLIDES * 2 * g)
    spot_index, z = lax.axis_index("spot"), lax.axis_index("col")
    core, plane = spot_index % 2, spot_index // 2
    place = jnp.stack([plane, core, z]).astype(jnp.int32)
    send = lambda value, perm: lax.ppermute(value, AXES, perm)
    swap = plan.swap_core()
    hops = [plan.hop(step) for step in range(plan.bits)]

    tie = lax.optimization_barrier
    tie = lax.optimization_barrier

    def meet(flying, work):
        names, jobs = list(flying), list(work)
        came, made = tie(([flying[name] for name in names], [work[job] for job in jobs]))
        return dict(zip(names, came)), dict(zip(jobs, made))

    is_first = core == 0
    place, is_first = tie((place, is_first))
    lane = lax.broadcasted_iota(jnp.int32, (plan.half, LANES), 1)
    describe = lambda slide, mask: jnp.where(lane == 0, slide[:, None], mask[:, None]).astype(F32)
    meta_own = describe(spot_slide, spot_mask)
    cell = jnp.broadcast_to(cell_slide[:, None].astype(F32), (plan.cells, LANES))
    got, slide_sib, mask_sib = send(cell_expr, swap), send(spot_slide, swap), send(spot_mask, swap)
    got, slide_sib, mask_sib, meta_own, logits, spot_expr = tie((got, slide_sib, mask_sib, meta_own, logits, spot_expr))
    meta_sib = describe(slide_sib, mask_sib)
    first, second = jnp.concatenate([cell_expr[:, :g], got[:, :g]]), jnp.concatenate([got[:, g:], cell_expr[:, g:]])
    unit = jnp.where(is_first, first, second)
    logits_sib, spot_sib = send(logits, swap), send(spot_expr, swap)

    plane_hops = [("plane", 1 << bit) for bit in range(plan.bits)]
    ring_hops = [("ring", 1 << bit) for bit in range(plan.n_col.bit_length() - 1)]
    sum_orders = (plane_hops + ring_hops, ring_hops + plane_hops)

    def sum_hop(index):
        perm = []
        for q, c, i in plan.all_places():
            kind, bit = sum_orders[c][index]
            there = plan.device(q ^ bit, c, i) if kind == "plane" else plan.device(q, c, i ^ bit)
            perm.append((plan.device(q, c, i), there))
        return perm

    sum_hops = [sum_hop(index) for index in range(len(plane_hops) + len(ring_hops))]

    ring_sums = [
        [(plan.device(q, c, i), plan.device(q, c, i ^ bit)) for q, c, i in plan.all_places()] for _, bit in ring_hops
    ]
    plane_sums = [plan.hop(step) for step in range(plan.bits)]

    def sum_round(index):
        perms = []
        for other in range(1, plan.plane):
            perm = []
            for q, c, i in plan.all_places():
                there = plan.device(q ^ other, c, i) if c == index else plan.device(q, c, i ^ other)
                perm.append((plan.device(q, c, i), there))
            perms.append(perm)
        return perms

    n_col, bits = plan.n_col, plan.bits
    ring = plan.ring()
    units = {0: unit}
    parts = {}
    carry = mapping = spots = None
    row = None
    ng_left = [ring_hop for ring_hop in ring_sums] + [plane_hop for plane_hop in plane_sums]
    windows = n_col + bits - 1
    for w in range(windows):
        flying = {}
        if w + 1 < n_col:
            flying["unit"] = send(units[w], ring)
        for k in range(max(0, w - bits + 1), min(w + 1, n_col)):
            held = parts.setdefault(k, {0: units[k]})
            step = w - k
            fresh = [m for m in held if m.bit_length() == step] if step else [0]
            for m in fresh:
                for later in range(step, bits):
                    flying[k, m | (1 << later)] = send(held[m], hops[later])
        work = {}
        if w == 0:
            own = make_mapping(plan, place, logits, cell, meta_own)
            work["row"] = own[4]
            work["mapping"] = own
            flying["logits"], flying["spot"] = logits_sib, spot_sib
        elif w == 1:
            work["mapping"] = make_mapping(plan, place, logits_sib, cell, meta_sib, mapping)
        if w == 2:
            work["spots"] = make_spots(plan, place, spot_expr, spot_sib, meta_own, meta_sib)
        if w >= bits:
            k = w - bits
            pieces = [parts[k][m] for m in range(plan.plane)]
            work["carry"] = make_predict(plan, k, pieces, mapping[2], mapping[3], carry)
            parts[k] = None
        if spots is not None and ng_left:
            flying["ng"] = send(spots[2], ng_left.pop(0))
        flying, work = meet(flying, work)
        if "ng" in flying:
            spots = (*spots[:2], spots[2] + flying["ng"])
        for key, value in flying.items():
            if key == "unit":
                units[w + 1] = value
            elif isinstance(key, tuple):
                parts[key[0]][key[1]] = value
        if w == 0:
            logits_sib, spot_sib = flying["logits"], flying["spot"]
        mapping, spots, carry = work.get("mapping", mapping), work.get("spots", spots), work.get("carry", carry)
        row = work.get("row", row)
    mhi, mlo, hit, lot, _ = mapping
    spot, true_sq, ng_sum = spots
    meta = jnp.concatenate([meta_own, meta_sib])
    k = n_col - 1
    pieces = [parts[k][m] for m in range(plan.plane)]
    pred, chi, clo, stat, sums = make_predict(plan, k, pieces, hit, lot, carry, (spot, true_sq, meta))

    stat_other = send(stat, swap)
    spot_loss = make_spot_loss(plan, stat, stat_other, meta, row)
    rounds = [sum_round(0), sum_round(1)] if plan.plane == n_col else [[perm] for perm in sum_hops]
    for index, perms in enumerate(rounds):
        came = [send(sums, perm) for perm in perms]
        if index == 0:
            came, spot_loss = tie((came, spot_loss))
            came.append(jnp.concatenate([jnp.zeros((PACKED - 8, g), F32), spot_loss]))
        if ng_left:
            ng_came = send(ng_sum, ng_left.pop(0))
            came, ng_came = tie((came, ng_came))
            ng_sum = ng_sum + ng_came
        sums = sum(came, sums)
    for perm in ng_left:
        ng_sum = ng_sum + send(ng_sum, perm)
    order = [k % n_col for k in range(1, n_col + 1)]
    last = n_col - 1
    ghi, glo, keep, away, loss = make_gradient(
        plan, order[0], coef_gene, coef_spot, pred, spot, stat, stat_other, meta, sums, ng_sum, mhi, mlo
    )
    half = plan.chunk // 2
    state = {0: (bits - 1, keep, away)}
    pending = {}
    travelling = None
    other = other_sib = grad_logits = None
    at = LOSS_ROW % 8
    part = sums[PACKED - 8 :, :LANES]
    w = 0
    while True:
        flying = {("chunk", i): send(value[2], hops[value[0]]) for i, value in state.items()}
        if travelling is not None:
            flying["ring"] = send(travelling, ring)
        work = {}
        if w == 0 and plan.cells <= 2048:
            made = make_cells(plan, order[1:], [half] * (2 * last), mhi, mlo, ghi, glo)
            for i in range(1, n_col):
                work["chunk", i] = (made[2 * i - 2], made[2 * i - 1])
        elif w < last and plan.cells > 2048:
            work["chunk", w + 1] = tuple(make_cells(plan, [order[w + 1]], [half, half], mhi, mlo, ghi, glo))
        if w == 1:
            work["other"] = make_other(plan, chi, clo, ghi, glo)
        elif w == 2:
            flying["other"] = send(other, swap)
        elif w == 3:
            work["logits"] = make_logits(plan, coef_spot, place, chi, clo, ghi, glo, other_sib, mhi, mlo, cell, meta, row)
        elif w == 4:
            for index, perm in enumerate(rounds[0]):
                flying[f"part{index}"] = send(part, perm)
        flying, work = meet(flying, work)
        other, other_sib = work.get("other", other), flying.get("other", other_sib)
        grad_logits = work.get("logits", grad_logits)
        if w == 4:
            part = sum([flying[f"part{index}"] for index in range(len(rounds[0]))], part)[at : at + 1, :] + loss[0:1, :]
        for key, value in work.items():
            if isinstance(key, tuple):
                pending[key[1]] = value
        ended = None
        for i in list(state):
            step, keep, _ = state[i]
            came = flying["chunk", i]
            if step > 0:
                n = keep.shape[0] // 2
                state[i] = (step - 1, keep[:n] + came[:n], keep[n:] + came[n:])
            else:
                del state[i]
                ended = keep + came
                if "ring" in flying:
                    ended = ended + flying["ring"]
                finished = i
        travelling = ended
        if w + 1 < n_col:
            state[w + 1] = (bits - 1, *pending.pop(w + 1))
        w += 1
        if ended is not None and finished == last:
            result = ended
            break
    got = send(result, swap)
    def own_rows(result, got):
        first = jnp.concatenate([result[:rows], got[:rows]], axis=1)
        second = jnp.concatenate([got[rows:], result[rows:]], axis=1)
        return jnp.where(is_first, first, second)

    grad_expr = own_rows(result, got)
    part = part + send(part, swap)
    return part[0, 0], grad_logits, grad_expr


def solution(mesh):
    in_specs = (
        P(None, AXES),
        P(AXES, None),
        P(AXES, None),
        P(),
        P(AXES),
        P(AXES),
    )
    out_specs = (P(), P(None, AXES), P(AXES, None))

    def whole(logits, cell_expr, spot_expr, cell_slide, spot_slide, spot_mask):
        n_spot, n_col = mesh.shape["spot"], mesh.shape["col"]
        plan = Plan(n_spot, n_col, logits.shape[0], logits.shape[1] // (n_spot * n_col), cell_expr.shape[1])
        return jax.shard_map(
            functools.partial(on_device, plan), mesh=mesh, in_specs=in_specs, out_specs=out_specs, check_vma=False
        )(logits, cell_expr, spot_expr, cell_slide, spot_slide, spot_mask)

    return whole
```

```python
import functools

import jax
import jax.numpy as jnp
from jax import lax
from jax.experimental import pallas as pl
from jax.experimental.pallas import tpu as pltpu
from jax.sharding import PartitionSpec as P

SLIDES = 11
ROWS = 16
PACKED = 24
LOSS_ROW = 22
PREDICT_TILE = 1024
GRADIENT_TILE = 512
SCALE = 0.001
EPS = 1e-06
AXES = ("spot", "col")
F32 = jnp.float32
BF16 = jnp.bfloat16
LANES = 128


def split(x):
    hi = x.astype(BF16)
    return hi, (x - hi.astype(F32)).astype(BF16)


def params(plan, small=16):
    return pltpu.CompilerParams(vmem_limit_bytes=(small if plan.cells <= 2048 else 60) << 20)


def kept(plan, shape, dtype):
    return pltpu.VMEM(shape, dtype) if plan.cells <= 2048 else jax.ShapeDtypeStruct(shape, dtype)


def pin(plan, *values):
    if plan.cells > 2048:
        return values
    return tuple(pltpu.with_memory_space_constraint(v, pltpu.VMEM) for v in values)


def cost(flops, bytes_accessed):
    return pl.CostEstimate(flops=int(flops * SCALE), bytes_accessed=int(bytes_accessed * SCALE), transcendentals=0)


class Plan:
    def __init__(self, n_spot, n_col, cells, spots, genes):
        self.n_col = n_col
        self.plane = n_spot // 2
        self.bits = self.plane.bit_length() - 1
        self.rows = cells // (n_spot * n_col)
        self.cells = cells
        self.half = spots
        self.pair = 2 * spots
        self.genes = genes // 2
        self.unit = 2 * self.rows
        self.chunk = self.plane * self.unit
        self.n_spot = n_spot
        self.total = n_spot * n_col
        self.tile = 256 if cells <= 2048 else 128

    def order(self, core):
        return list(range(self.bits)) if core == 0 else list(range(self.bits))[::-1]

    def reverse(self, m):
        return sum(((m >> b) & 1) << (self.bits - 1 - b) for b in range(self.bits))

    def device(self, plane, core, z):
        return (plane * 2 + core) * self.n_col + z

    def all_places(self):
        for plane in range(self.plane):
            for core in range(2):
                for z in range(self.n_col):
                    yield plane, core, z

    def swap_core(self):
        return [(self.device(q, c, z), self.device(q, 1 - c, z)) for q, c, z in self.all_places()]

    def ring(self):
        return [(self.device(q, c, z), self.device(q, c, (z + 1) % self.n_col)) for q, c, z in self.all_places()]

    def hop(self, step):
        return [
            (self.device(q, c, z), self.device(q ^ (1 << self.order(c)[step]), c, z))
            for q, c, z in self.all_places()
        ]

    def block_start(self, place_ref, k, m, c):
        plane, core, z = place_ref[0], place_ref[1], place_ref[2]
        shift = [0, 0]
        for which in range(2):
            for step, bit in enumerate(self.order(which)):
                shift[which] |= ((m >> step) & 1) << bit
        xor = jnp.where(core == 0, shift[0], shift[1])
        q = jnp.bitwise_xor(plane, xor)
        ring = lax.rem(z - k + self.n_col, self.n_col)
        return ((q * 2 + c) * self.n_col + ring) * self.rows


def blocks(plan):
    for k in range(plan.n_col):
        for m in range(plan.plane):
            for c in range(2):
                yield k, m, c


def mapping_kernel(plan, again, place, logits_ref, cell_ref, meta_ref, *refs):
    hi_ref, lo_ref, hit_ref, lot_ref, row_ref, w_ref = refs[4:] if again else refs
    meta = jnp.transpose(meta_ref[...])
    slide = meta[0:1, :]
    cell = jnp.concatenate([cell_ref[...]] * (plan.tile // LANES), axis=1)
    same = cell == slide
    x = logits_ref[...]
    masked = jnp.where(same, x, -jnp.inf)
    col_max = jnp.max(masked, axis=0, keepdims=True)
    w = jnp.exp(masked - col_max)
    total = jnp.sum(w, axis=0, keepdims=True)
    w_ref[...] = w * (1.0 / total)
    if again:
        row_ref[...] = jnp.zeros_like(row_ref)
    else:
        counts = jnp.sum(jnp.where(same, 1.0, 0.0), axis=0, keepdims=True)
        mean = jnp.sum(jnp.where(same, x, 0.0), axis=0, keepdims=True) / counts
        kl = (col_max + jnp.log(total) - mean - jnp.log(counts)) * meta[1:2, :]
        row = lax.broadcasted_iota(jnp.int32, (8, plan.tile), 0)
        row_ref[...] = jnp.where(row == 0, kl, counts)
    gather = max(LANES // plan.rows, 1)
    held = []
    for i, (k, m, c) in enumerate(blocks(plan)):
        start = pl.multiple_of(plan.block_start(place, k, m, c), plan.rows)
        block = w_ref[pl.ds(start, plan.rows), :]
        hi, lo = split(block)
        hi_ref[i * plan.rows : (i + 1) * plan.rows, :] = hi
        lo_ref[i * plan.rows : (i + 1) * plan.rows, :] = lo
        held.append(block)
        if len(held) == gather:
            wide = jnp.transpose(jnp.concatenate(held, axis=0))
            hi, lo = split(wide)
            end = (i + 1) * plan.rows
            hit_ref[:, end - LANES : end] = hi
            lot_ref[:, end - LANES : end] = lo
            held = []


def make_mapping(plan, place, logits, cell, meta, earlier=None):
    t, tiles = plan.tile, plan.half // plan.tile
    again = earlier is not None
    at = tiles if again else 0
    wide = kept(plan, (plan.cells, plan.pair), BF16)
    tall = kept(plan, (plan.pair, plan.cells), BF16)
    operands = [place, logits, cell, meta]
    in_specs = [
        pl.BlockSpec((plan.cells, t), lambda j, *_: (0, j)),
        pl.BlockSpec((plan.cells, LANES), lambda j, *_: (0, 0)),
        pl.BlockSpec((t, LANES), lambda j, *_: (j, 0)),
    ]
    if again:
        operands += list(pin(plan, *earlier[:4]))
        in_specs += [pl.BlockSpec(memory_space=pl.ANY)] * 4
    return pl.pallas_call(
        functools.partial(mapping_kernel, plan, again),
        out_shape=(wide, wide, tall, tall, jax.ShapeDtypeStruct((8, plan.half), F32)),
        grid_spec=pltpu.PrefetchScalarGridSpec(
            num_scalar_prefetch=1,
            grid=(tiles,),
            in_specs=in_specs,
            out_specs=[
                pl.BlockSpec((plan.cells, t), lambda j, *_: (0, j + at)),
                pl.BlockSpec((plan.cells, t), lambda j, *_: (0, j + at)),
                pl.BlockSpec((t, plan.cells), lambda j, *_: (j + at, 0)),
                pl.BlockSpec((t, plan.cells), lambda j, *_: (j + at, 0)),
                pl.BlockSpec((8, t), lambda j, *_: (0, j)),
            ],
            scratch_shapes=[pltpu.VMEM((plan.cells, t), F32)],
        ),
        input_output_aliases={4 + i: i for i in range(4)} if again else {},
        compiler_params=params(plan),
        cost_estimate=cost(plan.cells * plan.half * 20, plan.cells * plan.half * 12),
        name="mapping",
    )(*operands)


def onehot_rows(plan, meta):
    turned = jnp.transpose(meta)
    slide = lax.broadcasted_iota(jnp.int32, (ROWS, meta.shape[0]), 0).astype(F32)
    return jnp.where(turned[0:1, :] == slide, turned[1:2, :], 0.0).astype(BF16)


def slide_sum(onehot, value):
    hi, lo = split(value)
    return jnp.dot(
        jnp.concatenate([onehot, onehot], axis=1),
        jnp.concatenate([hi, lo], axis=0),
        preferred_element_type=F32,
    )


def row_sum(value):
    return jnp.sum(value, axis=1, keepdims=True)


def spots_kernel(plan, place, own_ref, sib_ref, meta_own, meta_sib, spot_ref, stat_ref, ng_ref):
    tiles = plan.half // 256
    j = pl.program_id(0)

    @pl.when(j == 0)
    def _():
        ng_ref[...] = jnp.zeros_like(ng_ref)

    def run(value_ref, meta_ref):
        value = value_ref[...]
        square = value * value
        spot_ref[...] = value
        stat_ref[...] = jnp.broadcast_to(row_sum(square), stat_ref.shape)
        ng_ref[...] += slide_sum(onehot_rows(plan, meta_ref[...]), square)

    @pl.when(j < tiles)
    def _():
        run(own_ref, meta_own)

    @pl.when(j >= tiles)
    def _():
        run(sib_ref, meta_sib)


def make_spots(plan, place, own, sib, meta_own, meta_sib):
    t, tiles, g = 256, plan.half // 256, plan.genes
    return pl.pallas_call(
        functools.partial(spots_kernel, plan),
        out_shape=(
            kept(plan, (plan.pair, g), F32),
            kept(plan, (plan.pair, LANES), F32),
            jax.ShapeDtypeStruct((ROWS, g), F32),
        ),
        grid_spec=pltpu.PrefetchScalarGridSpec(
            num_scalar_prefetch=1,
            grid=(2 * tiles,),
            in_specs=[
                pl.BlockSpec((t, g), lambda j, place: (jnp.minimum(j, tiles - 1), place[1])),
                pl.BlockSpec((t, g), lambda j, place: (jnp.maximum(j - tiles, 0), place[1])),
                pl.BlockSpec((t, LANES), lambda j, place: (jnp.minimum(j, tiles - 1), 0)),
                pl.BlockSpec((t, LANES), lambda j, place: (jnp.maximum(j - tiles, 0), 0)),
            ],
            out_specs=[
                pl.BlockSpec((t, g), lambda j, place: (j, 0)),
                pl.BlockSpec((t, LANES), lambda j, place: (j, 0)),
                pl.BlockSpec((ROWS, g), lambda j, place: (0, 0)),
            ],
        ),
        compiler_params=params(plan),
        cost_estimate=cost(plan.pair * g * 64, plan.pair * g * 8),
        name="spots",
    )(place, own, sib, meta_own, meta_sib)


def predict_kernel(plan, n_parts, first, last, *refs):
    refs = list(refs)
    parts = [refs.pop(0) for _ in range(n_parts)]
    hit_ref, lot_ref = refs.pop(0), refs.pop(0)
    acc_in = None
    if not first:
        acc_in = refs.pop(0)
        refs.pop(0), refs.pop(0)
    if last:
        spot_ref, gg_ref, meta_ref = refs.pop(0), refs.pop(0), refs.pop(0)
    acc_ref, chi_ref, clo_ref = refs.pop(0), refs.pop(0), refs.pop(0)
    if last:
        stat_ref, sums_ref = refs.pop(0), refs.pop(0)
    stack_ref = refs.pop(0)
    j = pl.program_id(0)
    size = plan.chunk

    @pl.when(j == 0)
    def _():
        at = 0
        for part in parts:
            n = part.shape[0]
            hi, lo = split(part[...])
            stack_ref[at : at + n, :] = hi
            stack_ref[size + at : size + at + n, :] = lo
            stack_ref[2 * size + at : 2 * size + at + n, :] = hi
            chi_ref[at : at + n, :] = hi
            clo_ref[at : at + n, :] = lo
            at += n
        if last:
            sums_ref[...] = jnp.zeros_like(sums_ref)

    left = jnp.concatenate([hit_ref[...], hit_ref[...], lot_ref[...]], axis=1)
    value = jnp.dot(left, stack_ref[...], preferred_element_type=F32)
    if not first:
        value = value + acc_in[...]
    acc_ref[...] = value
    if last:
        spot = spot_ref[...]
        square, cross = value * value, value * spot
        lane = lax.broadcasted_iota(jnp.int32, stat_ref.shape, 1)
        stat_ref[...] = jnp.where(lane == 0, row_sum(square), jnp.where(lane == 1, row_sum(cross), gg_ref[...]))
        turned = jnp.transpose(meta_ref[...])
        row = lax.broadcasted_iota(jnp.int32, (PACKED, value.shape[0]), 0).astype(F32)
        pick = lambda first: jnp.where(turned[0:1, :] + first == row, turned[1:2, :], 0.0).astype(BF16)
        left = jnp.concatenate([pick(0), pick(0), pick(SLIDES), pick(SLIDES)], axis=1)
        right = jnp.concatenate([*split(square), *split(cross)], axis=0)
        sums_ref[...] += jnp.dot(left, right, preferred_element_type=F32)


def make_predict(plan, k, parts, hit, lot, carry, last=None):
    t, g, size = PREDICT_TILE if plan.cells <= 2048 else 256, plan.genes, plan.chunk
    const = lambda j: (0, 0)
    in_specs = [pl.BlockSpec(p.shape, const) for p in parts]
    in_specs += [pl.BlockSpec((t, size), lambda j: (j, k))] * 2
    operands = [*parts, *pin(plan, hit, lot)]
    aliases = {}
    if carry is not None:
        at = len(operands)
        operands += list(pin(plan, *carry))
        in_specs += [pl.BlockSpec((t, g), lambda j: (j, 0)), pl.BlockSpec(memory_space=pl.ANY), pl.BlockSpec(memory_space=pl.ANY)]
        aliases = {at: 0, at + 1: 1, at + 2: 2}
    out_shape = [
        kept(plan, (plan.pair, g), F32),
        kept(plan, (plan.cells, g), BF16),
        kept(plan, (plan.cells, g), BF16),
    ]
    out_specs = [pl.BlockSpec((t, g), lambda j: (j, 0))] + [pl.BlockSpec((size, g), lambda j: (k, 0))] * 2
    if last is not None:
        operands += list(pin(plan, *last[:2])) + list(last[2:])
        in_specs += [pl.BlockSpec((t, g), lambda j: (j, 0))] + [pl.BlockSpec((t, LANES), lambda j: (j, 0))] * 2
        out_shape += [jax.ShapeDtypeStruct((plan.pair, LANES), F32), jax.ShapeDtypeStruct((PACKED, g), F32)]
        out_specs += [pl.BlockSpec((t, LANES), lambda j: (j, 0)), pl.BlockSpec((PACKED, g), const)]
    return pl.pallas_call(
        functools.partial(predict_kernel, plan, len(parts), carry is None, last is not None),
        out_shape=tuple(out_shape),
        grid=(plan.pair // t,),
        in_specs=in_specs,
        out_specs=out_specs,
        scratch_shapes=[pltpu.VMEM((3 * size, g), BF16)],
        input_output_aliases=aliases,
        compiler_params=params(plan),
        cost_estimate=cost(6 * plan.pair * g * size, plan.pair * g * 8),
        name="predict",
    )(*operands)


def spot_loss_kernel(plan, mine_ref, other_ref, meta_ref, row_ref, out_ref):
    stat = mine_ref[0 : plan.half, :] + other_ref[plan.half :, :]
    cosine = stat[:, 1:2] * (lax.rsqrt(stat[:, 0:1] + EPS) * lax.rsqrt(stat[:, 2:3] + EPS))
    total = jnp.sum(row_ref[0:1, :], keepdims=True) - jnp.sum(cosine * meta_ref[...][0 : plan.half, 1:2], keepdims=True)
    row = lax.broadcasted_iota(jnp.int32, out_ref.shape, 0)
    out_ref[...] = jnp.where(row == LOSS_ROW % 8, total / (plan.half * plan.total), 0.0)


def make_spot_loss(plan, mine, other, meta, row):
    return pl.pallas_call(
        functools.partial(spot_loss_kernel, plan),
        out_shape=jax.ShapeDtypeStruct((8, plan.genes), F32),
        in_specs=[pl.BlockSpec(memory_space=pltpu.VMEM)] * 4,
        out_specs=pl.BlockSpec(memory_space=pltpu.VMEM),
        compiler_params=params(plan),
        cost_estimate=cost(plan.half * 8, plan.half * 1024),
        name="spot_loss",
    )(*pin(plan, mine), other, meta, row)


def gradient_kernel(plan, coef_gene, coef_spot, pred_ref, spot_ref, mine_ref, other_ref, meta_ref, sums_ref, ng_ref,
                    mhi_ref, mlo_ref, ghi_ref, glo_ref, keep_ref, send_ref, loss_ref, a_ref, b_ref, acc_ref):
    j = pl.program_id(0)

    @pl.when(j == 0)
    def _():
        pad = jnp.zeros((ROWS - SLIDES, sums_ref.shape[1]), F32)
        parts = [sums_ref[i * SLIDES : (i + 1) * SLIDES, :] for i in range(2)]
        np_sum, dots = [jnp.concatenate([part, pad], axis=0) for part in parts]
        ng_sum = ng_ref[...]
        scale = lax.rsqrt(np_sum + EPS) * lax.rsqrt(ng_sum + EPS)
        cosine = dots * scale
        hi, lo = split(-coef_gene * scale)
        a_ref[0:ROWS, :] = hi
        a_ref[ROWS : 2 * ROWS, :] = lo
        hi, lo = split(coef_gene * (cosine / (np_sum + EPS)))
        b_ref[0:ROWS, :] = hi
        b_ref[ROWS : 2 * ROWS, :] = lo
        acc_ref[...] = jnp.zeros_like(acc_ref)
        row = lax.broadcasted_iota(jnp.int32, cosine.shape, 0)
        gene = jnp.sum(jnp.where(row < SLIDES, cosine, 0.0), keepdims=True) / (SLIDES * 2 * plan.genes)
        loss_ref[...] = jnp.broadcast_to(-gene, loss_ref.shape)

    stat = mine_ref[...] + other_ref[...]
    spot_sq, cross, true_sq = stat[:, 0:1], stat[:, 1:2], stat[:, 2:3]
    slide, mask = meta_ref[...][:, 0:1], meta_ref[...][:, 1:2]
    scale = lax.rsqrt(spot_sq + EPS) * lax.rsqrt(true_sq + EPS)
    cosine = cross * scale

    weight = coef_spot * mask
    lane = lax.broadcasted_iota(jnp.int32, (stat.shape[0], ROWS), 1).astype(F32)
    onehot = jnp.where(slide == lane, mask, 0.0).astype(BF16)
    onehot = jnp.concatenate([onehot, onehot], axis=1)
    gene_a = jnp.dot(onehot, a_ref[...], preferred_element_type=F32)
    gene_b = jnp.dot(onehot, b_ref[...], preferred_element_type=F32)
    grad = spot_ref[...] * (gene_a - weight * scale) + pred_ref[...] * (gene_b + weight * (cosine / (spot_sq + EPS)))
    hi, lo = split(grad)
    ghi_ref[...] = hi
    glo_ref[...] = lo
    left = jnp.concatenate([mhi_ref[...], mhi_ref[...], mlo_ref[...]], axis=1)
    right = jnp.concatenate([hi, lo, hi], axis=0)
    acc_ref[...] += jnp.dot(left, right, preferred_element_type=F32)

    @pl.when(j == pl.num_programs(0) - 1)
    def _():
        n = keep_ref.shape[0]
        keep_ref[...] = acc_ref[0:n, :]
        send_ref[...] = acc_ref[n:, :]


def make_gradient(plan, k, coef_gene, coef_spot, pred, spot, mine, other, meta, sums, ng_sum, mhi, mlo):
    t, g, size = GRADIENT_TILE if plan.cells <= 2048 else 256, plan.genes, plan.chunk
    tiles = plan.pair // t
    tile = lambda j: (j, 0)
    const = lambda j: (0, 0)
    halves = jax.ShapeDtypeStruct((size // 2, g), F32)
    return pl.pallas_call(
        functools.partial(gradient_kernel, plan, coef_gene, coef_spot),
        out_shape=(
            kept(plan, (plan.pair, g), BF16),
            kept(plan, (plan.pair, g), BF16),
            halves,
            halves,
            jax.ShapeDtypeStruct((8, LANES), F32),
        ),
        grid=(tiles,),
        in_specs=[
            pl.BlockSpec((t, g), tile),
            pl.BlockSpec((t, g), tile),
            pl.BlockSpec((t, LANES), tile),
            pl.BlockSpec((t, LANES), lambda j: ((j + tiles // 2) % tiles, 0)),
            pl.BlockSpec((t, LANES), tile),
            pl.BlockSpec((PACKED, g), const),
            pl.BlockSpec((ROWS, g), const),
            pl.BlockSpec((size, t), lambda j: (k, j)),
            pl.BlockSpec((size, t), lambda j: (k, j)),
        ],
        out_specs=[
            pl.BlockSpec((t, g), tile),
            pl.BlockSpec((t, g), tile),
            pl.BlockSpec((size // 2, g), const),
            pl.BlockSpec((size // 2, g), const),
            pl.BlockSpec((8, LANES), const),
        ],
        scratch_shapes=[pltpu.VMEM((2 * ROWS, g), BF16), pltpu.VMEM((2 * ROWS, g), BF16), pltpu.VMEM((size, g), F32)],
        compiler_params=params(plan),
        cost_estimate=cost(6 * plan.pair * g * size, plan.pair * g * 12),
        name="gradient",
    )(*pin(plan, pred, spot), mine, other, meta, sums, ng_sum, *pin(plan, mhi, mlo))


def cells_kernel(plan, ks, whole, mhi_ref, mlo_ref, ghi_ref, glo_ref, *outs):
    def rows(ref):
        if not whole:
            return ref[...]
        return jnp.concatenate([ref[k * plan.chunk : (k + 1) * plan.chunk, :] for k in ks], axis=0)

    hi, lo = rows(mhi_ref), rows(mlo_ref)
    left = jnp.concatenate([hi, hi, lo], axis=1)
    right = jnp.concatenate([ghi_ref[...], glo_ref[...], ghi_ref[...]], axis=0)
    value = jnp.dot(left, right, preferred_element_type=F32)
    at = 0
    for out in outs:
        out[...] = value[at : at + out.shape[0], :]
        at += out.shape[0]


def make_cells(plan, ks, sizes, mhi, mlo, ghi, glo):
    t, g, size = 256, plan.genes, plan.chunk
    whole = len(ks) > 1
    rows = (plan.cells, plan.pair) if whole else (size, plan.pair)
    at = 0 if whole else ks[0]
    return pl.pallas_call(
        functools.partial(cells_kernel, plan, ks, whole),
        out_shape=tuple(jax.ShapeDtypeStruct((n, g), F32) for n in sizes),
        grid=(g // t,),
        in_specs=[pl.BlockSpec(rows, lambda i: (at, 0))] * 2 + [pl.BlockSpec((plan.pair, t), lambda i: (0, i))] * 2,
        out_specs=[pl.BlockSpec((n, t), lambda i: (0, i)) for n in sizes],
        compiler_params=params(plan),
        cost_estimate=cost(6 * plan.pair * g * size * len(ks), plan.pair * g * 4),
        name="cells",
    )(*pin(plan, mhi, mlo, ghi, glo))


def turned_dot(chi, clo, ghi, glo):
    left = jnp.concatenate([chi, chi, clo], axis=1)
    right = jnp.concatenate([ghi, glo, ghi], axis=1)
    return lax.dot_general(left, right, (((1,), (1,)), ((), ())), preferred_element_type=F32)


def other_kernel(chi_ref, clo_ref, ghi_ref, glo_ref, out_ref):
    out_ref[...] = turned_dot(chi_ref[...], clo_ref[...], ghi_ref[...], glo_ref[...])


def cell_tile(plan):
    return min(plan.cells, 1024)


def make_other(plan, chi, clo, ghi, glo):
    t, g, ct = plan.tile, plan.genes, cell_tile(plan)
    tiles = plan.half // t
    return pl.pallas_call(
        other_kernel,
        out_shape=jax.ShapeDtypeStruct((plan.cells, plan.half), F32),
        grid=(tiles, plan.cells // ct),
        in_specs=[pl.BlockSpec((ct, g), lambda j, i: (i, 0))] * 2 + [pl.BlockSpec((t, g), lambda j, i: (j + tiles, 0))] * 2,
        out_specs=pl.BlockSpec((ct, t), lambda j, i: (i, j)),
        compiler_params=params(plan),
        cost_estimate=cost(6 * plan.cells * g * plan.half, plan.cells * plan.half * 12),
        name="other",
    )(*pin(plan, chi, clo, ghi, glo))


def logits_kernel(plan, coef_spot, place, chi_ref, clo_ref, ghi_ref, glo_ref, got_ref, mhi_ref, mlo_ref, cell_ref, meta_ref, row_ref,
                  out_ref, acc_ref):
    ct = cell_tile(plan)
    i = pl.program_id(1)
    rows = pl.ds(pl.multiple_of(i * ct, ct), ct)
    acc_ref[rows, :] = turned_dot(chi_ref[...], clo_ref[...], ghi_ref[...], glo_ref[...])

    @pl.when(i == pl.num_programs(1) - 1)
    def _():
        for k in range(plan.n_col):
            for m in range(plan.plane):
                at, there = (k * plan.plane + m) * plan.unit, (k * plan.plane + plan.reverse(m)) * plan.unit
                acc_ref[at : at + plan.unit, :] += got_ref[there : there + plan.unit, :]
        value = acc_ref[...]
        weight = mhi_ref[...].astype(F32) + mlo_ref[...].astype(F32)
        inner = jnp.sum(weight * value, axis=0, keepdims=True)
        meta = jnp.transpose(meta_ref[...])
        slide, coef = meta[0:1, :], coef_spot * meta[1:2, :]
        share = coef / row_ref[...][1:2, :]
        acc_ref[...] = weight * (value - inner + coef)
        for n, (k, m, c) in enumerate(blocks(plan)):
            start = pl.multiple_of(plan.block_start(place, k, m, c), plan.rows)
            cell = jnp.concatenate([cell_ref[pl.ds(start, plan.rows), :]] * (plan.tile // LANES), axis=1)
            out_ref[pl.ds(start, plan.rows), :] = acc_ref[n * plan.rows : (n + 1) * plan.rows, :] - jnp.where(cell == slide, share, 0.0)


def make_logits(plan, coef_spot, place, chi, clo, ghi, glo, got, mhi, mlo, cell, meta, row):
    t, g, ct = plan.tile, plan.genes, cell_tile(plan)
    column = lambda j, i, *_: (0, j)
    return pl.pallas_call(
        functools.partial(logits_kernel, plan, coef_spot),
        out_shape=jax.ShapeDtypeStruct((plan.cells, plan.half), F32),
        grid_spec=pltpu.PrefetchScalarGridSpec(
            num_scalar_prefetch=1,
            grid=(plan.half // t, plan.cells // ct),
            in_specs=[pl.BlockSpec((ct, g), lambda j, i, *_: (i, 0))] * 2
            + [pl.BlockSpec((t, g), lambda j, i, *_: (j, 0))] * 2
            + [pl.BlockSpec((plan.cells, t), column)] * 3
            + [
                pl.BlockSpec((plan.cells, LANES), lambda j, i, *_: (0, 0)),
                pl.BlockSpec((t, LANES), lambda j, i, *_: (j, 0)),
                pl.BlockSpec((8, t), column),
            ],
            out_specs=pl.BlockSpec((plan.cells, t), column),
            scratch_shapes=[pltpu.VMEM((plan.cells, t), F32)],
        ),
        compiler_params=params(plan, 24),
        cost_estimate=cost(6 * plan.cells * g * plan.half, plan.cells * plan.half * 20),
        name="logits",
    )(place, *pin(plan, chi, clo, ghi, glo), got, *pin(plan, mhi, mlo), cell, meta, row)


def on_device(plan, logits, cell_expr, spot_expr, cell_slide, spot_slide, spot_mask):
    g, rows = plan.genes, plan.rows
    spots_all = plan.half * plan.total
    factor = spots_all * plan.cells / SLIDES
    coef_spot = factor / spots_all
    coef_gene = factor / (SLIDES * 2 * g)
    spot_index, z = lax.axis_index("spot"), lax.axis_index("col")
    core, plane = spot_index % 2, spot_index // 2
    place = jnp.stack([plane, core, z]).astype(jnp.int32)
    send = lambda value, perm: lax.ppermute(value, AXES, perm)
    swap = plan.swap_core()
    hops = [plan.hop(step) for step in range(plan.bits)]

    tie = lax.optimization_barrier
    tie = lax.optimization_barrier

    def meet(flying, work):
        names, jobs = list(flying), list(work)
        came, made = tie(([flying[name] for name in names], [work[job] for job in jobs]))
        return dict(zip(names, came)), dict(zip(jobs, made))

    is_first = core == 0
    place, is_first = tie((place, is_first))
    lane = lax.broadcasted_iota(jnp.int32, (plan.half, LANES), 1)
    describe = lambda slide, mask: jnp.where(lane == 0, slide[:, None], mask[:, None]).astype(F32)
    meta_own = describe(spot_slide, spot_mask)
    cell = jnp.broadcast_to(cell_slide[:, None].astype(F32), (plan.cells, LANES))
    got, slide_sib, mask_sib = send(cell_expr, swap), send(spot_slide, swap), send(spot_mask, swap)
    got, slide_sib, mask_sib, meta_own, logits, spot_expr = tie((got, slide_sib, mask_sib, meta_own, logits, spot_expr))
    meta_sib = describe(slide_sib, mask_sib)
    first, second = jnp.concatenate([cell_expr[:, :g], got[:, :g]]), jnp.concatenate([got[:, g:], cell_expr[:, g:]])
    unit = jnp.where(is_first, first, second)
    logits_sib, spot_sib = send(logits, swap), send(spot_expr, swap)

    plane_hops = [("plane", 1 << bit) for bit in range(plan.bits)]
    ring_hops = [("ring", 1 << bit) for bit in range(plan.n_col.bit_length() - 1)]
    sum_orders = (plane_hops + ring_hops, ring_hops + plane_hops)

    def sum_hop(index):
        perm = []
        for q, c, i in plan.all_places():
            kind, bit = sum_orders[c][index]
            there = plan.device(q ^ bit, c, i) if kind == "plane" else plan.device(q, c, i ^ bit)
            perm.append((plan.device(q, c, i), there))
        return perm

    sum_hops = [sum_hop(index) for index in range(len(plane_hops) + len(ring_hops))]

    ring_sums = [
        [(plan.device(q, c, i), plan.device(q, c, i ^ bit)) for q, c, i in plan.all_places()] for _, bit in ring_hops
    ]
    plane_sums = [plan.hop(step) for step in range(plan.bits)]

    def sum_round(index):
        perms = []
        for other in reversed(range(1, plan.plane)):
            perm = []
            for q, c, i in plan.all_places():
                there = plan.device(q ^ other, c, i) if c == index else plan.device(q, c, i ^ other)
                perm.append((plan.device(q, c, i), there))
            perms.append(perm)
        return perms

    n_col, bits = plan.n_col, plan.bits
    ring = plan.ring()
    units = {0: unit}
    parts = {}
    carry = mapping = spots = None
    row = None
    ng_left = [ring_hop for ring_hop in ring_sums] + [plane_hop for plane_hop in plane_sums]
    windows = n_col + bits - 1
    for w in range(windows):
        flying = {}
        for k in range(max(0, w - bits + 1), min(w + 1, n_col)):
            held = parts.setdefault(k, {0: units[k]})
            step = w - k
            fresh = [m for m in held if m.bit_length() == step] if step else [0]
            for m in fresh:
                for later in range(step, bits):
                    flying[k, m | (1 << later)] = send(held[m], hops[later])
        if w + 1 < n_col:
            flying["unit"] = send(units[w], ring)
        work = {}
        if w == 0:
            own = make_mapping(plan, place, logits, cell, meta_own)
            work["row"] = own[4]
            work["mapping"] = own
            flying["logits"], flying["spot"] = logits_sib, spot_sib
        elif w == 1:
            work["mapping"] = make_mapping(plan, place, logits_sib, cell, meta_sib, mapping)
        if w == 2:
            work["spots"] = make_spots(plan, place, spot_expr, spot_sib, meta_own, meta_sib)
        if w >= bits:
            k = w - bits
            pieces = [parts[k][m] for m in range(plan.plane)]
            work["carry"] = make_predict(plan, k, pieces, mapping[2], mapping[3], carry)
            parts[k] = None
        if spots is not None and ng_left:
            flying["ng"] = send(spots[2], ng_left.pop(0))
        flying, work = meet(flying, work)
        if "ng" in flying:
            spots = (*spots[:2], spots[2] + flying["ng"])
        for key, value in flying.items():
            if key == "unit":
                units[w + 1] = value
            elif isinstance(key, tuple):
                parts[key[0]][key[1]] = value
        if w == 0:
            logits_sib, spot_sib = flying["logits"], flying["spot"]
        mapping, spots, carry = work.get("mapping", mapping), work.get("spots", spots), work.get("carry", carry)
        row = work.get("row", row)
    mhi, mlo, hit, lot, _ = mapping
    spot, true_sq, ng_sum = spots
    meta = jnp.concatenate([meta_own, meta_sib])
    k = n_col - 1
    pieces = [parts[k][m] for m in range(plan.plane)]
    pred, chi, clo, stat, sums = make_predict(plan, k, pieces, hit, lot, carry, (spot, true_sq, meta))

    stat_other = send(stat, swap)
    spot_loss = make_spot_loss(plan, stat, stat_other, meta, row)
    rounds = [sum_round(0), sum_round(1)] if plan.plane == n_col else [[perm] for perm in sum_hops]
    for index, perms in enumerate(rounds):
        came = [send(sums, perm) for perm in perms]
        if index == 0:
            came, spot_loss = tie((came, spot_loss))
            came.append(jnp.concatenate([jnp.zeros((PACKED - 8, g), F32), spot_loss]))
        if ng_left:
            ng_came = send(ng_sum, ng_left.pop(0))
            came, ng_came = tie((came, ng_came))
            ng_sum = ng_sum + ng_came
        sums = sum(came, sums)
    for perm in ng_left:
        ng_sum = ng_sum + send(ng_sum, perm)
    order = [k % n_col for k in range(1, n_col + 1)]
    last = n_col - 1
    ghi, glo, keep, away, loss = make_gradient(
        plan, order[0], coef_gene, coef_spot, pred, spot, stat, stat_other, meta, sums, ng_sum, mhi, mlo
    )
    half = plan.chunk // 2
    state = {0: (bits - 1, keep, away)}
    pending = {}
    travelling = None
    other = other_sib = grad_logits = None
    at = LOSS_ROW % 8
    part = sums[PACKED - 8 :, :LANES]
    w = 0
    while True:
        flying = {}
        for i, value in reversed(list(state.items())):
            flying["chunk", i] = send(value[2], hops[value[0]])
        if travelling is not None:
            flying["ring"] = send(travelling, ring)
        work = {}
        if w == 0 and plan.cells <= 2048:
            made = make_cells(plan, order[1:], [half] * (2 * last), mhi, mlo, ghi, glo)
            for i in range(1, n_col):
                work["chunk", i] = (made[2 * i - 2], made[2 * i - 1])
        elif w < last and plan.cells > 2048:
            work["chunk", w + 1] = tuple(make_cells(plan, [order[w + 1]], [half, half], mhi, mlo, ghi, glo))
        if w == 1:
            work["other"] = make_other(plan, chi, clo, ghi, glo)
        elif w == 2:
            flying["other"] = send(other, swap)
        elif w == 3:
            work["logits"] = make_logits(plan, coef_spot, place, chi, clo, ghi, glo, other_sib, mhi, mlo, cell, meta, row)
        if w == 1:
            for index, perm in enumerate(rounds[0]):
                flying[f"part{index}"] = send(part, perm)
        elif w == 2:
            flying["part"] = send(part, swap)
        flying, work = meet(flying, work)
        other, other_sib = work.get("other", other), flying.get("other", other_sib)
        grad_logits = work.get("logits", grad_logits)
        if w == 1:
            part = sum([flying[f"part{index}"] for index in range(len(rounds[0]))], part)[at : at + 1, :] + loss[0:1, :]
        elif w == 2:
            part = part + flying["part"]
        for key, value in work.items():
            if isinstance(key, tuple):
                pending[key[1]] = value
        ended = None
        for i in list(state):
            step, keep, _ = state[i]
            came = flying["chunk", i]
            if step > 0:
                n = keep.shape[0] // 2
                state[i] = (step - 1, keep[:n] + came[:n], keep[n:] + came[n:])
            else:
                del state[i]
                ended = keep + came
                if "ring" in flying:
                    ended = ended + flying["ring"]
                finished = i
        travelling = ended
        if w + 1 < n_col:
            state[w + 1] = (bits - 1, *pending.pop(w + 1))
        w += 1
        if ended is not None and finished == last:
            result = ended
            break
    got = send(result, swap)
    def own_rows(result, got):
        first = jnp.concatenate([result[:rows], got[:rows]], axis=1)
        second = jnp.concatenate([got[rows:], result[rows:]], axis=1)
        return jnp.where(is_first, first, second)

    grad_expr = own_rows(result, got)
    return part[0, 0], grad_logits, grad_expr


def solution(mesh):
    in_specs = (
        P(None, AXES),
        P(AXES, None),
        P(AXES, None),
        P(),
        P(AXES),
        P(AXES),
    )
    out_specs = (P(), P(None, AXES), P(AXES, None))

    def whole(logits, cell_expr, spot_expr, cell_slide, spot_slide, spot_mask):
        n_spot, n_col = mesh.shape["spot"], mesh.shape["col"]
        plan = Plan(n_spot, n_col, logits.shape[0], logits.shape[1] // (n_spot * n_col), cell_expr.shape[1])
        return jax.shard_map(
            functools.partial(on_device, plan), mesh=mesh, in_specs=in_specs, out_specs=out_specs, check_vma=False
        )(logits, cell_expr, spot_expr, cell_slide, spot_slide, spot_mask)

    return whole
```

```python
import functools

import jax
import jax.numpy as jnp
from jax import lax
from jax.experimental import pallas as pl
from jax.experimental.pallas import tpu as pltpu
from jax.sharding import PartitionSpec as P

SLIDES = 11
ROWS = 16
PACKED = 24
LOSS_ROW = 22
PREDICT_TILE = 1024
GRADIENT_TILE = 512
SCALE = 0.001
EPS = 1e-06
AXES = ("spot", "col")
F32 = jnp.float32
BF16 = jnp.bfloat16
LANES = 128


def split(x):
    hi = x.astype(BF16)
    return hi, (x - hi.astype(F32)).astype(BF16)


def params(plan, small=16):
    return pltpu.CompilerParams(vmem_limit_bytes=(small if plan.cells <= 2048 else 60) << 20)


def kept(plan, shape, dtype):
    return pltpu.VMEM(shape, dtype) if plan.cells <= 2048 else jax.ShapeDtypeStruct(shape, dtype)


def pin(plan, *values):
    if plan.cells > 2048:
        return values
    return tuple(pltpu.with_memory_space_constraint(v, pltpu.VMEM) for v in values)


def cost(flops, bytes_accessed):
    return pl.CostEstimate(flops=int(flops * SCALE), bytes_accessed=int(bytes_accessed * SCALE), transcendentals=0)


class Plan:
    def __init__(self, n_spot, n_col, cells, spots, genes):
        self.n_col = n_col
        self.plane = n_spot // 2
        self.bits = self.plane.bit_length() - 1
        self.rows = cells // (n_spot * n_col)
        self.cells = cells
        self.half = spots
        self.pair = 2 * spots
        self.genes = genes // 2
        self.unit = 2 * self.rows
        self.chunk = self.plane * self.unit
        self.n_spot = n_spot
        self.total = n_spot * n_col
        self.tile = 256 if cells <= 2048 else 128

    def order(self, core):
        return list(range(self.bits)) if core == 0 else list(range(self.bits))[::-1]

    def reverse(self, m):
        return sum(((m >> b) & 1) << (self.bits - 1 - b) for b in range(self.bits))

    def device(self, plane, core, z):
        return (plane * 2 + core) * self.n_col + z

    def all_places(self):
        for plane in range(self.plane):
            for core in range(2):
                for z in range(self.n_col):
                    yield plane, core, z

    def swap_core(self):
        return [(self.device(q, c, z), self.device(q, 1 - c, z)) for q, c, z in self.all_places()]

    def ring(self):
        return [(self.device(q, c, z), self.device(q, c, (z + 1) % self.n_col)) for q, c, z in self.all_places()]

    def hop(self, step):
        return [
            (self.device(q, c, z), self.device(q ^ (1 << self.order(c)[step]), c, z))
            for q, c, z in self.all_places()
        ]

    def block_start(self, place_ref, k, m, c):
        plane, core, z = place_ref[0], place_ref[1], place_ref[2]
        shift = [0, 0]
        for which in range(2):
            for step, bit in enumerate(self.order(which)):
                shift[which] |= ((m >> step) & 1) << bit
        xor = jnp.where(core == 0, shift[0], shift[1])
        q = jnp.bitwise_xor(plane, xor)
        ring = lax.rem(z - k + self.n_col, self.n_col)
        return ((q * 2 + c) * self.n_col + ring) * self.rows


def blocks(plan):
    for k in range(plan.n_col):
        for m in range(plan.plane):
            for c in range(2):
                yield k, m, c


def mapping_kernel(plan, again, place, logits_ref, cell_ref, meta_ref, *refs):
    hi_ref, lo_ref, hit_ref, lot_ref, row_ref, w_ref = refs[4:] if again else refs
    meta = jnp.transpose(meta_ref[...])
    slide = meta[0:1, :]
    cell = jnp.concatenate([cell_ref[...]] * (plan.tile // LANES), axis=1)
    same = cell == slide
    x = logits_ref[...]
    masked = jnp.where(same, x, -jnp.inf)
    col_max = jnp.max(masked, axis=0, keepdims=True)
    w = jnp.exp(masked - col_max)
    total = jnp.sum(w, axis=0, keepdims=True)
    w_ref[...] = w * (1.0 / total)
    if again:
        row_ref[...] = jnp.zeros_like(row_ref)
    else:
        counts = jnp.sum(jnp.where(same, 1.0, 0.0), axis=0, keepdims=True)
        mean = jnp.sum(jnp.where(same, x, 0.0), axis=0, keepdims=True) / counts
        kl = (col_max + jnp.log(total) - mean - jnp.log(counts)) * meta[1:2, :]
        row = lax.broadcasted_iota(jnp.int32, (8, plan.tile), 0)
        row_ref[...] = jnp.where(row == 0, kl, counts)
    gather = max(LANES // plan.rows, 1)
    held = []
    for i, (k, m, c) in enumerate(blocks(plan)):
        start = pl.multiple_of(plan.block_start(place, k, m, c), plan.rows)
        block = w_ref[pl.ds(start, plan.rows), :]
        hi, lo = split(block)
        hi_ref[i * plan.rows : (i + 1) * plan.rows, :] = hi
        lo_ref[i * plan.rows : (i + 1) * plan.rows, :] = lo
        held.append(block)
        if len(held) == gather:
            wide = jnp.transpose(jnp.concatenate(held, axis=0))
            hi, lo = split(wide)
            end = (i + 1) * plan.rows
            hit_ref[:, end - LANES : end] = hi
            lot_ref[:, end - LANES : end] = lo
            held = []


def make_mapping(plan, place, logits, cell, meta, earlier=None):
    t, tiles = plan.tile, plan.half // plan.tile
    again = earlier is not None
    at = tiles if again else 0
    wide = kept(plan, (plan.cells, plan.pair), BF16)
    tall = kept(plan, (plan.pair, plan.cells), BF16)
    operands = [place, logits, cell, meta]
    in_specs = [
        pl.BlockSpec((plan.cells, t), lambda j, *_: (0, j)),
        pl.BlockSpec((plan.cells, LANES), lambda j, *_: (0, 0)),
        pl.BlockSpec((t, LANES), lambda j, *_: (j, 0)),
    ]
    if again:
        operands += list(pin(plan, *earlier[:4]))
        in_specs += [pl.BlockSpec(memory_space=pl.ANY)] * 4
    return pl.pallas_call(
        functools.partial(mapping_kernel, plan, again),
        out_shape=(wide, wide, tall, tall, jax.ShapeDtypeStruct((8, plan.half), F32)),
        grid_spec=pltpu.PrefetchScalarGridSpec(
            num_scalar_prefetch=1,
            grid=(tiles,),
            in_specs=in_specs,
            out_specs=[
                pl.BlockSpec((plan.cells, t), lambda j, *_: (0, j + at)),
                pl.BlockSpec((plan.cells, t), lambda j, *_: (0, j + at)),
                pl.BlockSpec((t, plan.cells), lambda j, *_: (j + at, 0)),
                pl.BlockSpec((t, plan.cells), lambda j, *_: (j + at, 0)),
                pl.BlockSpec((8, t), lambda j, *_: (0, j)),
            ],
            scratch_shapes=[pltpu.VMEM((plan.cells, t), F32)],
        ),
        input_output_aliases={4 + i: i for i in range(4)} if again else {},
        compiler_params=params(plan),
        cost_estimate=cost(plan.cells * plan.half * 20, plan.cells * plan.half * 12),
        name="mapping",
    )(*operands)


def onehot_rows(plan, meta):
    turned = jnp.transpose(meta)
    slide = lax.broadcasted_iota(jnp.int32, (ROWS, meta.shape[0]), 0).astype(F32)
    return jnp.where(turned[0:1, :] == slide, turned[1:2, :], 0.0).astype(BF16)


def slide_sum(onehot, value):
    hi, lo = split(value)
    return jnp.dot(
        jnp.concatenate([onehot, onehot], axis=1),
        jnp.concatenate([hi, lo], axis=0),
        preferred_element_type=F32,
    )


def row_sum(value):
    return jnp.sum(value, axis=1, keepdims=True)


def spots_kernel(plan, place, own_ref, sib_ref, meta_own, meta_sib, spot_ref, stat_ref, ng_ref):
    tiles = plan.half // 256
    j = pl.program_id(0)

    @pl.when(j == 0)
    def _():
        ng_ref[...] = jnp.zeros_like(ng_ref)

    def run(value_ref, meta_ref):
        value = value_ref[...]
        square = value * value
        spot_ref[...] = value
        stat_ref[...] = jnp.broadcast_to(row_sum(square), stat_ref.shape)
        ng_ref[...] += slide_sum(onehot_rows(plan, meta_ref[...]), square)

    @pl.when(j < tiles)
    def _():
        run(own_ref, meta_own)

    @pl.when(j >= tiles)
    def _():
        run(sib_ref, meta_sib)


def make_spots(plan, place, own, sib, meta_own, meta_sib):
    t, tiles, g = 256, plan.half // 256, plan.genes
    return pl.pallas_call(
        functools.partial(spots_kernel, plan),
        out_shape=(
            kept(plan, (plan.pair, g), F32),
            kept(plan, (plan.pair, LANES), F32),
            jax.ShapeDtypeStruct((ROWS, g), F32),
        ),
        grid_spec=pltpu.PrefetchScalarGridSpec(
            num_scalar_prefetch=1,
            grid=(2 * tiles,),
            in_specs=[
                pl.BlockSpec((t, g), lambda j, place: (jnp.minimum(j, tiles - 1), place[1])),
                pl.BlockSpec((t, g), lambda j, place: (jnp.maximum(j - tiles, 0), place[1])),
                pl.BlockSpec((t, LANES), lambda j, place: (jnp.minimum(j, tiles - 1), 0)),
                pl.BlockSpec((t, LANES), lambda j, place: (jnp.maximum(j - tiles, 0), 0)),
            ],
            out_specs=[
                pl.BlockSpec((t, g), lambda j, place: (j, 0)),
                pl.BlockSpec((t, LANES), lambda j, place: (j, 0)),
                pl.BlockSpec((ROWS, g), lambda j, place: (0, 0)),
            ],
        ),
        compiler_params=params(plan),
        cost_estimate=cost(plan.pair * g * 64, plan.pair * g * 8),
        name="spots",
    )(place, own, sib, meta_own, meta_sib)


def predict_kernel(plan, n_parts, first, last, *refs):
    refs = list(refs)
    parts = [refs.pop(0) for _ in range(n_parts)]
    hit_ref, lot_ref = refs.pop(0), refs.pop(0)
    acc_in = None
    if not first:
        acc_in = refs.pop(0)
        refs.pop(0), refs.pop(0)
    if last:
        spot_ref, gg_ref, meta_ref = refs.pop(0), refs.pop(0), refs.pop(0)
    acc_ref, chi_ref, clo_ref = refs.pop(0), refs.pop(0), refs.pop(0)
    if last:
        stat_ref, sums_ref = refs.pop(0), refs.pop(0)
    stack_ref = refs.pop(0)
    j = pl.program_id(0)
    size = plan.chunk

    @pl.when(j == 0)
    def _():
        at = 0
        for part in parts:
            n = part.shape[0]
            hi, lo = split(part[...])
            stack_ref[at : at + n, :] = hi
            stack_ref[size + at : size + at + n, :] = lo
            stack_ref[2 * size + at : 2 * size + at + n, :] = hi
            chi_ref[at : at + n, :] = hi
            clo_ref[at : at + n, :] = lo
            at += n
        if last:
            sums_ref[...] = jnp.zeros_like(sums_ref)

    left = jnp.concatenate([hit_ref[...], hit_ref[...], lot_ref[...]], axis=1)
    value = jnp.dot(left, stack_ref[...], preferred_element_type=F32)
    if not first:
        value = value + acc_in[...]
    acc_ref[...] = value
    if last:
        spot = spot_ref[...]
        square, cross = value * value, value * spot
        lane = lax.broadcasted_iota(jnp.int32, stat_ref.shape, 1)
        stat_ref[...] = jnp.where(lane == 0, row_sum(square), jnp.where(lane == 1, row_sum(cross), gg_ref[...]))
        turned = jnp.transpose(meta_ref[...])
        row = lax.broadcasted_iota(jnp.int32, (PACKED, value.shape[0]), 0).astype(F32)
        pick = lambda first: jnp.where(turned[0:1, :] + first == row, turned[1:2, :], 0.0).astype(BF16)
        left = jnp.concatenate([pick(0), pick(0), pick(SLIDES), pick(SLIDES)], axis=1)
        right = jnp.concatenate([*split(square), *split(cross)], axis=0)
        sums_ref[...] += jnp.dot(left, right, preferred_element_type=F32)


def make_predict(plan, k, parts, hit, lot, carry, last=None):
    t, g, size = PREDICT_TILE if plan.cells <= 2048 else 256, plan.genes, plan.chunk
    const = lambda j: (0, 0)
    in_specs = [pl.BlockSpec(p.shape, const) for p in parts]
    in_specs += [pl.BlockSpec((t, size), lambda j: (j, k))] * 2
    operands = [*parts, *pin(plan, hit, lot)]
    aliases = {}
    if carry is not None:
        at = len(operands)
        operands += list(pin(plan, *carry))
        in_specs += [pl.BlockSpec((t, g), lambda j: (j, 0)), pl.BlockSpec(memory_space=pl.ANY), pl.BlockSpec(memory_space=pl.ANY)]
        aliases = {at: 0, at + 1: 1, at + 2: 2}
    out_shape = [
        kept(plan, (plan.pair, g), F32),
        kept(plan, (plan.cells, g), BF16),
        kept(plan, (plan.cells, g), BF16),
    ]
    out_specs = [pl.BlockSpec((t, g), lambda j: (j, 0))] + [pl.BlockSpec((size, g), lambda j: (k, 0))] * 2
    if last is not None:
        operands += list(pin(plan, *last[:2])) + list(last[2:])
        in_specs += [pl.BlockSpec((t, g), lambda j: (j, 0))] + [pl.BlockSpec((t, LANES), lambda j: (j, 0))] * 2
        out_shape += [jax.ShapeDtypeStruct((plan.pair, LANES), F32), jax.ShapeDtypeStruct((PACKED, g), F32)]
        out_specs += [pl.BlockSpec((t, LANES), lambda j: (j, 0)), pl.BlockSpec((PACKED, g), const)]
    return pl.pallas_call(
        functools.partial(predict_kernel, plan, len(parts), carry is None, last is not None),
        out_shape=tuple(out_shape),
        grid=(plan.pair // t,),
        in_specs=in_specs,
        out_specs=out_specs,
        scratch_shapes=[pltpu.VMEM((3 * size, g), BF16)],
        input_output_aliases=aliases,
        compiler_params=params(plan),
        cost_estimate=cost(6 * plan.pair * g * size, plan.pair * g * 8),
        name="predict",
    )(*operands)


def spot_loss_kernel(plan, mine_ref, other_ref, meta_ref, row_ref, out_ref):
    stat = mine_ref[0 : plan.half, :] + other_ref[plan.half :, :]
    cosine = stat[:, 1:2] * (lax.rsqrt(stat[:, 0:1] + EPS) * lax.rsqrt(stat[:, 2:3] + EPS))
    total = jnp.sum(row_ref[0:1, :], keepdims=True) - jnp.sum(cosine * meta_ref[...][0 : plan.half, 1:2], keepdims=True)
    row = lax.broadcasted_iota(jnp.int32, out_ref.shape, 0)
    out_ref[...] = jnp.where(row == LOSS_ROW % 8, total / (plan.half * plan.total), 0.0)


def make_spot_loss(plan, mine, other, meta, row):
    return pl.pallas_call(
        functools.partial(spot_loss_kernel, plan),
        out_shape=jax.ShapeDtypeStruct((8, plan.genes), F32),
        in_specs=[pl.BlockSpec(memory_space=pltpu.VMEM)] * 4,
        out_specs=pl.BlockSpec(memory_space=pltpu.VMEM),
        compiler_params=params(plan),
        cost_estimate=cost(plan.half * 8, plan.half * 1024),
        name="spot_loss",
    )(*pin(plan, mine), other, meta, row)


def gradient_kernel(plan, coef_gene, coef_spot, pred_ref, spot_ref, mine_ref, other_ref, meta_ref, sums_ref, ng_ref,
                    mhi_ref, mlo_ref, ghi_ref, glo_ref, keep_ref, send_ref, loss_ref, a_ref, b_ref, acc_ref):
    j = pl.program_id(0)

    @pl.when(j == 0)
    def _():
        pad = jnp.zeros((ROWS - SLIDES, sums_ref.shape[1]), F32)
        parts = [sums_ref[i * SLIDES : (i + 1) * SLIDES, :] for i in range(2)]
        np_sum, dots = [jnp.concatenate([part, pad], axis=0) for part in parts]
        ng_sum = ng_ref[...]
        scale = lax.rsqrt(np_sum + EPS) * lax.rsqrt(ng_sum + EPS)
        cosine = dots * scale
        hi, lo = split(-coef_gene * scale)
        a_ref[0:ROWS, :] = hi
        a_ref[ROWS : 2 * ROWS, :] = lo
        hi, lo = split(coef_gene * (cosine / (np_sum + EPS)))
        b_ref[0:ROWS, :] = hi
        b_ref[ROWS : 2 * ROWS, :] = lo
        acc_ref[...] = jnp.zeros_like(acc_ref)
        row = lax.broadcasted_iota(jnp.int32, cosine.shape, 0)
        gene = jnp.sum(jnp.where(row < SLIDES, cosine, 0.0), keepdims=True) / (SLIDES * 2 * plan.genes)
        loss_ref[...] = jnp.broadcast_to(-gene, loss_ref.shape)

    stat = mine_ref[...] + other_ref[...]
    spot_sq, cross, true_sq = stat[:, 0:1], stat[:, 1:2], stat[:, 2:3]
    slide, mask = meta_ref[...][:, 0:1], meta_ref[...][:, 1:2]
    scale = lax.rsqrt(spot_sq + EPS) * lax.rsqrt(true_sq + EPS)
    cosine = cross * scale

    weight = coef_spot * mask
    lane = lax.broadcasted_iota(jnp.int32, (stat.shape[0], ROWS), 1).astype(F32)
    onehot = jnp.where(slide == lane, mask, 0.0).astype(BF16)
    onehot = jnp.concatenate([onehot, onehot], axis=1)
    gene_a = jnp.dot(onehot, a_ref[...], preferred_element_type=F32)
    gene_b = jnp.dot(onehot, b_ref[...], preferred_element_type=F32)
    grad = spot_ref[...] * (gene_a - weight * scale) + pred_ref[...] * (gene_b + weight * (cosine / (spot_sq + EPS)))
    hi, lo = split(grad)
    ghi_ref[...] = hi
    glo_ref[...] = lo
    left = jnp.concatenate([mhi_ref[...], mhi_ref[...], mlo_ref[...]], axis=1)
    right = jnp.concatenate([hi, lo, hi], axis=0)
    acc_ref[...] += jnp.dot(left, right, preferred_element_type=F32)

    @pl.when(j == pl.num_programs(0) - 1)
    def _():
        n = keep_ref.shape[0]
        keep_ref[...] = acc_ref[0:n, :]
        send_ref[...] = acc_ref[n:, :]


def make_gradient(plan, k, coef_gene, coef_spot, pred, spot, mine, other, meta, sums, ng_sum, mhi, mlo):
    t, g, size = GRADIENT_TILE if plan.cells <= 2048 else 256, plan.genes, plan.chunk
    tiles = plan.pair // t
    tile = lambda j: (j, 0)
    const = lambda j: (0, 0)
    halves = jax.ShapeDtypeStruct((size // 2, g), F32)
    return pl.pallas_call(
        functools.partial(gradient_kernel, plan, coef_gene, coef_spot),
        out_shape=(
            kept(plan, (plan.pair, g), BF16),
            kept(plan, (plan.pair, g), BF16),
            halves,
            halves,
            jax.ShapeDtypeStruct((8, LANES), F32),
        ),
        grid=(tiles,),
        in_specs=[
            pl.BlockSpec((t, g), tile),
            pl.BlockSpec((t, g), tile),
            pl.BlockSpec((t, LANES), tile),
            pl.BlockSpec((t, LANES), lambda j: ((j + tiles // 2) % tiles, 0)),
            pl.BlockSpec((t, LANES), tile),
            pl.BlockSpec((PACKED, g), const),
            pl.BlockSpec((ROWS, g), const),
            pl.BlockSpec((size, t), lambda j: (k, j)),
            pl.BlockSpec((size, t), lambda j: (k, j)),
        ],
        out_specs=[
            pl.BlockSpec((t, g), tile),
            pl.BlockSpec((t, g), tile),
            pl.BlockSpec((size // 2, g), const),
            pl.BlockSpec((size // 2, g), const),
            pl.BlockSpec((8, LANES), const),
        ],
        scratch_shapes=[pltpu.VMEM((2 * ROWS, g), BF16), pltpu.VMEM((2 * ROWS, g), BF16), pltpu.VMEM((size, g), F32)],
        compiler_params=params(plan),
        cost_estimate=cost(6 * plan.pair * g * size, plan.pair * g * 12),
        name="gradient",
    )(*pin(plan, pred, spot), mine, other, meta, sums, ng_sum, *pin(plan, mhi, mlo))


def cells_kernel(plan, ks, whole, mhi_ref, mlo_ref, ghi_ref, glo_ref, *outs):
    def rows(ref):
        if not whole:
            return ref[...]
        return jnp.concatenate([ref[k * plan.chunk : (k + 1) * plan.chunk, :] for k in ks], axis=0)

    hi, lo = rows(mhi_ref), rows(mlo_ref)
    left = jnp.concatenate([hi, hi, lo], axis=1)
    right = jnp.concatenate([ghi_ref[...], glo_ref[...], ghi_ref[...]], axis=0)
    value = jnp.dot(left, right, preferred_element_type=F32)
    at = 0
    for out in outs:
        out[...] = value[at : at + out.shape[0], :]
        at += out.shape[0]


def make_cells(plan, ks, sizes, mhi, mlo, ghi, glo):
    t, g, size = 256, plan.genes, plan.chunk
    whole = len(ks) > 1
    rows = (plan.cells, plan.pair) if whole else (size, plan.pair)
    at = 0 if whole else ks[0]
    return pl.pallas_call(
        functools.partial(cells_kernel, plan, ks, whole),
        out_shape=tuple(jax.ShapeDtypeStruct((n, g), F32) for n in sizes),
        grid=(g // t,),
        in_specs=[pl.BlockSpec(rows, lambda i: (at, 0))] * 2 + [pl.BlockSpec((plan.pair, t), lambda i: (0, i))] * 2,
        out_specs=[pl.BlockSpec((n, t), lambda i: (0, i)) for n in sizes],
        compiler_params=params(plan),
        cost_estimate=cost(6 * plan.pair * g * size * len(ks), plan.pair * g * 4),
        name="cells",
    )(*pin(plan, mhi, mlo, ghi, glo))


def turned_dot(chi, clo, ghi, glo):
    left = jnp.concatenate([chi, chi, clo], axis=1)
    right = jnp.concatenate([ghi, glo, ghi], axis=1)
    return lax.dot_general(left, right, (((1,), (1,)), ((), ())), preferred_element_type=F32)


def other_kernel(chi_ref, clo_ref, ghi_ref, glo_ref, out_ref):
    out_ref[...] = turned_dot(chi_ref[...], clo_ref[...], ghi_ref[...], glo_ref[...])


def cell_tile(plan):
    return min(plan.cells, 1024)


def make_other(plan, chi, clo, ghi, glo):
    t, g, ct = plan.tile, plan.genes, cell_tile(plan)
    tiles = plan.half // t
    return pl.pallas_call(
        other_kernel,
        out_shape=jax.ShapeDtypeStruct((plan.cells, plan.half), F32),
        grid=(tiles, plan.cells // ct),
        in_specs=[pl.BlockSpec((ct, g), lambda j, i: (i, 0))] * 2 + [pl.BlockSpec((t, g), lambda j, i: (j + tiles, 0))] * 2,
        out_specs=pl.BlockSpec((ct, t), lambda j, i: (i, j)),
        compiler_params=params(plan),
        cost_estimate=cost(6 * plan.cells * g * plan.half, plan.cells * plan.half * 12),
        name="other",
    )(*pin(plan, chi, clo, ghi, glo))


def logits_kernel(plan, coef_spot, place, chi_ref, clo_ref, ghi_ref, glo_ref, got_ref, mhi_ref, mlo_ref, cell_ref, meta_ref, row_ref,
                  out_ref, acc_ref):
    ct = cell_tile(plan)
    i = pl.program_id(1)
    rows = pl.ds(pl.multiple_of(i * ct, ct), ct)
    acc_ref[rows, :] = turned_dot(chi_ref[...], clo_ref[...], ghi_ref[...], glo_ref[...])

    @pl.when(i == pl.num_programs(1) - 1)
    def _():
        for k in range(plan.n_col):
            for m in range(plan.plane):
                at, there = (k * plan.plane + m) * plan.unit, (k * plan.plane + plan.reverse(m)) * plan.unit
                acc_ref[at : at + plan.unit, :] += got_ref[there : there + plan.unit, :]
        value = acc_ref[...]
        weight = mhi_ref[...].astype(F32) + mlo_ref[...].astype(F32)
        inner = jnp.sum(weight * value, axis=0, keepdims=True)
        meta = jnp.transpose(meta_ref[...])
        slide, coef = meta[0:1, :], coef_spot * meta[1:2, :]
        share = coef / row_ref[...][1:2, :]
        acc_ref[...] = weight * (value - inner + coef)
        for n, (k, m, c) in enumerate(blocks(plan)):
            start = pl.multiple_of(plan.block_start(place, k, m, c), plan.rows)
            cell = jnp.concatenate([cell_ref[pl.ds(start, plan.rows), :]] * (plan.tile // LANES), axis=1)
            out_ref[pl.ds(start, plan.rows), :] = acc_ref[n * plan.rows : (n + 1) * plan.rows, :] - jnp.where(cell == slide, share, 0.0)


def make_logits(plan, coef_spot, place, chi, clo, ghi, glo, got, mhi, mlo, cell, meta, row):
    t, g, ct = plan.tile, plan.genes, cell_tile(plan)
    column = lambda j, i, *_: (0, j)
    return pl.pallas_call(
        functools.partial(logits_kernel, plan, coef_spot),
        out_shape=jax.ShapeDtypeStruct((plan.cells, plan.half), F32),
        grid_spec=pltpu.PrefetchScalarGridSpec(
            num_scalar_prefetch=1,
            grid=(plan.half // t, plan.cells // ct),
            in_specs=[pl.BlockSpec((ct, g), lambda j, i, *_: (i, 0))] * 2
            + [pl.BlockSpec((t, g), lambda j, i, *_: (j, 0))] * 2
            + [pl.BlockSpec((plan.cells, t), column)] * 3
            + [
                pl.BlockSpec((plan.cells, LANES), lambda j, i, *_: (0, 0)),
                pl.BlockSpec((t, LANES), lambda j, i, *_: (j, 0)),
                pl.BlockSpec((8, t), column),
            ],
            out_specs=pl.BlockSpec((plan.cells, t), column),
            scratch_shapes=[pltpu.VMEM((plan.cells, t), F32)],
        ),
        compiler_params=params(plan, 24),
        cost_estimate=cost(6 * plan.cells * g * plan.half, plan.cells * plan.half * 20),
        name="logits",
    )(place, *pin(plan, chi, clo, ghi, glo), got, *pin(plan, mhi, mlo), cell, meta, row)


def on_device(plan, logits, cell_expr, spot_expr, cell_slide, spot_slide, spot_mask):
    g, rows = plan.genes, plan.rows
    spots_all = plan.half * plan.total
    factor = spots_all * plan.cells / SLIDES
    coef_spot = factor / spots_all
    coef_gene = factor / (SLIDES * 2 * g)
    spot_index, z = lax.axis_index("spot"), lax.axis_index("col")
    core, plane = spot_index % 2, spot_index // 2
    place = jnp.stack([plane, core, z]).astype(jnp.int32)
    send = lambda value, perm: lax.ppermute(value, AXES, perm)
    swap = plan.swap_core()
    hops = [plan.hop(step) for step in range(plan.bits)]

    tie = lax.optimization_barrier
    tie = lax.optimization_barrier

    def meet(flying, work):
        names, jobs = list(flying), list(work)
        came, made = tie(([flying[name] for name in names], [work[job] for job in jobs]))
        return dict(zip(names, came)), dict(zip(jobs, made))

    is_first = core == 0
    place, is_first = tie((place, is_first))
    lane = lax.broadcasted_iota(jnp.int32, (plan.half, LANES), 1)
    describe = lambda slide, mask: jnp.where(lane == 0, slide[:, None], mask[:, None]).astype(F32)
    meta_own = describe(spot_slide, spot_mask)
    cell = jnp.broadcast_to(cell_slide[:, None].astype(F32), (plan.cells, LANES))
    got, slide_sib, mask_sib = send(cell_expr, swap), send(spot_slide, swap), send(spot_mask, swap)
    got, slide_sib, mask_sib, meta_own, logits, spot_expr = tie((got, slide_sib, mask_sib, meta_own, logits, spot_expr))
    meta_sib = describe(slide_sib, mask_sib)
    first, second = jnp.concatenate([cell_expr[:, :g], got[:, :g]]), jnp.concatenate([got[:, g:], cell_expr[:, g:]])
    unit = jnp.where(is_first, first, second)
    logits_sib = spot_sib = None

    plane_hops = [("plane", 1 << bit) for bit in range(plan.bits)]
    ring_hops = [("ring", 1 << bit) for bit in range(plan.n_col.bit_length() - 1)]
    sum_orders = (plane_hops + ring_hops, ring_hops + plane_hops)

    def sum_hop(index):
        perm = []
        for q, c, i in plan.all_places():
            kind, bit = sum_orders[c][index]
            there = plan.device(q ^ bit, c, i) if kind == "plane" else plan.device(q, c, i ^ bit)
            perm.append((plan.device(q, c, i), there))
        return perm

    sum_hops = [sum_hop(index) for index in range(len(plane_hops) + len(ring_hops))]

    ring_sums = [
        [(plan.device(q, c, i), plan.device(q, c, i ^ bit)) for q, c, i in plan.all_places()] for _, bit in ring_hops
    ]
    plane_sums = [plan.hop(step) for step in range(plan.bits)]

    def sum_step(bit):
        perm = []
        for q, c, i in plan.all_places():
            there = plan.device(q ^ (1 << bit), c, i) if c == 0 else plan.device(q, c, i ^ (1 << bit))
            perm.append((plan.device(q, c, i), there))
        return perm

    def sum_round(index):
        perms = []
        for other in reversed(range(1, plan.plane)):
            perm = []
            for q, c, i in plan.all_places():
                there = plan.device(q ^ other, c, i) if c == index else plan.device(q, c, i ^ other)
                perm.append((plan.device(q, c, i), there))
            perms.append(perm)
        return perms

    n_col, bits = plan.n_col, plan.bits
    ring = plan.ring()
    units = {0: unit}
    parts = {}
    carry = mapping = spots = None
    row = None
    ng_left = [ring_hop for ring_hop in ring_sums] + [plane_hop for plane_hop in plane_sums]
    windows = n_col + bits - 1
    for w in range(windows):
        flying = {}
        for k in range(max(0, w - bits + 1), min(w + 1, n_col)):
            held = parts.setdefault(k, {0: units[k]})
            step = w - k
            fresh = [m for m in held if m.bit_length() == step] if step else [0]
            for m in fresh:
                for later in range(step, bits):
                    flying[k, m | (1 << later)] = send(held[m], hops[later])
        if w + 1 < n_col:
            flying["unit"] = send(units[w], ring)
        work = {}
        if w == 0:
            logits_sib, spot_sib = send(logits, swap), send(spot_expr, swap)
            own = make_mapping(plan, place, logits, cell, meta_own)
            work["row"] = own[4]
            work["mapping"] = own
            flying["logits"], flying["spot"] = logits_sib, spot_sib
        elif w == 1:
            work["mapping"] = make_mapping(plan, place, logits_sib, cell, meta_sib, mapping)
        if w == 2:
            work["spots"] = make_spots(plan, place, spot_expr, spot_sib, meta_own, meta_sib)
        if w >= bits:
            k = w - bits
            pieces = [parts[k][m] for m in range(plan.plane)]
            work["carry"] = make_predict(plan, k, pieces, mapping[2], mapping[3], carry)
            parts[k] = None
        if spots is not None and ng_left:
            flying["ng"] = send(spots[2], ng_left.pop(0))
        flying, work = meet(flying, work)
        if "ng" in flying:
            spots = (*spots[:2], spots[2] + flying["ng"])
        for key, value in flying.items():
            if key == "unit":
                units[w + 1] = value
            elif isinstance(key, tuple):
                parts[key[0]][key[1]] = value
        if w == 0:
            logits_sib, spot_sib = flying["logits"], flying["spot"]
        mapping, spots, carry = work.get("mapping", mapping), work.get("spots", spots), work.get("carry", carry)
        row = work.get("row", row)
    mhi, mlo, hit, lot, _ = mapping
    spot, true_sq, ng_sum = spots
    meta = jnp.concatenate([meta_own, meta_sib])
    k = n_col - 1
    pieces = [parts[k][m] for m in range(plan.plane)]
    pred, chi, clo, stat, sums = make_predict(plan, k, pieces, hit, lot, carry, (spot, true_sq, meta))

    stat_other = send(stat, swap)
    spot_loss = make_spot_loss(plan, stat, stat_other, meta, row)
    rounds = [sum_round(0), sum_round(1)] if plan.plane == n_col else [[perm] for perm in sum_hops]
    for index, perms in enumerate(rounds):
        came = [send(sums, perm) for perm in perms]
        if index == 0:
            came, spot_loss = tie((came, spot_loss))
            came.append(jnp.concatenate([jnp.zeros((PACKED - 8, g), F32), spot_loss]))
        if ng_left:
            ng_came = send(ng_sum, ng_left.pop(0))
            came, ng_came = tie((came, ng_came))
            ng_sum = ng_sum + ng_came
        sums = sum(came, sums)
    for perm in ng_left:
        ng_sum = ng_sum + send(ng_sum, perm)
    order = [k % n_col for k in range(1, n_col + 1)]
    last = n_col - 1
    ghi, glo, keep, away, loss = make_gradient(
        plan, order[0], coef_gene, coef_spot, pred, spot, stat, stat_other, meta, sums, ng_sum, mhi, mlo
    )
    half = plan.chunk // 2
    state = {0: (bits - 1, keep, away)}
    pending = {}
    travelling = None
    other = other_sib = grad_logits = None
    at = LOSS_ROW % 8
    part = sums[PACKED - 8 :, :LANES]
    if plan.plane == n_col:
        part_hops = [sum_step(bit) for bit in range(bits)] + [swap]
    else:
        part_hops = [sum_hops[0], swap]
    w = 0
    while True:
        flying = {}
        for i, value in reversed(list(state.items())):
            flying["chunk", i] = send(value[2], hops[value[0]])
        if travelling is not None:
            flying["ring"] = send(travelling, ring)
        work = {}
        if w == 0 and plan.cells <= 2048:
            made = make_cells(plan, order[1:], [half] * (2 * last), mhi, mlo, ghi, glo)
            for i in range(1, n_col):
                work["chunk", i] = (made[2 * i - 2], made[2 * i - 1])
        elif w < last and plan.cells > 2048:
            work["chunk", w + 1] = tuple(make_cells(plan, [order[w + 1]], [half, half], mhi, mlo, ghi, glo))
        if w == 2:
            work["other"] = make_other(plan, chi, clo, ghi, glo)
        elif w == 3:
            flying["other"] = send(other, swap)
        elif w == 4:
            work["logits"] = make_logits(plan, coef_spot, place, chi, clo, ghi, glo, other_sib, mhi, mlo, cell, meta, row)
        if 1 <= w <= len(part_hops):
            flying["part"] = send(part, part_hops[w - 1])
        flying, work = meet(flying, work)
        other, other_sib = work.get("other", other), flying.get("other", other_sib)
        grad_logits = work.get("logits", grad_logits)
        if "part" in flying:
            part = part + flying["part"]
            if w == len(part_hops) - 1:
                part = part[at : at + 1, :] + loss[0:1, :]
        for key, value in work.items():
            if isinstance(key, tuple):
                pending[key[1]] = value
        ended = None
        for i in list(state):
            step, keep, _ = state[i]
            came = flying["chunk", i]
            if step > 0:
                n = keep.shape[0] // 2
                state[i] = (step - 1, keep[:n] + came[:n], keep[n:] + came[n:])
            else:
                del state[i]
                ended = keep + came
                if "ring" in flying:
                    ended = ended + flying["ring"]
                finished = i
        travelling = ended
        if w + 1 < n_col:
            state[w + 1] = (bits - 1, *pending.pop(w + 1))
        w += 1
        if ended is not None and finished == last:
            result = ended
            break
    got = send(result, swap)
    def own_rows(result, got):
        first = jnp.concatenate([result[:rows], got[:rows]], axis=1)
        second = jnp.concatenate([got[rows:], result[rows:]], axis=1)
        return jnp.where(is_first, first, second)

    grad_expr = own_rows(result, got)
    return part[0, 0], grad_logits, grad_expr


def solution(mesh):
    in_specs = (
        P(None, AXES),
        P(AXES, None),
        P(AXES, None),
        P(),
        P(AXES),
        P(AXES),
    )
    out_specs = (P(), P(None, AXES), P(AXES, None))

    def whole(logits, cell_expr, spot_expr, cell_slide, spot_slide, spot_mask):
        n_spot, n_col = mesh.shape["spot"], mesh.shape["col"]
        plan = Plan(n_spot, n_col, logits.shape[0], logits.shape[1] // (n_spot * n_col), cell_expr.shape[1])
        return jax.shard_map(
            functools.partial(on_device, plan), mesh=mesh, in_specs=in_specs, out_specs=out_specs, check_vma=False
        )(logits, cell_expr, spot_expr, cell_slide, spot_slide, spot_mask)

    return whole
```

```python
import functools

import jax
import jax.numpy as jnp
from jax import lax
from jax.experimental import pallas as pl
from jax.experimental.pallas import tpu as pltpu
from jax.sharding import PartitionSpec as P

SLIDES = 11
ROWS = 16
PACKED = 24
LOSS_ROW = 22
PREDICT_TILE = 1024
GRADIENT_TILE = 512
SCALE = 0.001
EPS = 1e-06
AXES = ("spot", "col")
F32 = jnp.float32
BF16 = jnp.bfloat16
LANES = 128


def split(x):
    hi = x.astype(BF16)
    return hi, (x - hi.astype(F32)).astype(BF16)


def split3(x):
    hi = x.astype(BF16)
    rest = x - hi.astype(F32)
    mid = rest.astype(BF16)
    return hi, mid, (rest - mid.astype(F32)).astype(BF16)


def params(plan, small=16):
    return pltpu.CompilerParams(vmem_limit_bytes=(small if plan.cells <= 2048 else 60) << 20)


def kept(plan, shape, dtype):
    return pltpu.VMEM(shape, dtype) if plan.cells <= 2048 else jax.ShapeDtypeStruct(shape, dtype)


def pin(plan, *values):
    if plan.cells > 2048:
        return values
    return tuple(pltpu.with_memory_space_constraint(v, pltpu.VMEM) for v in values)


def cost(flops, bytes_accessed):
    return pl.CostEstimate(flops=int(flops * SCALE), bytes_accessed=int(bytes_accessed * SCALE), transcendentals=0)


class Plan:
    def __init__(self, n_spot, n_col, cells, spots, genes):
        self.n_col = n_col
        self.plane = n_spot // 2
        self.bits = self.plane.bit_length() - 1
        self.rows = cells // (n_spot * n_col)
        self.cells = cells
        self.half = spots
        self.pair = 2 * spots
        self.genes = genes // 2
        self.unit = 2 * self.rows
        self.chunk = self.plane * self.unit
        self.n_spot = n_spot
        self.total = n_spot * n_col
        self.tile = 256 if cells <= 2048 else 128

    def order(self, core):
        return list(range(self.bits)) if core == 0 else list(range(self.bits))[::-1]

    def reverse(self, m):
        return sum(((m >> b) & 1) << (self.bits - 1 - b) for b in range(self.bits))

    def device(self, plane, core, z):
        return (plane * 2 + core) * self.n_col + z

    def all_places(self):
        for plane in range(self.plane):
            for core in range(2):
                for z in range(self.n_col):
                    yield plane, core, z

    def swap_core(self):
        return [(self.device(q, c, z), self.device(q, 1 - c, z)) for q, c, z in self.all_places()]

    def ring(self):
        return [(self.device(q, c, z), self.device(q, c, (z + 1) % self.n_col)) for q, c, z in self.all_places()]

    def hop(self, step):
        return [
            (self.device(q, c, z), self.device(q ^ (1 << self.order(c)[step]), c, z))
            for q, c, z in self.all_places()
        ]

    def block_start(self, place_ref, k, m, c):
        plane, core, z = place_ref[0], place_ref[1], place_ref[2]
        shift = [0, 0]
        for which in range(2):
            for step, bit in enumerate(self.order(which)):
                shift[which] |= ((m >> step) & 1) << bit
        xor = jnp.where(core == 0, shift[0], shift[1])
        q = jnp.bitwise_xor(plane, xor)
        ring = lax.rem(z - k + self.n_col, self.n_col)
        return ((q * 2 + c) * self.n_col + ring) * self.rows


def blocks(plan):
    for k in range(plan.n_col):
        for m in range(plan.plane):
            for c in range(2):
                yield k, m, c


def mapping_kernel(plan, again, place, logits_ref, cell_ref, meta_ref, *refs):
    hi_ref, lo_ref, hit_ref, lot_ref, row_ref, w_ref = refs[4:] if again else refs
    meta = jnp.transpose(meta_ref[...])
    slide = meta[0:1, :]
    cell = jnp.concatenate([cell_ref[...]] * (plan.tile // LANES), axis=1)
    same = cell == slide
    x = logits_ref[...]
    masked = jnp.where(same, x, -jnp.inf)
    col_max = jnp.max(masked, axis=0, keepdims=True)
    w = jnp.exp(masked - col_max)
    total = jnp.sum(w, axis=0, keepdims=True)
    w_ref[...] = w * (1.0 / total)
    if again:
        row_ref[...] = jnp.zeros_like(row_ref)
    else:
        counts = jnp.sum(jnp.where(same, 1.0, 0.0), axis=0, keepdims=True)
        mean = jnp.sum(jnp.where(same, x, 0.0), axis=0, keepdims=True) / counts
        kl = (col_max + jnp.log(total) - mean - jnp.log(counts)) * meta[1:2, :]
        row = lax.broadcasted_iota(jnp.int32, (8, plan.tile), 0)
        row_ref[...] = jnp.where(row == 0, kl, counts)
    gather = max(LANES // plan.rows, 1)
    held = []
    for i, (k, m, c) in enumerate(blocks(plan)):
        start = pl.multiple_of(plan.block_start(place, k, m, c), plan.rows)
        block = w_ref[pl.ds(start, plan.rows), :]
        hi, lo = split(block)
        hi_ref[i * plan.rows : (i + 1) * plan.rows, :] = hi
        lo_ref[i * plan.rows : (i + 1) * plan.rows, :] = lo
        held.append(block)
        if len(held) == gather:
            wide = jnp.transpose(jnp.concatenate(held, axis=0))
            hi, lo = split(wide)
            end = (i + 1) * plan.rows
            hit_ref[:, end - LANES : end] = hi
            lot_ref[:, end - LANES : end] = lo
            held = []


def make_mapping(plan, place, logits, cell, meta, earlier=None):
    t, tiles = plan.tile, plan.half // plan.tile
    again = earlier is not None
    at = tiles if again else 0
    wide = kept(plan, (plan.cells, plan.pair), BF16)
    tall = kept(plan, (plan.pair, plan.cells), BF16)
    operands = [place, logits, cell, meta]
    in_specs = [
        pl.BlockSpec((plan.cells, t), lambda j, *_: (0, j)),
        pl.BlockSpec((plan.cells, LANES), lambda j, *_: (0, 0)),
        pl.BlockSpec((t, LANES), lambda j, *_: (j, 0)),
    ]
    if again:
        operands += list(pin(plan, *earlier[:4]))
        in_specs += [pl.BlockSpec(memory_space=pl.ANY)] * 4
    return pl.pallas_call(
        functools.partial(mapping_kernel, plan, again),
        out_shape=(wide, wide, tall, tall, jax.ShapeDtypeStruct((8, plan.half), F32)),
        grid_spec=pltpu.PrefetchScalarGridSpec(
            num_scalar_prefetch=1,
            grid=(tiles,),
            in_specs=in_specs,
            out_specs=[
                pl.BlockSpec((plan.cells, t), lambda j, *_: (0, j + at)),
                pl.BlockSpec((plan.cells, t), lambda j, *_: (0, j + at)),
                pl.BlockSpec((t, plan.cells), lambda j, *_: (j + at, 0)),
                pl.BlockSpec((t, plan.cells), lambda j, *_: (j + at, 0)),
                pl.BlockSpec((8, t), lambda j, *_: (0, j)),
            ],
            scratch_shapes=[pltpu.VMEM((plan.cells, t), F32)],
        ),
        input_output_aliases={4 + i: i for i in range(4)} if again else {},
        compiler_params=params(plan),
        cost_estimate=cost(plan.cells * plan.half * 20, plan.cells * plan.half * 12),
        name="mapping",
    )(*operands)


def onehot_rows(plan, meta):
    turned = jnp.transpose(meta)
    slide = lax.broadcasted_iota(jnp.int32, (ROWS, meta.shape[0]), 0).astype(F32)
    return jnp.where(turned[0:1, :] == slide, turned[1:2, :], 0.0).astype(BF16)


def slide_sum(onehot, value):
    return jnp.dot(
        jnp.concatenate([onehot] * 3, axis=1),
        jnp.concatenate(split3(value), axis=0),
        preferred_element_type=F32,
    )


def row_sum(value):
    return jnp.sum(value, axis=1, keepdims=True)


def spots_kernel(plan, place, own_ref, sib_ref, meta_own, meta_sib, spot_ref, stat_ref, ng_ref):
    tiles = plan.half // 256
    j = pl.program_id(0)

    @pl.when(j == 0)
    def _():
        ng_ref[...] = jnp.zeros_like(ng_ref)

    def run(value_ref, meta_ref):
        value = value_ref[...]
        square = value * value
        spot_ref[...] = value
        stat_ref[...] = jnp.broadcast_to(row_sum(square), stat_ref.shape)
        ng_ref[...] += slide_sum(onehot_rows(plan, meta_ref[...]), square)

    @pl.when(j < tiles)
    def _():
        run(own_ref, meta_own)

    @pl.when(j >= tiles)
    def _():
        run(sib_ref, meta_sib)


def make_spots(plan, place, own, sib, meta_own, meta_sib):
    t, tiles, g = 256, plan.half // 256, plan.genes
    return pl.pallas_call(
        functools.partial(spots_kernel, plan),
        out_shape=(
            kept(plan, (plan.pair, g), F32),
            kept(plan, (plan.pair, LANES), F32),
            jax.ShapeDtypeStruct((ROWS, g), F32),
        ),
        grid_spec=pltpu.PrefetchScalarGridSpec(
            num_scalar_prefetch=1,
            grid=(2 * tiles,),
            in_specs=[
                pl.BlockSpec((t, g), lambda j, place: (jnp.minimum(j, tiles - 1), place[1])),
                pl.BlockSpec((t, g), lambda j, place: (jnp.maximum(j - tiles, 0), place[1])),
                pl.BlockSpec((t, LANES), lambda j, place: (jnp.minimum(j, tiles - 1), 0)),
                pl.BlockSpec((t, LANES), lambda j, place: (jnp.maximum(j - tiles, 0), 0)),
            ],
            out_specs=[
                pl.BlockSpec((t, g), lambda j, place: (j, 0)),
                pl.BlockSpec((t, LANES), lambda j, place: (j, 0)),
                pl.BlockSpec((ROWS, g), lambda j, place: (0, 0)),
            ],
        ),
        compiler_params=params(plan),
        cost_estimate=cost(plan.pair * g * 64, plan.pair * g * 8),
        name="spots",
    )(place, own, sib, meta_own, meta_sib)


def predict_kernel(plan, n_parts, first, last, *refs):
    refs = list(refs)
    parts = [refs.pop(0) for _ in range(n_parts)]
    hit_ref, lot_ref = refs.pop(0), refs.pop(0)
    acc_in = None
    if not first:
        acc_in = refs.pop(0)
        refs.pop(0), refs.pop(0)
    if last:
        spot_ref, gg_ref, meta_ref = refs.pop(0), refs.pop(0), refs.pop(0)
    acc_ref, chi_ref, clo_ref = refs.pop(0), refs.pop(0), refs.pop(0)
    if last:
        stat_ref, sums_ref = refs.pop(0), refs.pop(0)
    stack_ref = refs.pop(0)
    j = pl.program_id(0)
    size = plan.chunk

    @pl.when(j == 0)
    def _():
        at = 0
        for part in parts:
            n = part.shape[0]
            hi, lo = split(part[...])
            stack_ref[at : at + n, :] = hi
            stack_ref[size + at : size + at + n, :] = lo
            stack_ref[2 * size + at : 2 * size + at + n, :] = hi
            chi_ref[at : at + n, :] = hi
            clo_ref[at : at + n, :] = lo
            at += n
        if last:
            sums_ref[...] = jnp.zeros_like(sums_ref)

    left = jnp.concatenate([hit_ref[...], hit_ref[...], lot_ref[...]], axis=1)
    value = jnp.dot(left, stack_ref[...], preferred_element_type=F32)
    if not first:
        value = value + acc_in[...]
    acc_ref[...] = value
    if last:
        spot = spot_ref[...]
        square, cross = value * value, value * spot
        lane = lax.broadcasted_iota(jnp.int32, stat_ref.shape, 1)
        stat_ref[...] = jnp.where(lane == 0, row_sum(square), jnp.where(lane == 1, row_sum(cross), gg_ref[...]))
        turned = jnp.transpose(meta_ref[...])
        row = lax.broadcasted_iota(jnp.int32, (PACKED, value.shape[0]), 0).astype(F32)
        pick = lambda first: jnp.where(turned[0:1, :] + first == row, turned[1:2, :], 0.0).astype(BF16)
        left = jnp.concatenate([pick(0)] * 3 + [pick(SLIDES)] * 3, axis=1)
        right = jnp.concatenate([*split3(square), *split3(cross)], axis=0)
        sums_ref[...] += jnp.dot(left, right, preferred_element_type=F32)


def make_predict(plan, k, parts, hit, lot, carry, last=None):
    t, g, size = PREDICT_TILE if plan.cells <= 2048 else 256, plan.genes, plan.chunk
    const = lambda j: (0, 0)
    in_specs = [pl.BlockSpec(p.shape, const) for p in parts]
    in_specs += [pl.BlockSpec((t, size), lambda j: (j, k))] * 2
    operands = [*parts, *pin(plan, hit, lot)]
    aliases = {}
    if carry is not None:
        at = len(operands)
        operands += list(pin(plan, *carry))
        in_specs += [pl.BlockSpec((t, g), lambda j: (j, 0)), pl.BlockSpec(memory_space=pl.ANY), pl.BlockSpec(memory_space=pl.ANY)]
        aliases = {at: 0, at + 1: 1, at + 2: 2}
    out_shape = [
        kept(plan, (plan.pair, g), F32),
        kept(plan, (plan.cells, g), BF16),
        kept(plan, (plan.cells, g), BF16),
    ]
    out_specs = [pl.BlockSpec((t, g), lambda j: (j, 0))] + [pl.BlockSpec((size, g), lambda j: (k, 0))] * 2
    if last is not None:
        operands += list(pin(plan, *last[:2])) + list(last[2:])
        in_specs += [pl.BlockSpec((t, g), lambda j: (j, 0))] + [pl.BlockSpec((t, LANES), lambda j: (j, 0))] * 2
        out_shape += [jax.ShapeDtypeStruct((plan.pair, LANES), F32), jax.ShapeDtypeStruct((PACKED, g), F32)]
        out_specs += [pl.BlockSpec((t, LANES), lambda j: (j, 0)), pl.BlockSpec((PACKED, g), const)]
    return pl.pallas_call(
        functools.partial(predict_kernel, plan, len(parts), carry is None, last is not None),
        out_shape=tuple(out_shape),
        grid=(plan.pair // t,),
        in_specs=in_specs,
        out_specs=out_specs,
        scratch_shapes=[pltpu.VMEM((3 * size, g), BF16)],
        input_output_aliases=aliases,
        compiler_params=params(plan),
        cost_estimate=cost(6 * plan.pair * g * size, plan.pair * g * 8),
        name="predict",
    )(*operands)


def spot_loss_kernel(plan, mine_ref, other_ref, meta_ref, row_ref, out_ref):
    stat = mine_ref[0 : plan.half, :] + other_ref[plan.half :, :]
    cosine = stat[:, 1:2] * (lax.rsqrt(stat[:, 0:1] + EPS) * lax.rsqrt(stat[:, 2:3] + EPS))
    total = jnp.sum(row_ref[0:1, :], keepdims=True) - jnp.sum(cosine * meta_ref[...][0 : plan.half, 1:2], keepdims=True)
    row = lax.broadcasted_iota(jnp.int32, out_ref.shape, 0)
    out_ref[...] = jnp.where(row == LOSS_ROW % 8, total / (plan.half * plan.total), 0.0)


def make_spot_loss(plan, mine, other, meta, row):
    return pl.pallas_call(
        functools.partial(spot_loss_kernel, plan),
        out_shape=jax.ShapeDtypeStruct((8, plan.genes), F32),
        in_specs=[pl.BlockSpec(memory_space=pltpu.VMEM)] * 4,
        out_specs=pl.BlockSpec(memory_space=pltpu.VMEM),
        compiler_params=params(plan),
        cost_estimate=cost(plan.half * 8, plan.half * 1024),
        name="spot_loss",
    )(*pin(plan, mine), other, meta, row)


def gradient_kernel(plan, coef_gene, coef_spot, pred_ref, spot_ref, mine_ref, other_ref, meta_ref, sums_ref, ng_ref,
                    mhi_ref, mlo_ref, ghi_ref, glo_ref, keep_ref, send_ref, loss_ref, a_ref, b_ref, acc_ref):
    j = pl.program_id(0)

    @pl.when(j == 0)
    def _():
        pad = jnp.zeros((ROWS - SLIDES, sums_ref.shape[1]), F32)
        parts = [sums_ref[i * SLIDES : (i + 1) * SLIDES, :] for i in range(2)]
        np_sum, dots = [jnp.concatenate([part, pad], axis=0) for part in parts]
        ng_sum = ng_ref[...]
        scale = lax.rsqrt(np_sum + EPS) * lax.rsqrt(ng_sum + EPS)
        cosine = dots * scale
        a_ref[...] = jnp.concatenate(split3(-coef_gene * scale), axis=0)
        b_ref[...] = jnp.concatenate(split3(coef_gene * (cosine / (np_sum + EPS))), axis=0)
        acc_ref[...] = jnp.zeros_like(acc_ref)
        row = lax.broadcasted_iota(jnp.int32, cosine.shape, 0)
        gene = jnp.sum(jnp.where(row < SLIDES, cosine, 0.0), keepdims=True) / (SLIDES * 2 * plan.genes)
        loss_ref[...] = jnp.broadcast_to(-gene, loss_ref.shape)

    stat = mine_ref[...] + other_ref[...]
    spot_sq, cross, true_sq = stat[:, 0:1], stat[:, 1:2], stat[:, 2:3]
    slide, mask = meta_ref[...][:, 0:1], meta_ref[...][:, 1:2]
    scale = lax.rsqrt(spot_sq + EPS) * lax.rsqrt(true_sq + EPS)
    cosine = cross * scale

    weight = coef_spot * mask
    lane = lax.broadcasted_iota(jnp.int32, (stat.shape[0], ROWS), 1).astype(F32)
    onehot = jnp.where(slide == lane, mask, 0.0).astype(BF16)
    onehot = jnp.concatenate([onehot] * 3, axis=1)
    gene_a = jnp.dot(onehot, a_ref[...], preferred_element_type=F32)
    gene_b = jnp.dot(onehot, b_ref[...], preferred_element_type=F32)
    grad = spot_ref[...] * (gene_a - weight * scale) + pred_ref[...] * (gene_b + weight * (cosine / (spot_sq + EPS)))
    hi, lo = split(grad)
    ghi_ref[...] = hi
    glo_ref[...] = lo
    left = jnp.concatenate([mhi_ref[...], mhi_ref[...], mlo_ref[...]], axis=1)
    right = jnp.concatenate([hi, lo, hi], axis=0)
    acc_ref[...] += jnp.dot(left, right, preferred_element_type=F32)

    @pl.when(j == pl.num_programs(0) - 1)
    def _():
        n = keep_ref.shape[0]
        keep_ref[...] = acc_ref[0:n, :]
        send_ref[...] = acc_ref[n:, :]


def make_gradient(plan, k, coef_gene, coef_spot, pred, spot, mine, other, meta, sums, ng_sum, mhi, mlo):
    t, g, size = GRADIENT_TILE if plan.cells <= 2048 else 256, plan.genes, plan.chunk
    tiles = plan.pair // t
    tile = lambda j: (j, 0)
    const = lambda j: (0, 0)
    halves = jax.ShapeDtypeStruct((size // 2, g), F32)
    return pl.pallas_call(
        functools.partial(gradient_kernel, plan, coef_gene, coef_spot),
        out_shape=(
            kept(plan, (plan.pair, g), BF16),
            kept(plan, (plan.pair, g), BF16),
            halves,
            halves,
            jax.ShapeDtypeStruct((8, LANES), F32),
        ),
        grid=(tiles,),
        in_specs=[
            pl.BlockSpec((t, g), tile),
            pl.BlockSpec((t, g), tile),
            pl.BlockSpec((t, LANES), tile),
            pl.BlockSpec((t, LANES), lambda j: ((j + tiles // 2) % tiles, 0)),
            pl.BlockSpec((t, LANES), tile),
            pl.BlockSpec((PACKED, g), const),
            pl.BlockSpec((ROWS, g), const),
            pl.BlockSpec((size, t), lambda j: (k, j)),
            pl.BlockSpec((size, t), lambda j: (k, j)),
        ],
        out_specs=[
            pl.BlockSpec((t, g), tile),
            pl.BlockSpec((t, g), tile),
            pl.BlockSpec((size // 2, g), const),
            pl.BlockSpec((size // 2, g), const),
            pl.BlockSpec((8, LANES), const),
        ],
        scratch_shapes=[pltpu.VMEM((3 * ROWS, g), BF16), pltpu.VMEM((3 * ROWS, g), BF16), pltpu.VMEM((size, g), F32)],
        compiler_params=params(plan),
        cost_estimate=cost(6 * plan.pair * g * size, plan.pair * g * 12),
        name="gradient",
    )(*pin(plan, pred, spot), mine, other, meta, sums, ng_sum, *pin(plan, mhi, mlo))


def cells_kernel(plan, ks, whole, mhi_ref, mlo_ref, ghi_ref, glo_ref, *outs):
    def rows(ref):
        if not whole:
            return ref[...]
        return jnp.concatenate([ref[k * plan.chunk : (k + 1) * plan.chunk, :] for k in ks], axis=0)

    hi, lo = rows(mhi_ref), rows(mlo_ref)
    left = jnp.concatenate([hi, hi, lo], axis=1)
    right = jnp.concatenate([ghi_ref[...], glo_ref[...], ghi_ref[...]], axis=0)
    value = jnp.dot(left, right, preferred_element_type=F32)
    at = 0
    for out in outs:
        out[...] = value[at : at + out.shape[0], :]
        at += out.shape[0]


def make_cells(plan, ks, sizes, mhi, mlo, ghi, glo):
    t, g, size = 256, plan.genes, plan.chunk
    whole = len(ks) > 1
    rows = (plan.cells, plan.pair) if whole else (size, plan.pair)
    at = 0 if whole else ks[0]
    return pl.pallas_call(
        functools.partial(cells_kernel, plan, ks, whole),
        out_shape=tuple(jax.ShapeDtypeStruct((n, g), F32) for n in sizes),
        grid=(g // t,),
        in_specs=[pl.BlockSpec(rows, lambda i: (at, 0))] * 2 + [pl.BlockSpec((plan.pair, t), lambda i: (0, i))] * 2,
        out_specs=[pl.BlockSpec((n, t), lambda i: (0, i)) for n in sizes],
        compiler_params=params(plan),
        cost_estimate=cost(6 * plan.pair * g * size * len(ks), plan.pair * g * 4),
        name="cells",
    )(*pin(plan, mhi, mlo, ghi, glo))


def turned_dot(chi, clo, ghi, glo):
    left = jnp.concatenate([chi, chi, clo], axis=1)
    right = jnp.concatenate([ghi, glo, ghi], axis=1)
    return lax.dot_general(left, right, (((1,), (1,)), ((), ())), preferred_element_type=F32)


def other_kernel(chi_ref, clo_ref, ghi_ref, glo_ref, out_ref):
    out_ref[...] = turned_dot(chi_ref[...], clo_ref[...], ghi_ref[...], glo_ref[...])


def cell_tile(plan):
    return min(plan.cells, 1024)


def make_other(plan, chi, clo, ghi, glo):
    t, g, ct = plan.tile, plan.genes, cell_tile(plan)
    tiles = plan.half // t
    return pl.pallas_call(
        other_kernel,
        out_shape=jax.ShapeDtypeStruct((plan.cells, plan.half), F32),
        grid=(tiles, plan.cells // ct),
        in_specs=[pl.BlockSpec((ct, g), lambda j, i: (i, 0))] * 2 + [pl.BlockSpec((t, g), lambda j, i: (j + tiles, 0))] * 2,
        out_specs=pl.BlockSpec((ct, t), lambda j, i: (i, j)),
        compiler_params=params(plan),
        cost_estimate=cost(6 * plan.cells * g * plan.half, plan.cells * plan.half * 12),
        name="other",
    )(*pin(plan, chi, clo, ghi, glo))


def logits_kernel(plan, coef_spot, place, chi_ref, clo_ref, ghi_ref, glo_ref, got_ref, mhi_ref, mlo_ref, cell_ref, meta_ref, row_ref,
                  out_ref, acc_ref):
    ct = cell_tile(plan)
    i = pl.program_id(1)
    rows = pl.ds(pl.multiple_of(i * ct, ct), ct)
    acc_ref[rows, :] = turned_dot(chi_ref[...], clo_ref[...], ghi_ref[...], glo_ref[...])

    @pl.when(i == pl.num_programs(1) - 1)
    def _():
        for k in range(plan.n_col):
            for m in range(plan.plane):
                at, there = (k * plan.plane + m) * plan.unit, (k * plan.plane + plan.reverse(m)) * plan.unit
                acc_ref[at : at + plan.unit, :] += got_ref[there : there + plan.unit, :]
        value = acc_ref[...]
        weight = mhi_ref[...].astype(F32) + mlo_ref[...].astype(F32)
        inner = jnp.sum(weight * value, axis=0, keepdims=True)
        meta = jnp.transpose(meta_ref[...])
        slide, coef = meta[0:1, :], coef_spot * meta[1:2, :]
        share = coef / row_ref[...][1:2, :]
        acc_ref[...] = weight * (value - inner + coef)
        for n, (k, m, c) in enumerate(blocks(plan)):
            start = pl.multiple_of(plan.block_start(place, k, m, c), plan.rows)
            cell = jnp.concatenate([cell_ref[pl.ds(start, plan.rows), :]] * (plan.tile // LANES), axis=1)
            out_ref[pl.ds(start, plan.rows), :] = acc_ref[n * plan.rows : (n + 1) * plan.rows, :] - jnp.where(cell == slide, share, 0.0)


def make_logits(plan, coef_spot, place, chi, clo, ghi, glo, got, mhi, mlo, cell, meta, row):
    t, g, ct = plan.tile, plan.genes, cell_tile(plan)
    column = lambda j, i, *_: (0, j)
    return pl.pallas_call(
        functools.partial(logits_kernel, plan, coef_spot),
        out_shape=jax.ShapeDtypeStruct((plan.cells, plan.half), F32),
        grid_spec=pltpu.PrefetchScalarGridSpec(
            num_scalar_prefetch=1,
            grid=(plan.half // t, plan.cells // ct),
            in_specs=[pl.BlockSpec((ct, g), lambda j, i, *_: (i, 0))] * 2
            + [pl.BlockSpec((t, g), lambda j, i, *_: (j, 0))] * 2
            + [pl.BlockSpec((plan.cells, t), column)] * 3
            + [
                pl.BlockSpec((plan.cells, LANES), lambda j, i, *_: (0, 0)),
                pl.BlockSpec((t, LANES), lambda j, i, *_: (j, 0)),
                pl.BlockSpec((8, t), column),
            ],
            out_specs=pl.BlockSpec((plan.cells, t), column),
            scratch_shapes=[pltpu.VMEM((plan.cells, t), F32)],
        ),
        compiler_params=params(plan, 24),
        cost_estimate=cost(6 * plan.cells * g * plan.half, plan.cells * plan.half * 20),
        name="logits",
    )(place, *pin(plan, chi, clo, ghi, glo), got, *pin(plan, mhi, mlo), cell, meta, row)


def on_device(plan, logits, cell_expr, spot_expr, cell_slide, spot_slide, spot_mask):
    g, rows = plan.genes, plan.rows
    spots_all = plan.half * plan.total
    factor = spots_all * plan.cells / SLIDES
    coef_spot = factor / spots_all
    coef_gene = factor / (SLIDES * 2 * g)
    spot_index, z = lax.axis_index("spot"), lax.axis_index("col")
    core, plane = spot_index % 2, spot_index // 2
    place = jnp.stack([plane, core, z]).astype(jnp.int32)
    send = lambda value, perm: lax.ppermute(value, AXES, perm)
    swap = plan.swap_core()
    hops = [plan.hop(step) for step in range(plan.bits)]

    tie = lax.optimization_barrier
    tie = lax.optimization_barrier

    def meet(flying, work):
        names, jobs = list(flying), list(work)
        came, made = tie(([flying[name] for name in names], [work[job] for job in jobs]))
        return dict(zip(names, came)), dict(zip(jobs, made))

    is_first = core == 0
    place, is_first = tie((place, is_first))
    lane = lax.broadcasted_iota(jnp.int32, (plan.half, LANES), 1)
    describe = lambda slide, mask: jnp.where(lane == 0, slide[:, None], mask[:, None]).astype(F32)
    meta_own = describe(spot_slide, spot_mask)
    cell = jnp.broadcast_to(cell_slide[:, None].astype(F32), (plan.cells, LANES))
    got, slide_sib, mask_sib = send(cell_expr, swap), send(spot_slide, swap), send(spot_mask, swap)
    got, slide_sib, mask_sib, meta_own, logits, spot_expr = tie((got, slide_sib, mask_sib, meta_own, logits, spot_expr))
    meta_sib = describe(slide_sib, mask_sib)
    first, second = jnp.concatenate([cell_expr[:, :g], got[:, :g]]), jnp.concatenate([got[:, g:], cell_expr[:, g:]])
    unit = jnp.where(is_first, first, second)
    logits_sib = spot_sib = None

    plane_hops = [("plane", 1 << bit) for bit in range(plan.bits)]
    ring_hops = [("ring", 1 << bit) for bit in range(plan.n_col.bit_length() - 1)]
    sum_orders = (plane_hops + ring_hops, ring_hops + plane_hops)

    def sum_hop(index):
        perm = []
        for q, c, i in plan.all_places():
            kind, bit = sum_orders[c][index]
            there = plan.device(q ^ bit, c, i) if kind == "plane" else plan.device(q, c, i ^ bit)
            perm.append((plan.device(q, c, i), there))
        return perm

    sum_hops = [sum_hop(index) for index in range(len(plane_hops) + len(ring_hops))]

    ring_sums = [
        [(plan.device(q, c, i), plan.device(q, c, i ^ bit)) for q, c, i in plan.all_places()] for _, bit in ring_hops
    ]
    plane_sums = [plan.hop(step) for step in range(plan.bits)]

    def sum_step(bit):
        perm = []
        for q, c, i in plan.all_places():
            there = plan.device(q ^ (1 << bit), c, i) if c == 0 else plan.device(q, c, i ^ (1 << bit))
            perm.append((plan.device(q, c, i), there))
        return perm

    def sum_round(index):
        perms = []
        for other in reversed(range(1, plan.plane)):
            perm = []
            for q, c, i in plan.all_places():
                there = plan.device(q ^ other, c, i) if c == index else plan.device(q, c, i ^ other)
                perm.append((plan.device(q, c, i), there))
            perms.append(perm)
        return perms

    n_col, bits = plan.n_col, plan.bits
    ring = plan.ring()
    units = {0: unit}
    parts = {}
    carry = mapping = spots = None
    row = None
    ng_left = [ring_hop for ring_hop in ring_sums] + [plane_hop for plane_hop in plane_sums]
    windows = n_col + bits - 1
    for w in range(windows):
        flying = {}
        for k in range(max(0, w - bits + 1), min(w + 1, n_col)):
            held = parts.setdefault(k, {0: units[k]})
            step = w - k
            fresh = [m for m in held if m.bit_length() == step] if step else [0]
            for m in fresh:
                for later in range(step, bits):
                    flying[k, m | (1 << later)] = send(held[m], hops[later])
        if w + 1 < n_col:
            flying["unit"] = send(units[w], ring)
        work = {}
        if w == 0:
            logits_sib, spot_sib = send(logits, swap), send(spot_expr, swap)
            own = make_mapping(plan, place, logits, cell, meta_own)
            work["row"] = own[4]
            work["mapping"] = own
            flying["logits"], flying["spot"] = logits_sib, spot_sib
        elif w == 1:
            work["mapping"] = make_mapping(plan, place, logits_sib, cell, meta_sib, mapping)
        if w == 2:
            work["spots"] = make_spots(plan, place, spot_expr, spot_sib, meta_own, meta_sib)
        if w >= bits:
            k = w - bits
            pieces = [parts[k][m] for m in range(plan.plane)]
            work["carry"] = make_predict(plan, k, pieces, mapping[2], mapping[3], carry)
            parts[k] = None
        if spots is not None and ng_left:
            flying["ng"] = send(spots[2], ng_left.pop(0))
        flying, work = meet(flying, work)
        if "ng" in flying:
            spots = (*spots[:2], spots[2] + flying["ng"])
        for key, value in flying.items():
            if key == "unit":
                units[w + 1] = value
            elif isinstance(key, tuple):
                parts[key[0]][key[1]] = value
        if w == 0:
            logits_sib, spot_sib = flying["logits"], flying["spot"]
        mapping, spots, carry = work.get("mapping", mapping), work.get("spots", spots), work.get("carry", carry)
        row = work.get("row", row)
    mhi, mlo, hit, lot, _ = mapping
    spot, true_sq, ng_sum = spots
    meta = jnp.concatenate([meta_own, meta_sib])
    k = n_col - 1
    pieces = [parts[k][m] for m in range(plan.plane)]
    pred, chi, clo, stat, sums = make_predict(plan, k, pieces, hit, lot, carry, (spot, true_sq, meta))

    stat_other = send(stat, swap)
    spot_loss = make_spot_loss(plan, stat, stat_other, meta, row)
    rounds = [sum_round(0), sum_round(1)] if plan.plane == n_col else [[perm] for perm in sum_hops]
    for index, perms in enumerate(rounds):
        came = [send(sums, perm) for perm in perms]
        if index == 0:
            came, spot_loss = tie((came, spot_loss))
            came.append(jnp.concatenate([jnp.zeros((PACKED - 8, g), F32), spot_loss]))
        if ng_left:
            ng_came = send(ng_sum, ng_left.pop(0))
            came, ng_came = tie((came, ng_came))
            ng_sum = ng_sum + ng_came
        sums = sum(came, sums)
    for perm in ng_left:
        ng_sum = ng_sum + send(ng_sum, perm)
    order = [k % n_col for k in range(1, n_col + 1)]
    last = n_col - 1
    ghi, glo, keep, away, loss = make_gradient(
        plan, order[0], coef_gene, coef_spot, pred, spot, stat, stat_other, meta, sums, ng_sum, mhi, mlo
    )
    half = plan.chunk // 2
    state = {0: (bits - 1, keep, away)}
    pending = {}
    travelling = None
    other = other_sib = grad_logits = None
    at = LOSS_ROW % 8
    part = sums[PACKED - 8 :, :LANES]
    if plan.plane == n_col:
        part_hops = [sum_step(bit) for bit in range(bits)] + [swap]
    else:
        part_hops = [sum_hops[0], swap]
    w = 0
    while True:
        flying = {}
        for i, value in reversed(list(state.items())):
            flying["chunk", i] = send(value[2], hops[value[0]])
        if travelling is not None:
            flying["ring"] = send(travelling, ring)
        work = {}
        if w == 0 and plan.cells <= 2048:
            made = make_cells(plan, order[1:], [half] * (2 * last), mhi, mlo, ghi, glo)
            for i in range(1, n_col):
                work["chunk", i] = (made[2 * i - 2], made[2 * i - 1])
        elif w < last and plan.cells > 2048:
            work["chunk", w + 1] = tuple(make_cells(plan, [order[w + 1]], [half, half], mhi, mlo, ghi, glo))
        if w == 2:
            work["other"] = make_other(plan, chi, clo, ghi, glo)
        elif w == 3:
            flying["other"] = send(other, swap)
        elif w == 4:
            work["logits"] = make_logits(plan, coef_spot, place, chi, clo, ghi, glo, other_sib, mhi, mlo, cell, meta, row)
        if 1 <= w <= len(part_hops):
            flying["part"] = send(part, part_hops[w - 1])
        flying, work = meet(flying, work)
        other, other_sib = work.get("other", other), flying.get("other", other_sib)
        grad_logits = work.get("logits", grad_logits)
        if "part" in flying:
            part = part + flying["part"]
            if w == len(part_hops) - 1:
                part = part[at : at + 1, :] + loss[0:1, :]
        for key, value in work.items():
            if isinstance(key, tuple):
                pending[key[1]] = value
        ended = None
        for i in list(state):
            step, keep, _ = state[i]
            came = flying["chunk", i]
            if step > 0:
                n = keep.shape[0] // 2
                state[i] = (step - 1, keep[:n] + came[:n], keep[n:] + came[n:])
            else:
                del state[i]
                ended = keep + came
                if "ring" in flying:
                    ended = ended + flying["ring"]
                finished = i
        travelling = ended
        if w + 1 < n_col:
            state[w + 1] = (bits - 1, *pending.pop(w + 1))
        w += 1
        if ended is not None and finished == last:
            result = ended
            break
    got = send(result, swap)
    def own_rows(result, got):
        first = jnp.concatenate([result[:rows], got[:rows]], axis=1)
        second = jnp.concatenate([got[rows:], result[rows:]], axis=1)
        return jnp.where(is_first, first, second)

    grad_expr = own_rows(result, got)
    return part[0, 0], grad_logits, grad_expr


def solution(mesh):
    in_specs = (
        P(None, AXES),
        P(AXES, None),
        P(AXES, None),
        P(),
        P(AXES),
        P(AXES),
    )
    out_specs = (P(), P(None, AXES), P(AXES, None))

    def whole(logits, cell_expr, spot_expr, cell_slide, spot_slide, spot_mask):
        n_spot, n_col = mesh.shape["spot"], mesh.shape["col"]
        plan = Plan(n_spot, n_col, logits.shape[0], logits.shape[1] // (n_spot * n_col), cell_expr.shape[1])
        return jax.shard_map(
            functools.partial(on_device, plan), mesh=mesh, in_specs=in_specs, out_specs=out_specs, check_vma=False
        )(logits, cell_expr, spot_expr, cell_slide, spot_slide, spot_mask)

    return whole
```
